32 devices in a mesh: dp: 8 (over y, x, core), fsdp: 4 (over z).
Axes of the slice: x: 2, y: 2, z: 4, core: 2. Of those that a mesh axis runs over, the one named last changes fastest.
Arguments:
- layer_input: bfloat16 [64, 1024, 768], P(('dp', 'fsdp')), may hold values from -8 to 8
- cotangent: bfloat16 [64, 1024, 768], P(('dp', 'fsdp')), may hold values from -6 to 6
- doc_lengths: int32 [64, 8], P(('dp', 'fsdp')), may hold values from 1 to 512, 1024 in all within a row
- pad_tail: int32 [64], P(('dp', 'fsdp')), may hold values from 0 to 256
- query_weight: bfloat16 [768, 768], P(('dp', 'fsdp')), may hold values from -0.25 to 0.25
- query_bias: bfloat16 [768], P(('dp', 'fsdp')), may hold values from -3 to 3
- key_weight: bfloat16 [768, 768], P(('dp', 'fsdp')), may hold values from -0.25 to 0.25
- value_weight: bfloat16 [768, 768], P(('dp', 'fsdp')), may hold values from -0.21875 to 0.21875
- value_bias: bfloat16 [768], P(('dp', 'fsdp')), may hold values from -3 to 3
- merge_weight: bfloat16 [768, 768], P(('dp', 'fsdp')), may hold values from -0.875 to 0.875
- merge_bias: bfloat16 [768], P(('dp', 'fsdp')), may hold values from -1.75 to 1.75
- first_gain: bfloat16 [768], P(('dp', 'fsdp')), may hold values from 0.099609375 to 1.8984375
- first_shift: bfloat16 [768], P(('dp', 'fsdp')), may hold values from -1.75 to 1.75
- inner_weight: bfloat16 [768, 3072], P(('dp', 'fsdp')), may hold values from -0.21875 to 0.21875
- inner_bias: bfloat16 [3072], P(('dp', 'fsdp')), may hold values from -3 to 3
- outer_weight: bfloat16 [3072, 768], P(('dp', 'fsdp')), may hold values from -0.109375 to 0.109375
- outer_bias: bfloat16 [768], P(('dp', 'fsdp')), may hold values from -1.75 to 1.75
- second_gain: bfloat16 [768], P(('dp', 'fsdp')), may hold values from 0.099609375 to 1.8984375
- second_shift: bfloat16 [768], P(('dp', 'fsdp')), may hold values from -1.75 to 1.75
Outputs:
- layer_output: bfloat16 [64, 1024, 768], P(('dp', 'fsdp'))
- input_gradient: float32 [64, 1024, 768], P(('dp', 'fsdp'))
- query_weight_gradient: float32 [768, 768], P(('dp', 'fsdp'))
- query_bias_gradient: float32 [768], P(('dp', 'fsdp'))
- key_weight_gradient: float32 [768, 768], P(('dp', 'fsdp'))
- value_weight_gradient: float32 [768, 768], P(('dp', 'fsdp'))
- value_bias_gradient: float32 [768], P(('dp', 'fsdp'))
- merge_weight_gradient: float32 [768, 768], P(('dp', 'fsdp'))
- merge_bias_gradient: float32 [768], P(('dp', 'fsdp'))
- first_gain_gradient: float32 [768], P(('dp', 'fsdp'))
- first_shift_gradient: float32 [768], P(('dp', 'fsdp'))
- inner_weight_gradient: float32 [768, 3072], P(('dp', 'fsdp'))
- inner_bias_gradient: float32 [3072], P(('dp', 'fsdp'))
- outer_weight_gradient: float32 [3072, 768], P(('dp', 'fsdp'))
- outer_bias_gradient: float32 [768], P(('dp', 'fsdp'))
- second_gain_gradient: float32 [768], P(('dp', 'fsdp'))
- second_shift_gradient: float32 [768], P(('dp', 'fsdp'))
- layer_stats: float32 [5], replicated
The draws below stay inside these ranges and needn't reach their ends.
Inputs may be any that keep to these rules, and one draw needn't show every extreme that they name: `doc_lengths`: each row sums to 1024.
All inputs are finite; a program needn't handle non-finite values.
Results may differ from the reference program's by a relative error of at most 0.014.
Values may be sent and summed in bfloat16 or wider, within the bound.
No kernel may reach another device: no remote copies, remote signals or barrier semaphores. Data moves between devices by JAX's collectives and lax.ppermute only.
A program may use at most 256 MiB of HBM per device.

```python
import math
import jax
import jax.numpy as jnp
import numpy as np
from jax import lax

D = 768
HEADS = 12
HEAD_DIM = 64
FF = 3072
LEN = 1024
DOCS = 8
SEQS = 64


def draw_layer_input(key, part):
    shape = (SEQS, LEN, D)
    rising = 0.75 * 2.0 ** (jnp.arange(SEQS, dtype=jnp.float32) / (SEQS - 1))
    values = jax.random.normal(key, shape, jnp.float32) * rising[:, None, None]
    return jnp.clip(values, -8.0, 8.0).astype(jnp.bfloat16)


def touch_ends(values, rng, least, largest):
    longest = values.shape.index(max(values.shape))
    spots = []
    for shift in (0, 1):
        where = [jax.random.randint(jax.random.fold_in(rng, axis), (), 0, length) for axis, length in enumerate(values.shape)]
        where[longest] = (where[longest] + shift) % values.shape[longest]
        spots.append(tuple(where))
    return values.at[spots[0]].set(least).at[spots[1]].set(largest)


def shard_levels(rng, dims, cuts, smallest, high):
    factor_of, own = 1.0, jax.random.fold_in(rng, 6)
    for dim, shards_of in cuts:
        steps = jnp.exp(jax.random.uniform(jax.random.fold_in(own, dim), (shards_of,), jnp.float32, smallest / len(cuts), high / len(cuts)))
        factor_of = factor_of * jnp.repeat(steps, dims[dim] // shards_of).reshape([-1 if axis == dim else 1 for axis in range(len(dims))])
    return factor_of


def length_profile(amount, total, bound, slope):
    portions = [(1 << 20) // math.isqrt(standing ** slope) + 1 for standing in range(2, amount + 1)]
    rest, counts = total - bound - (amount - 1), [1] * (amount - 1)
    while rest > 0:
        movable = [i for i in range(amount - 1) if counts[i] < bound]
        pool, remaining = sum([portions[i] for i in movable]), rest
        for i in movable:
            more = min(bound - counts[i], max(1, remaining * portions[i] // pool), rest)
            counts[i] = counts[i] + more
            rest = rest - more
    return np.array([bound] + counts)


def uneven(key, number_of, total, bound, slope):
    if number_of == 2:
        one = jax.random.randint(key, (), max(1, total - bound), min(bound, total - 1) + 1)
        return jnp.stack([one, total - one])
    lengths = jnp.asarray(length_profile(number_of, total, bound, slope), jnp.int32)
    pairs = (number_of - 1) // 2
    donor, sink = lengths[1:1 + 2 * pairs:2], lengths[2:2 + 2 * pairs:2]
    room = jnp.minimum(donor - 1, bound - sink)
    shifted = jax.random.randint(jax.random.fold_in(key, 1), (pairs,), 0, 1 << 20) % (room + 1)
    lengths = lengths.at[1:1 + 2 * pairs:2].set(donor - shifted).at[2:2 + 2 * pairs:2].set(sink + shifted)
    return lengths[jax.random.permutation(jax.random.fold_in(key, 2), number_of)]


def normal_values(rng, shape, scale, limit, shards=(), held_as=jnp.bfloat16):
    values = jax.random.normal(rng, shape, jnp.float32) * scale
    if len(shards) > 0:
        values = shard_levels(rng, shape, shards, -0.22, 0.18) * values
    return jnp.clip(values, min=-limit, max=limit).astype(held_as)


def setup_inputs(seed: int = 0) -> dict:
    seeds = jax.random.split(jax.random.key(seed), 20)
    layer_input = draw_layer_input(jax.random.fold_in(seeds[19], 71), 0)
    cotangent = normal_values(seeds[1], (SEQS, LEN, D), 1.0, 6.0, ((0, 32),))
    doc_lengths = jax.vmap(lambda own: uneven(own, DOCS, LEN, LEN // 2, 2))(jax.random.split(seeds[2], SEQS)).reshape((SEQS, DOCS)).astype(jnp.int32)
    pad_tail = touch_ends(jax.random.randint(seeds[3], (SEQS,), 0, LEN // 4 + 1), jax.random.fold_in(seeds[3], 1), 0, (LEN // 4 + 1) - 1).astype(jnp.int32)
    query_weight = normal_values(seeds[4], (D, D), (D * 3 // 4) ** -0.5, 0.25, ((0, 32),))
    query_bias = normal_values(seeds[5], (D,), 0.5, 3.0, ((0, 32),))
    key_weight = normal_values(seeds[6], (D, D), (D * 3 // 4) ** -0.5, 0.25, ((0, 32),))
    value_weight = normal_values(seeds[7], (D, D), D ** -0.5, 0.21875, ((0, 32),))
    value_bias = normal_values(seeds[8], (D,), 0.5, 3.0, ((0, 32),))
    merge_weight = normal_values(seeds[9], (D, D), (D // 16) ** -0.5, 0.875, ((0, 32),))
    merge_bias = normal_values(seeds[10], (D,), 0.3, 1.75, ((0, 32),))
    first_gain = jnp.clip(1.0 + 0.18 * jax.random.normal(seeds[11], (D,), jnp.float32), 0.099609375, 1.8984375).astype(jnp.bfloat16)
    first_shift = normal_values(seeds[12], (D,), 0.3, 1.75, ((0, 32),))
    inner_weight = normal_values(seeds[13], (D, FF), D ** -0.5, 0.21875, ((0, 32),))
    inner_bias = normal_values(seeds[14], (FF,), 0.5, 3.0, ((0, 32),))
    outer_weight = normal_values(seeds[15], (FF, D), FF ** -0.5, 0.109375, ((0, 32),))
    outer_bias = normal_values(seeds[16], (D,), 0.3, 1.75, ((0, 32),))
    second_gain = jnp.clip(1.0 + 0.18 * jax.random.normal(seeds[17], (D,), jnp.float32), 0.099609375, 1.8984375).astype(jnp.bfloat16)
    second_shift = normal_values(seeds[18], (D,), 0.3, 1.75, ((0, 32),))
    return dict(layer_input=layer_input, cotangent=cotangent, doc_lengths=doc_lengths, pad_tail=pad_tail, query_weight=query_weight, query_bias=query_bias, key_weight=key_weight, value_weight=value_weight, value_bias=value_bias, merge_weight=merge_weight, merge_bias=merge_bias, first_gain=first_gain, first_shift=first_shift, inner_weight=inner_weight, inner_bias=inner_bias, outer_weight=outer_weight, outer_bias=outer_bias, second_gain=second_gain, second_shift=second_shift)


@jax.custom_vjp
def low(v):
    return lax.optimization_barrier(v.astype(jnp.bfloat16)).astype(jnp.float32)

@jax.custom_vjp
def low_back(v):
    return v

def low_keep(v):
    return (low(v), None)

def low_pass(kept, grad):
    return (grad,)

def back_keep(v):
    return (v, None)

def back_low(kept, grad):
    return (low(grad),)
low.defvjp(low_keep, low_pass)
low_back.defvjp(back_keep, back_low)
HIGH = lax.Precision.HIGHEST
EPSILON = 1e-12
NEGATIVE = -1e+30
ROOT_HALF = 0.7071067811865476

def positions(lengths_row, pad_count):
    doc_ends = jnp.cumsum(lengths_row).astype(jnp.int32)
    places = jnp.arange(LEN, dtype=jnp.int32)
    segment = lax.optimization_barrier(jnp.sum((places[:, None] >= doc_ends[None, :]).astype(jnp.int32), axis=1))
    is_valid = places < LEN - pad_count
    return (jnp.where(is_valid, segment, DOCS).astype(jnp.int32), is_valid)

def layer_norm(values, gain, shift):
    center = lax.optimization_barrier(jnp.mean(values, axis=-1, keepdims=True))
    centred = values - center
    spread = lax.optimization_barrier(jnp.mean(centred * centred, axis=-1, keepdims=True))
    return centred * lax.rsqrt(spread + EPSILON) * gain + shift

def gelu_value(inner):
    return 0.5 * inner * (1.0 + lax.erf(inner * ROOT_HALF))

def sequence_forward(weights, rows, segment):
    query_mat, query_add, key_mat, value_mat, value_add, merge_mat, merge_add, first_scale, first_offset, inner_mat, inner_add, outer_mat, outer_add, second_scale, second_offset = weights
    queries = low(low_back(jnp.dot(rows, query_mat, precision=HIGH) + query_add))
    key_rows = low(low_back(jnp.dot(rows, key_mat, precision=HIGH)))
    value_rows = low(low_back(jnp.dot(rows, value_mat, precision=HIGH) + value_add))
    query_heads = queries.reshape(LEN, HEADS, HEAD_DIM)
    key_heads = key_rows.reshape(LEN, HEADS, HEAD_DIM)
    value_heads = value_rows.reshape(LEN, HEADS, HEAD_DIM)
    scores = low_back(jnp.einsum('qhd,khd->hqk', query_heads, key_heads, precision=HIGH) * HEAD_DIM ** (-0.5))
    allowed = segment[:, None] == segment[None, :]
    masked = jnp.where(allowed[None], scores, NEGATIVE)
    top = lax.optimization_barrier(jnp.max(masked, axis=-1, keepdims=True))
    expo = jnp.exp(masked - top)
    probs = expo / lax.optimization_barrier(jnp.sum(expo, axis=-1, keepdims=True))
    mixed = low(low_back(jnp.einsum('hqk,khd->qhd', low(probs), value_heads, precision=HIGH))).reshape(LEN, D)
    branch = low_back(jnp.dot(mixed, merge_mat, precision=HIGH) + merge_add)
    first = layer_norm(rows + branch, first_scale, first_offset)
    inner = low_back(jnp.dot(low(first), inner_mat, precision=HIGH) + inner_add)
    hidden = low(gelu_value(inner))
    second = low_back(jnp.dot(hidden, outer_mat, precision=HIGH) + outer_add)
    result = layer_norm(first + second, second_scale, second_offset)
    return (result, branch, second)

def reference(layer_input, cotangent, doc_lengths, pad_tail, query_weight, query_bias, key_weight, value_weight, value_bias, merge_weight, merge_bias, first_gain, first_shift, inner_weight, inner_bias, outer_weight, outer_bias, second_gain, second_shift):
    params = (query_weight.astype(jnp.float32), query_bias.astype(jnp.float32), key_weight.astype(jnp.float32), value_weight.astype(jnp.float32), value_bias.astype(jnp.float32), merge_weight.astype(jnp.float32), merge_bias.astype(jnp.float32), first_gain.astype(jnp.float32), first_shift.astype(jnp.float32), inner_weight.astype(jnp.float32), inner_bias.astype(jnp.float32), outer_weight.astype(jnp.float32), outer_bias.astype(jnp.float32), second_gain.astype(jnp.float32), second_shift.astype(jnp.float32))
    rows_all = layer_input.astype(jnp.float32)
    segments, validity = jax.vmap(positions)(doc_lengths, pad_tail)
    sequence_step = jax.checkpoint(sequence_forward)

    def forward(weights, inputs):

        def scan_step(carry, item):
            rows, segment, is_valid = item
            result, branch, second = sequence_step(weights, rows, segment)
            weight = is_valid.astype(jnp.float32)[:, None]
            sums = jnp.stack([jnp.sum(weight * rows * rows), jnp.sum(weight * branch * branch), jnp.sum(weight * second * second), jnp.sum(weight * result * result)])
            return (carry + sums, result)
        sums, results = lax.scan(scan_step, jnp.zeros((4,), jnp.float32), (inputs, segments, validity))
        return (results, sums)
    results, pullback, sums = jax.vjp(forward, params, rows_all, has_aux=True)
    upstream = cotangent.astype(jnp.float32) * validity.astype(jnp.float32)[:, :, None]
    grads, input_grad = pullback(upstream)
    count = jnp.sum(validity.astype(jnp.float32))
    stats = jnp.concatenate([jnp.reshape(count / (SEQS * LEN), (1,)), jnp.sqrt(sums / (count * D))])
    return (results.astype(jnp.bfloat16), input_grad, grads[0], grads[1], grads[2], grads[3], grads[4], grads[5], grads[6], grads[7], grads[8], grads[9], grads[10], grads[11], grads[12], grads[13], grads[14], stats)
```

```python
import functools

import jax
import jax.numpy as jnp
from jax import lax
from jax.experimental import pallas as pl
from jax.experimental.pallas import tpu as pltpu
from jax.sharding import PartitionSpec as P

HEAD_DIM = 64
LEN = 1024
DOCS = 8
EPSILON = 1e-12
NEGATIVE = -1e30
ROOT_HALF = 0.7071067811865476
INV_ROOT_TWO_PI = 0.3989422804014327
AXES = ("dp", "fsdp")
F32 = jnp.float32
BF16 = jnp.bfloat16

GROUP = 256
HEADS_IN = GROUP // HEAD_DIM
TRIPLE = 3 * GROUP
QB = 256
CHUNK = 256
VEC = 128


def dot(left, right, left_dim=1, right_dim=0):
    return lax.dot_general(
        left, right, (((left_dim,), (right_dim,)), ((), ())), preferred_element_type=F32
    )


def head_masks():
    lane = lax.broadcasted_iota(jnp.int32, (1, GROUP), 1) // HEAD_DIM
    return [lane == h for h in range(HEADS_IN)]


def segments(doc_lengths, pad_tail):
    ends = jnp.cumsum(doc_lengths, axis=1)
    limit = (LEN - pad_tail)[:, None]
    places = jnp.arange(LEN, dtype=jnp.int32)
    segment = jnp.sum((places[None, :, None] >= ends[:, None, :]).astype(jnp.int32), axis=2)
    segment = jnp.where(places[None] < limit, segment, DOCS)
    borders = jnp.concatenate(
        [jnp.zeros_like(limit), jnp.minimum(ends, limit), limit, jnp.full_like(limit, LEN)], axis=1
    )[:, None, :]
    first = (jnp.arange(LEN // QB, dtype=jnp.int32) * QB)[None, :, None]
    low = jnp.max(jnp.where(borders <= first, borders, 0), axis=2)
    high = jnp.min(jnp.where(borders > first + QB - 1, borders, LEN), axis=2)
    low = (low // 128) * 128
    count = (high - low + CHUNK - 1) // CHUNK
    low = jnp.minimum(low, LEN - CHUNK * count)
    return segment, low.astype(jnp.int32), count.astype(jnp.int32)


def forward_kernel(
    low_ref, count_ref, rows_ref, w_ref, bias_ref, segc_ref, segr_ref,
    qkv_ref, mixed_ref, lse_ref, keyt_ref,
):
    s = pl.program_id(0)
    qkv_ref[...] = (dot(rows_ref[...], w_ref[...]) + bias_ref[0:1, :]).astype(BF16)
    keyt_ref[...] = qkv_ref[:, GROUP : 2 * GROUP].T
    masks = head_masks()

    def block(i, carry):
        start = pl.multiple_of(i * QB, QB)
        queries = qkv_ref[pl.ds(start, QB), :GROUP] * BF16(HEAD_DIM**-0.5)
        zero = jnp.zeros_like(queries)
        own = segc_ref[pl.ds(start, QB), :][:, :1]
        low = pl.multiple_of(low_ref[s, i], 128)
        count = count_ref[s, i]
        for c in range(1, LEN // CHUNK + 1):

            @pl.when(count == c)
            def _():
                span = pl.ds(low, CHUNK * c)
                keys = keyt_ref[:, span]
                values = qkv_ref[span, 2 * GROUP :]
                allowed = own == segr_ref[0:1, span]
                lane = lax.broadcasted_iota(jnp.int32, (QB, 128), 1)
                mixed = None
                for h in range(HEADS_IN):
                    scores = dot(jnp.where(masks[h], queries, zero), keys)
                    scores = jnp.where(allowed, scores, NEGATIVE)
                    top = jnp.max(scores, axis=1, keepdims=True)
                    expo = jnp.exp(scores - top)
                    total = jnp.sum(expo, axis=1, keepdims=True)
                    part = dot(expo.astype(BF16), values) * (1.0 / total)
                    logsum = top + jnp.log(total)
                    if h == 0:
                        mixed, sums = part, jnp.broadcast_to(logsum, (QB, 128))
                    else:
                        mixed, sums = jnp.where(masks[h], part, mixed), jnp.where(lane == h, logsum, sums)
                mixed_ref[pl.ds(start, QB), :] = mixed.astype(BF16)
                lse_ref[:, pl.ds(start, QB)] = sums.T[:8]

        return carry

    lax.fori_loop(0, LEN // QB, block, 0)


def attention_forward(rows, w, bias, segc, segr, low, count):
    seqs, _, width = rows.shape
    groups = width // GROUP
    return pl.pallas_call(
        forward_kernel,
        grid_spec=pltpu.PrefetchScalarGridSpec(
            num_scalar_prefetch=2,
            grid=(seqs, groups),
            in_specs=[
                pl.BlockSpec((None, LEN, width), lambda s, g, *_: (s, 0, 0)),
                pl.BlockSpec((width, TRIPLE), lambda s, g, *_: (0, g)),
                pl.BlockSpec((8, TRIPLE), lambda s, g, *_: (0, g)),
                pl.BlockSpec((None, LEN, 128), lambda s, g, *_: (s, 0, 0)),
                pl.BlockSpec((None, 8, LEN), lambda s, g, *_: (s, 0, 0)),
            ],
            out_specs=[
                pl.BlockSpec((None, LEN, TRIPLE), lambda s, g, *_: (s, 0, g)),
                pl.BlockSpec((None, LEN, GROUP), lambda s, g, *_: (s, 0, g)),
                pl.BlockSpec((None, None, 8, LEN), lambda s, g, *_: (s, g, 0, 0)),
            ],
            scratch_shapes=[pltpu.VMEM((GROUP, LEN), BF16)],
        ),
        out_shape=[
            jax.ShapeDtypeStruct((seqs, LEN, 3 * width), BF16),
            jax.ShapeDtypeStruct((seqs, LEN, width), BF16),
            jax.ShapeDtypeStruct((seqs, groups, 8, LEN), F32),
        ],
        compiler_params=pltpu.CompilerParams(vmem_limit_bytes=48 * 2**20),
        name="attention_forward",
    )(low, count, rows, w, bias, segc, segr)


def backward_kernel(
    low_ref, count_ref, qkv_ref, mixed_ref, grad_ref, rowst_ref, lse_ref, segc_ref, segr_ref,
    dqkv_ref, dw_ref, sums_ref,
    q_ref, qt_ref, gt_ref, kt_ref, dqt_ref, acc_ref, delta_ref,
):
    s = pl.program_id(1)
    masks = head_masks()
    grad = grad_ref[...]
    prod = grad.astype(F32) * mixed_ref[...].astype(F32)
    coarse = prod.astype(BF16)
    fine = (prod - coarse.astype(F32)).astype(BF16)
    pick = lax.broadcasted_iota(jnp.int32, (8, GROUP), 1) // HEAD_DIM
    pick = (pick == lax.broadcasted_iota(jnp.int32, (8, GROUP), 0)).astype(F32).astype(BF16)
    delta_ref[...] = dot(pick, coarse, 1, 1) + dot(pick, fine, 1, 1)
    queries = qkv_ref[:, :GROUP] * BF16(HEAD_DIM**-0.5)
    q_ref[...] = queries
    qt_ref[...] = queries.T
    gt_ref[...] = grad.T
    kt_ref[...] = qkv_ref[:, GROUP : 2 * GROUP].T
    dqt_ref[...] = jnp.zeros_like(dqt_ref)

    def block(i, carry):
        start = pl.multiple_of(i * QB, QB)
        mine = pl.ds(start, QB)
        keys = qkv_ref[mine, GROUP : 2 * GROUP]
        values = qkv_ref[mine, 2 * GROUP :]
        zero = jnp.zeros_like(keys)
        own = segc_ref[mine, :][:, :1]
        low = pl.multiple_of(low_ref[s, i], 128)
        count = count_ref[s, i]
        for c in range(1, LEN // CHUNK + 1):

            @pl.when(count == c)
            def _():
                span = pl.ds(low, CHUNK * c)
                allowed = own == segr_ref[0:1, span]
                dkey = dvalue = None
                for h in range(HEADS_IN):
                    scores = dot(jnp.where(masks[h], keys, zero), qt_ref[:, span])
                    probs = jnp.exp(jnp.where(allowed, scores, NEGATIVE) - lse_ref[h : h + 1, span])
                    pgrad = dot(jnp.where(masks[h], values, zero), gt_ref[:, span])
                    low_score = (probs * (pgrad - delta_ref[h : h + 1, span])).astype(BF16)
                    v_part = dot(probs.astype(BF16), grad_ref[span, :])
                    k_part = dot(low_score, q_ref[span, :])
                    head = slice(h * HEAD_DIM, (h + 1) * HEAD_DIM)
                    dqt_ref[head, span] += dot(kt_ref[head, mine], low_score)
                    if h == 0:
                        dkey, dvalue = k_part, v_part
                    else:
                        dkey, dvalue = jnp.where(masks[h], k_part, dkey), jnp.where(masks[h], v_part, dvalue)
                dqkv_ref[mine, GROUP : 2 * GROUP] = dkey.astype(BF16)
                dqkv_ref[mine, 2 * GROUP :] = dvalue.astype(BF16)

        return carry

    lax.fori_loop(0, LEN // QB, block, 0)
    dqkv_ref[:, :GROUP] = (dqt_ref[...] * HEAD_DIM**-0.5).astype(BF16).T
    dqkv = dqkv_ref[...]
    dw = dot(rowst_ref[...], dqkv)
    sums = jnp.broadcast_to(jnp.sum(dqkv.astype(F32), axis=0, keepdims=True), sums_ref.shape)

    @pl.when(s == 0)
    def _():
        acc_ref[...] = dw
        sums_ref[...] = sums

    @pl.when(s > 0)
    def _():
        acc_ref[...] += dw
        sums_ref[...] += sums

    @pl.when(s == pl.num_programs(1) - 1)
    def _():
        dw_ref[...] = acc_ref[...].astype(BF16)


def attention_backward(qkv, mixed, grad, rowst, lse, segc, segr, low, count):
    seqs, _, width = mixed.shape
    groups = width // GROUP
    return pl.pallas_call(
        backward_kernel,
        grid_spec=pltpu.PrefetchScalarGridSpec(
            num_scalar_prefetch=2,
            grid=(groups, seqs),
            in_specs=[
                pl.BlockSpec((None, LEN, TRIPLE), lambda g, s, *_: (s, 0, g)),
                pl.BlockSpec((None, LEN, GROUP), lambda g, s, *_: (s, 0, g)),
                pl.BlockSpec((None, LEN, GROUP), lambda g, s, *_: (s, 0, g)),
                pl.BlockSpec((None, width, LEN), lambda g, s, *_: (s, 0, 0)),
                pl.BlockSpec((None, None, 8, LEN), lambda g, s, *_: (s, g, 0, 0)),
                pl.BlockSpec((None, LEN, 128), lambda g, s, *_: (s, 0, 0)),
                pl.BlockSpec((None, 8, LEN), lambda g, s, *_: (s, 0, 0)),
            ],
            out_specs=[
                pl.BlockSpec((None, LEN, TRIPLE), lambda g, s, *_: (s, 0, g)),
                pl.BlockSpec((width, TRIPLE), lambda g, s, *_: (0, g)),
                pl.BlockSpec((8, TRIPLE), lambda g, s, *_: (0, g)),
            ],
            scratch_shapes=[
                pltpu.VMEM((LEN, GROUP), BF16),
                pltpu.VMEM((GROUP, LEN), BF16),
                pltpu.VMEM((GROUP, LEN), BF16),
                pltpu.VMEM((GROUP, LEN), BF16),
                pltpu.VMEM((GROUP, LEN), F32),
                pltpu.VMEM((width, TRIPLE), F32),
                pltpu.VMEM((8, LEN), F32),
            ],
        ),
        out_shape=[
            jax.ShapeDtypeStruct((seqs, LEN, 3 * width), BF16),
            jax.ShapeDtypeStruct((width, 3 * width), BF16),
            jax.ShapeDtypeStruct((8, 3 * width), F32),
        ],
        compiler_params=pltpu.CompilerParams(vmem_limit_bytes=48 * 2**20),
        name="attention_backward",
    )(low, count, qkv, mixed, grad, rowst, lse, segc, segr)


def middle_kernel(
    parts, width, tokens,
    pad_ref, mixed_ref, rows_ref, cot_ref, w_ref, vec_ref,
    out_ref, res_ref, mgrad_ref, dw_ref, sums_ref, stats_ref,
    hidden_ref, slope_ref, first_ref, normed_ref, upper_ref, wide_ref, acc_ref, stage_ref, sem,
):
    i = pl.program_id(0)
    per_seq = LEN // tokens

    @pl.when(i == 0)
    def _():
        acc_ref[...] = jnp.zeros_like(acc_ref)
        sums_ref[...] = jnp.zeros_like(sums_ref)
        stats_ref[...] = jnp.zeros_like(stats_ref)

    def weight(k):
        if isinstance(k, int):
            return w_ref[:, k * width : (k + 1) * width]
        return w_ref[:, pl.ds(pl.multiple_of(k * width, width), width)]

    def vector(row):
        return vec_ref[row : row + 1, :]

    def add_sum(row, values):
        sums_ref[row : row + 1, :] += jnp.sum(values, axis=0, keepdims=True)

    place = (i % per_seq) * tokens + lax.broadcasted_iota(jnp.int32, (tokens, 1), 0)
    valid = (place < LEN - pad_ref[i // per_seq]).astype(F32)

    def add_stat(row, values):
        stats_ref[row : row + 1, :] += jnp.sum(valid * values * values, axis=0, keepdims=True)

    def mean(values):
        return jnp.mean(values, axis=1, keepdims=True)

    def normed_of(values):
        centred = values - mean(values)
        inverse = lax.rsqrt(mean(centred * centred) + EPSILON)
        return centred * inverse, inverse

    def norm_backward(scaled, normed, inverse):
        return inverse * (scaled - mean(scaled) - normed * mean(scaled * normed))

    rows = rows_ref[...].astype(F32)
    branch = dot(mixed_ref[...], weight(0)) + vector(0)
    add_stat(0, rows)
    add_stat(1, branch)
    first_normed, first_inverse = normed_of(rows + branch)
    normed_ref[...] = first_normed
    first = first_normed * vector(1) + vector(2)
    first_ref[...] = first.astype(BF16)
    wide_ref[...] = jnp.zeros_like(wide_ref)

    def feed(j, carry):
        inner = dot(first_ref[...], weight(1 + j)) + vec_ref[pl.ds(6 + j, 1), :]
        half = 0.5 * (1.0 + lax.erf(inner * ROOT_HALF))
        hidden = (inner * half).astype(BF16)
        hidden_ref[j] = hidden
        slope_ref[j] = (half + inner * jnp.exp(-0.5 * inner * inner) * INV_ROOT_TWO_PI).astype(BF16)
        wide_ref[...] += dot(hidden, weight(1 + parts + j))
        return carry

    lax.fori_loop(0, parts, feed, 0)
    second = wide_ref[...] + vector(3)
    add_stat(2, second)
    second_normed, second_inverse = normed_of(first + second)
    result = second_normed * vector(4) + vector(5)
    add_stat(3, result)
    out_ref[...] = result.astype(BF16)
    upstream = cot_ref[...].astype(F32) * valid
    add_sum(0, upstream * second_normed)
    add_sum(1, upstream)
    upper = norm_backward(upstream * vector(4), second_normed, second_inverse)
    upper_low = upper.astype(BF16)
    upper_ref[...] = upper_low
    add_sum(2, upper_low.astype(F32))
    wide_ref[...] = upper
    upper_t = upper_low.T
    first_t = first_ref[...].T

    def back(j, carry):
        acc_ref[1 + parts + j] += dot(upper_t, hidden_ref[j])
        inner_low = (dot(upper_ref[...], weight(1 + parts + j), 1, 1) * slope_ref[j].astype(F32)).astype(BF16)
        sums_ref[pl.ds(8 + j, 1), :] += jnp.sum(inner_low.astype(F32), axis=0, keepdims=True)
        acc_ref[1 + j] += dot(first_t, inner_low)
        wide_ref[...] += dot(inner_low, weight(1 + j), 1, 1)
        return carry

    lax.fori_loop(0, parts, back, 0)
    first_grad = wide_ref[...]
    first_normed = normed_ref[...]
    add_sum(3, first_grad * first_normed)
    add_sum(4, first_grad)
    residual = norm_backward(first_grad * vector(1), first_normed, first_inverse)
    res_ref[...] = residual
    branch_low = residual.astype(BF16)
    add_sum(5, branch_low.astype(F32))
    acc_ref[0] += dot(mixed_ref[...], branch_low, 0, 0)
    mgrad_ref[...] = dot(branch_low, weight(0), 1, 1).astype(BF16)

    @pl.when(i == pl.num_programs(0) - 1)
    def _():
        def copy(k, slot):
            columns = pl.ds(pl.multiple_of(k * width, width), width)
            return pltpu.make_async_copy(stage_ref.at[slot], dw_ref.at[:, columns], sem.at[slot])

        def flush(k, carry):
            slot = lax.rem(k, 2)

            @pl.when(k >= 2)
            def _():
                copy(k - 2, slot).wait()

            @pl.when(k > parts)
            def _():
                stage_ref[slot] = acc_ref[k].astype(BF16).T

            @pl.when(k <= parts)
            def _():
                stage_ref[slot] = acc_ref[k].astype(BF16)

            copy(k, slot).start()
            return carry

        lax.fori_loop(0, 1 + 2 * parts, flush, 0)
        copy(2 * parts - 1, (2 * parts - 1) % 2).wait()
        copy(2 * parts, (2 * parts) % 2).wait()


def middle(mixed, rows, cotangent, w, vec, pad):
    count, width = mixed.shape
    tokens = 256
    parts = (w.shape[1] // width - 1) // 2
    block = pl.BlockSpec((tokens, width), lambda i, *_: (i, 0))
    return pl.pallas_call(
        functools.partial(middle_kernel, parts, width, tokens),
        grid_spec=pltpu.PrefetchScalarGridSpec(
            num_scalar_prefetch=1,
            grid=(count // tokens,),
            in_specs=[
                block,
                block,
                block,
                pl.BlockSpec(w.shape, lambda i, *_: (0, 0), pipeline_mode=pl.Buffered(1)),
                pl.BlockSpec(vec.shape, lambda i, *_: (0, 0)),
            ],
            out_specs=[
                block,
                block,
                block,
                pl.BlockSpec(memory_space=pl.ANY),
                pl.BlockSpec((16, width), lambda i, *_: (0, 0)),
                pl.BlockSpec((8, width), lambda i, *_: (0, 0)),
            ],
            scratch_shapes=[
                pltpu.VMEM((parts, tokens, width), BF16),
                pltpu.VMEM((parts, tokens, width), BF16),
                pltpu.VMEM((tokens, width), BF16),
                pltpu.VMEM((tokens, width), F32),
                pltpu.VMEM((tokens, width), BF16),
                pltpu.VMEM((tokens, width), F32),
                pltpu.VMEM((1 + 2 * parts, width, width), F32),
                pltpu.VMEM((2, width, width), BF16),
                pltpu.SemaphoreType.DMA((2,)),
            ],
        ),
        out_shape=[
            jax.ShapeDtypeStruct((count, width), BF16),
            jax.ShapeDtypeStruct((count, width), F32),
            jax.ShapeDtypeStruct((count, width), BF16),
            jax.ShapeDtypeStruct((width, (1 + 2 * parts) * width), BF16),
            jax.ShapeDtypeStruct((16, width), F32),
            jax.ShapeDtypeStruct((8, width), F32),
        ],
        compiler_params=pltpu.CompilerParams(vmem_limit_bytes=60 * 2**20),
        name="middle",
    )(pad, mixed, rows, cotangent, w, vec)


def gather(shard):
    return lax.all_gather(shard, AXES, axis=0, tiled=True)


def scatter(partial):
    partial = lax.psum_scatter(partial, "dp", scatter_dimension=0, tiled=True)
    return lax.psum_scatter(partial, "fsdp", scatter_dimension=0, tiled=True)


def total_over_devices(values):
    for axis in AXES:
        size = lax.axis_size(axis)
        step = 1
        while step < size:
            values = values + lax.ppermute(values, axis, [(d, d ^ step) for d in range(size)])
            step *= 2
    return values


def per_device(
    layer_input, cotangent, doc_lengths, pad_tail,
    query_weight, query_bias, key_weight, value_weight, value_bias,
    merge_weight, merge_bias, first_gain, first_shift,
    inner_weight, inner_bias, outer_weight, outer_bias, second_gain, second_shift,
):
    seqs, _, width = layer_input.shape
    own = query_weight.shape[0]
    devices = width // own
    parts = inner_weight.shape[1] // width
    groups = width // GROUP

    vectors = [query_bias, value_bias, merge_bias, first_gain, first_shift, outer_bias, second_gain, second_shift]
    columns = jnp.concatenate([jnp.stack(vectors), inner_bias.reshape(parts, own)]).T
    columns = jnp.pad(columns, ((0, 0), (0, VEC - columns.shape[1])))
    triples = [
        mat[:, g * GROUP : (g + 1) * GROUP]
        for g in range(groups)
        for mat in (query_weight, key_weight, value_weight)
    ]
    near = gather(jnp.concatenate(triples + [columns], axis=1))
    inner_own = inner_weight.reshape(own, devices, parts, own).transpose(0, 2, 1, 3).reshape(own, parts * width)
    outer_own = outer_weight.reshape(parts, own, width).transpose(1, 0, 2).reshape(own, parts * width)
    far = gather(jnp.concatenate([merge_weight, inner_own, outer_own], axis=1))

    segment, low, count = segments(doc_lengths, pad_tail)
    segc = jnp.broadcast_to(segment[:, :, None], (seqs, LEN, 128))
    segr = jnp.broadcast_to(segment[:, None, :], (seqs, 8, LEN))
    rowst = jnp.swapaxes(layer_input, 1, 2)

    vec_rows = near[:, 3 * width :].T.astype(F32)
    bias = jnp.stack([vec_rows[0], jnp.zeros((width,), F32), vec_rows[1]])
    bias = bias.reshape(3, groups, GROUP).transpose(1, 0, 2).reshape(1, 3 * width)
    bias = jnp.broadcast_to(bias, (8, 3 * width))
    vec = vec_rows[2:18]

    qkv, mixed, lse = attention_forward(layer_input, near, bias, segc, segr, low, count)
    tokens = seqs * LEN
    output, residual, mixed_grad, far_partial, sums, stats = middle(
        mixed.reshape(tokens, width), layer_input.reshape(tokens, width), cotangent.reshape(tokens, width), far, vec, pad_tail
    )
    far_grad = scatter(far_partial)
    dqkv, near_partial, near_sums = attention_backward(
        qkv, mixed, mixed_grad.reshape(mixed.shape), rowst, lse, segc, segr, low, count
    )
    valid_count = jnp.sum(LEN - pad_tail).astype(F32)
    stat_row = jnp.concatenate([jnp.sum(stats[:4], axis=1), valid_count[None], jnp.zeros((width - 5,), F32)])
    totals = total_over_devices(jnp.concatenate([sums[:6], sums[8 : 8 + parts], stat_row[None]]))

    near_rows = near_sums[0].reshape(groups, 3, GROUP)
    near_cols = jnp.stack([near_rows[:, 0].reshape(width), near_rows[:, 2].reshape(width)])
    near_cols = jnp.pad(near_cols.T, ((0, 0), (0, VEC - 2))).astype(BF16)
    near_grad = scatter(jnp.concatenate([near_partial, near_cols], axis=1)).astype(F32)
    input_gradient = residual + dot(dqkv.reshape(tokens, 3 * width), near[:, : 3 * width], 1, 1)

    which = lax.axis_index(AXES)
    mine = lax.dynamic_slice_in_dim(totals[: 6 + parts], which * own, own, axis=1)
    inner_bias_gradient = mine[6:].reshape(parts * own)
    triple = near_grad[:, : 3 * width].reshape(own, groups, 3, GROUP)
    query_grad, key_grad, value_grad = (triple[:, :, k].reshape(own, width) for k in range(3))
    far_grad = far_grad.astype(F32)
    inner_grad = far_grad[:, width : (1 + parts) * width]
    inner_grad = inner_grad.reshape(own, parts, devices, own).transpose(0, 2, 1, 3).reshape(own, parts * width)
    outer_grad = far_grad[:, (1 + parts) * width :].reshape(own, parts, width).transpose(1, 0, 2)
    all_tokens = tokens * devices
    valid_total = totals[6 + parts, 4]
    share = jnp.reshape(valid_total / all_tokens, (1,))
    layer_stats = jnp.concatenate([share, jnp.sqrt(totals[6 + parts, :4] / (valid_total * width))])
    return (
        output.reshape(layer_input.shape),
        input_gradient.reshape(layer_input.shape),
        query_grad,
        near_grad[:, 3 * width],
        key_grad,
        value_grad,
        near_grad[:, 3 * width + 1],
        far_grad[:, :width],
        mine[5],
        mine[3],
        mine[4],
        inner_grad,
        inner_bias_gradient,
        outer_grad.reshape(parts * own, width),
        mine[2],
        mine[0],
        mine[1],
        layer_stats,
    )


def solution(mesh):
    matrix, vector, cube = P(AXES, None), P(AXES), P(AXES, None, None)
    in_specs = (
        cube, cube, matrix, vector,
        matrix, vector, matrix, matrix, vector,
        matrix, vector, vector, vector,
        matrix, vector, matrix, vector, vector, vector,
    )
    out_specs = (
        cube, cube,
        matrix, vector, matrix, matrix, vector,
        matrix, vector, vector, vector,
        matrix, vector, matrix, vector, vector, vector,
        P(),
    )
    return jax.shard_map(per_device, mesh=mesh, in_specs=in_specs, out_specs=out_specs, check_vma=False)
```

```python
import functools

import jax
import jax.numpy as jnp
from jax import lax
from jax.experimental import pallas as pl
from jax.experimental.pallas import tpu as pltpu
from jax.sharding import PartitionSpec as P

HEAD_DIM = 64
LEN = 1024
DOCS = 8
EPSILON = 1e-12
NEGATIVE = -1e30
ROOT_HALF = 0.7071067811865476
INV_ROOT_TWO_PI = 0.3989422804014327
AXES = ("dp", "fsdp")
F32 = jnp.float32
BF16 = jnp.bfloat16

GROUP = 256
HEADS_IN = GROUP // HEAD_DIM
TRIPLE = 3 * GROUP
QB = 256
CHUNK = 256
VEC = 128


def dot(left, right, left_dim=1, right_dim=0):
    return lax.dot_general(
        left, right, (((left_dim,), (right_dim,)), ((), ())), preferred_element_type=F32
    )


def head_masks():
    lane = lax.broadcasted_iota(jnp.int32, (1, GROUP), 1) // HEAD_DIM
    return [lane == h for h in range(HEADS_IN)]


def cost(flops, moved):
    return pl.CostEstimate(flops=int(flops), bytes_accessed=int(moved), transcendentals=0)


def segments(doc_lengths, pad_tail):
    ends = jnp.cumsum(doc_lengths, axis=1)
    limit = (LEN - pad_tail)[:, None]
    places = jnp.arange(LEN, dtype=jnp.int32)
    segment = jnp.sum((places[None, :, None] >= ends[:, None, :]).astype(jnp.int32), axis=2)
    segment = jnp.where(places[None] < limit, segment, DOCS)
    borders = jnp.concatenate(
        [jnp.zeros_like(limit), jnp.minimum(ends, limit), limit, jnp.full_like(limit, LEN)], axis=1
    )[:, None, :]
    first = (jnp.arange(LEN // QB, dtype=jnp.int32) * QB)[None, :, None]
    low = jnp.max(jnp.where(borders <= first, borders, 0), axis=2)
    high = jnp.min(jnp.where(borders > first + QB - 1, borders, LEN), axis=2)
    low = (low // 128) * 128
    count = (high - low + CHUNK - 1) // CHUNK
    low = jnp.minimum(low, LEN - CHUNK * count)
    return segment, low.astype(jnp.int32), count.astype(jnp.int32)


def forward_kernel(
    low_ref, count_ref, rows_ref, w_ref, bias_ref, segc_ref, segr_ref,
    qkv_ref, mixed_ref, lse_ref, keyt_ref,
):
    s = pl.program_id(0)
    qkv_ref[...] = (dot(rows_ref[...], w_ref[...]) + bias_ref[0:1, :]).astype(BF16)
    keyt_ref[...] = qkv_ref[:, GROUP : 2 * GROUP].T
    masks = head_masks()

    def block(i, carry):
        start = pl.multiple_of(i * QB, QB)
        queries = qkv_ref[pl.ds(start, QB), :GROUP] * BF16(HEAD_DIM**-0.5)
        zero = jnp.zeros_like(queries)
        own = segc_ref[pl.ds(start, QB), :][:, :1]
        low = pl.multiple_of(low_ref[s, i], 128)
        count = count_ref[s, i]
        for c in range(1, LEN // CHUNK + 1):

            @pl.when(count == c)
            def _():
                span = pl.ds(low, CHUNK * c)
                keys = keyt_ref[:, span]
                values = qkv_ref[span, 2 * GROUP :]
                allowed = own == segr_ref[0:1, span]
                lane = lax.broadcasted_iota(jnp.int32, (QB, 128), 1)
                mixed = None
                for h in range(HEADS_IN):
                    scores = dot(jnp.where(masks[h], queries, zero), keys)
                    scores = jnp.where(allowed, scores, NEGATIVE)
                    top = jnp.max(scores, axis=1, keepdims=True)
                    expo = jnp.exp(scores - top)
                    total = jnp.sum(expo, axis=1, keepdims=True)
                    part = dot(expo.astype(BF16), values) * (1.0 / total)
                    logsum = top + jnp.log(total)
                    if h == 0:
                        mixed, sums = part, jnp.broadcast_to(logsum, (QB, 128))
                    else:
                        mixed, sums = jnp.where(masks[h], part, mixed), jnp.where(lane == h, logsum, sums)
                mixed_ref[pl.ds(start, QB), :] = mixed.astype(BF16)
                lse_ref[:, pl.ds(start, QB)] = sums.T[:8]

        return carry

    lax.fori_loop(0, LEN // QB, block, 0)


def attention_forward(rows, w, bias, segc, segr, low, count):
    seqs, _, width = rows.shape
    groups = width // GROUP
    return pl.pallas_call(
        forward_kernel,
        grid_spec=pltpu.PrefetchScalarGridSpec(
            num_scalar_prefetch=2,
            grid=(seqs, groups),
            in_specs=[
                pl.BlockSpec((None, LEN, width), lambda s, g, *_: (s, 0, 0)),
                pl.BlockSpec((width, TRIPLE), lambda s, g, *_: (0, g)),
                pl.BlockSpec((8, TRIPLE), lambda s, g, *_: (0, g)),
                pl.BlockSpec((None, LEN, 128), lambda s, g, *_: (s, 0, 0)),
                pl.BlockSpec((None, 8, LEN), lambda s, g, *_: (s, 0, 0)),
            ],
            out_specs=[
                pl.BlockSpec((None, LEN, TRIPLE), lambda s, g, *_: (s, 0, g)),
                pl.BlockSpec((None, LEN, GROUP), lambda s, g, *_: (s, 0, g)),
                pl.BlockSpec((None, None, 8, LEN), lambda s, g, *_: (s, g, 0, 0)),
            ],
            scratch_shapes=[pltpu.VMEM((GROUP, LEN), BF16)],
        ),
        out_shape=[
            jax.ShapeDtypeStruct((seqs, LEN, 3 * width), BF16),
            jax.ShapeDtypeStruct((seqs, LEN, width), BF16),
            jax.ShapeDtypeStruct((seqs, groups, 8, LEN), F32),
        ],
        compiler_params=pltpu.CompilerParams(vmem_limit_bytes=48 * 2**20),
        cost_estimate=cost(2 * seqs * LEN * width * (3 * width + 16 * LEN), seqs * LEN * width * 10),
        name="attention_forward",
    )(low, count, rows, w, bias, segc, segr)


def backward_kernel(
    low_ref, count_ref, qkv_ref, mixed_ref, grad_ref, rowst_ref, lse_ref, segc_ref, segr_ref, vec_ref,
    dqkv_ref, dw_ref, columns_ref,
    q_ref, qt_ref, gt_ref, kt_ref, dqt_ref, acc_ref, delta_ref, sums_ref,
):
    g, s = pl.program_id(0), pl.program_id(1)
    masks = head_masks()

    @pl.when((g == 0) & (s == 0))
    def _():
        sums_ref[...] = jnp.zeros_like(sums_ref)
        sums_ref[:16, :] = vec_ref[...]

    grad = grad_ref[...]
    prod = grad.astype(F32) * mixed_ref[...].astype(F32)
    coarse = prod.astype(BF16)
    fine = (prod - coarse.astype(F32)).astype(BF16)
    pick = lax.broadcasted_iota(jnp.int32, (8, GROUP), 1) // HEAD_DIM
    pick = (pick == lax.broadcasted_iota(jnp.int32, (8, GROUP), 0)).astype(F32).astype(BF16)
    delta_ref[...] = dot(pick, coarse, 1, 1) + dot(pick, fine, 1, 1)
    queries = qkv_ref[:, :GROUP] * BF16(HEAD_DIM**-0.5)
    q_ref[...] = queries
    qt_ref[...] = queries.T
    gt_ref[...] = grad.T
    kt_ref[...] = qkv_ref[:, GROUP : 2 * GROUP].T
    dqt_ref[...] = jnp.zeros_like(dqt_ref)

    def block(i, carry):
        start = pl.multiple_of(i * QB, QB)
        mine = pl.ds(start, QB)
        keys = qkv_ref[mine, GROUP : 2 * GROUP]
        values = qkv_ref[mine, 2 * GROUP :]
        zero = jnp.zeros_like(keys)
        own = segc_ref[mine, :][:, :1]
        low = pl.multiple_of(low_ref[s, i], 128)
        count = count_ref[s, i]
        for c in range(1, LEN // CHUNK + 1):

            @pl.when(count == c)
            def _():
                span = pl.ds(low, CHUNK * c)
                allowed = own == segr_ref[0:1, span]
                dkey = dvalue = None
                for h in range(HEADS_IN):
                    scores = dot(jnp.where(masks[h], keys, zero), qt_ref[:, span])
                    probs = jnp.exp(jnp.where(allowed, scores, NEGATIVE) - lse_ref[h : h + 1, span])
                    pgrad = dot(jnp.where(masks[h], values, zero), gt_ref[:, span])
                    low_score = (probs * (pgrad - delta_ref[h : h + 1, span])).astype(BF16)
                    v_part = dot(probs.astype(BF16), grad_ref[span, :])
                    k_part = dot(low_score, q_ref[span, :])
                    head = slice(h * HEAD_DIM, (h + 1) * HEAD_DIM)
                    dqt_ref[head, span] += dot(kt_ref[head, mine], low_score)
                    if h == 0:
                        dkey, dvalue = k_part, v_part
                    else:
                        dkey, dvalue = jnp.where(masks[h], k_part, dkey), jnp.where(masks[h], v_part, dvalue)
                dqkv_ref[mine, GROUP : 2 * GROUP] = dkey.astype(BF16)
                dqkv_ref[mine, 2 * GROUP :] = dvalue.astype(BF16)

        return carry

    lax.fori_loop(0, LEN // QB, block, 0)
    dqkv_ref[:, :GROUP] = (dqt_ref[...] * HEAD_DIM**-0.5).astype(BF16).T
    dqkv = dqkv_ref[...]
    dw = dot(rowst_ref[...], dqkv)
    sums = jnp.sum(dqkv.astype(F32), axis=0, keepdims=True)
    lanes = pl.ds(pl.multiple_of(g * GROUP, GROUP), GROUP)
    sums_ref[6:7, lanes] += sums[:, :GROUP]
    sums_ref[7:8, lanes] += sums[:, 2 * GROUP :]

    @pl.when(s == 0)
    def _():
        acc_ref[...] = dw

    @pl.when(s > 0)
    def _():
        acc_ref[...] += dw

    @pl.when(s == pl.num_programs(1) - 1)
    def _():
        dw_ref[...] = acc_ref[...].astype(BF16)

    @pl.when((g == pl.num_programs(0) - 1) & (s == pl.num_programs(1) - 1))
    def _():
        columns_ref[...] = sums_ref[...].T.astype(BF16)


def attention_backward(qkv, mixed, grad, rowst, lse, segc, segr, vec, low, count):
    seqs, _, width = mixed.shape
    groups = width // GROUP
    return pl.pallas_call(
        backward_kernel,
        grid_spec=pltpu.PrefetchScalarGridSpec(
            num_scalar_prefetch=2,
            grid=(groups, seqs),
            in_specs=[
                pl.BlockSpec((None, LEN, TRIPLE), lambda g, s, *_: (s, 0, g)),
                pl.BlockSpec((None, LEN, GROUP), lambda g, s, *_: (s, 0, g)),
                pl.BlockSpec((None, LEN, GROUP), lambda g, s, *_: (s, 0, g)),
                pl.BlockSpec((None, width, LEN), lambda g, s, *_: (s, 0, 0)),
                pl.BlockSpec((None, None, 8, LEN), lambda g, s, *_: (s, g, 0, 0)),
                pl.BlockSpec((None, LEN, 128), lambda g, s, *_: (s, 0, 0)),
                pl.BlockSpec((None, 8, LEN), lambda g, s, *_: (s, 0, 0)),
                pl.BlockSpec((16, width), lambda g, s, *_: (0, 0)),
            ],
            out_specs=[
                pl.BlockSpec((None, LEN, TRIPLE), lambda g, s, *_: (s, 0, g)),
                pl.BlockSpec((width, TRIPLE), lambda g, s, *_: (0, g)),
                pl.BlockSpec((width, VEC), lambda g, s, *_: (0, 0)),
            ],
            scratch_shapes=[
                pltpu.VMEM((LEN, GROUP), BF16),
                pltpu.VMEM((GROUP, LEN), BF16),
                pltpu.VMEM((GROUP, LEN), BF16),
                pltpu.VMEM((GROUP, LEN), BF16),
                pltpu.VMEM((GROUP, LEN), F32),
                pltpu.VMEM((width, TRIPLE), F32),
                pltpu.VMEM((8, LEN), F32),
                pltpu.VMEM((VEC, width), F32),
            ],
        ),
        out_shape=[
            jax.ShapeDtypeStruct((seqs, LEN, 3 * width), BF16),
            jax.ShapeDtypeStruct((width, 3 * width), BF16),
            jax.ShapeDtypeStruct((width, VEC), BF16),
        ],
        compiler_params=pltpu.CompilerParams(vmem_limit_bytes=48 * 2**20),
        cost_estimate=cost(2 * seqs * LEN * width * (3 * width + 32 * LEN), seqs * LEN * width * 20),
        name="attention_backward",
    )(low, count, qkv, mixed, grad, rowst, lse, segc, segr, vec)


def middle_kernel(
    parts, width, tokens,
    pad_ref, mixed_ref, rows_ref, cot_ref, w_ref, vec_ref,
    out_ref, res_ref, mgrad_ref, dw_ref, sums_ref, stats_ref,
    hidden_ref, slope_ref, first_ref, normed_ref, upper_ref, wide_ref, acc_ref, stage_ref, sem,
):
    i = pl.program_id(0)
    per_seq = LEN // tokens

    @pl.when(i == 0)
    def _():
        acc_ref[...] = jnp.zeros_like(acc_ref)
        sums_ref[...] = jnp.zeros_like(sums_ref)
        stats_ref[...] = jnp.zeros_like(stats_ref)

    def weight(k):
        if isinstance(k, int):
            return w_ref[:, k * width : (k + 1) * width]
        return w_ref[:, pl.ds(pl.multiple_of(k * width, width), width)]

    def vector(row):
        return vec_ref[row : row + 1, :]

    def add_sum(row, values):
        sums_ref[row : row + 1, :] += jnp.sum(values, axis=0, keepdims=True)

    place = (i % per_seq) * tokens + lax.broadcasted_iota(jnp.int32, (tokens, 1), 0)
    valid = (place < LEN - pad_ref[i // per_seq]).astype(F32)

    def add_stat(row, values):
        stats_ref[row : row + 1, :] += jnp.sum(valid * values * values, axis=0, keepdims=True)

    def mean(values):
        return jnp.mean(values, axis=1, keepdims=True)

    def normed_of(values):
        centred = values - mean(values)
        inverse = lax.rsqrt(mean(centred * centred) + EPSILON)
        return centred * inverse, inverse

    def norm_backward(scaled, normed, inverse):
        return inverse * (scaled - mean(scaled) - normed * mean(scaled * normed))

    rows = rows_ref[...].astype(F32)
    branch = dot(mixed_ref[...], weight(0)) + vector(0)
    add_stat(0, rows)
    add_stat(1, branch)
    first_normed, first_inverse = normed_of(rows + branch)
    normed_ref[...] = first_normed
    first = first_normed * vector(1) + vector(2)
    first_ref[...] = first.astype(BF16)
    wide_ref[...] = jnp.zeros_like(wide_ref)

    def feed(j, carry):
        inner = dot(first_ref[...], weight(1 + j)) + vec_ref[pl.ds(6 + j, 1), :]
        half = 0.5 * (1.0 + lax.erf(inner * ROOT_HALF))
        hidden = (inner * half).astype(BF16)
        hidden_ref[j] = hidden
        slope_ref[j] = (half + inner * jnp.exp(-0.5 * inner * inner) * INV_ROOT_TWO_PI).astype(BF16)
        wide_ref[...] += dot(hidden, weight(1 + parts + j))
        return carry

    lax.fori_loop(0, parts, feed, 0)
    second = wide_ref[...] + vector(3)
    add_stat(2, second)
    second_normed, second_inverse = normed_of(first + second)
    result = second_normed * vector(4) + vector(5)
    add_stat(3, result)
    out_ref[...] = result.astype(BF16)
    upstream = cot_ref[...].astype(F32) * valid
    add_sum(0, upstream * second_normed)
    add_sum(1, upstream)
    upper = norm_backward(upstream * vector(4), second_normed, second_inverse)
    upper_low = upper.astype(BF16)
    upper_ref[...] = upper_low
    add_sum(2, upper_low.astype(F32))
    wide_ref[...] = upper
    upper_t = upper_low.T
    first_t = first_ref[...].T

    def back(j, carry):
        acc_ref[1 + parts + j] += dot(upper_t, hidden_ref[j])
        inner_low = (dot(upper_ref[...], weight(1 + parts + j), 1, 1) * slope_ref[j].astype(F32)).astype(BF16)
        sums_ref[pl.ds(8 + j, 1), :] += jnp.sum(inner_low.astype(F32), axis=0, keepdims=True)
        acc_ref[1 + j] += dot(first_t, inner_low)
        wide_ref[...] += dot(inner_low, weight(1 + j), 1, 1)
        return carry

    lax.fori_loop(0, parts, back, 0)
    first_grad = wide_ref[...]
    first_normed = normed_ref[...]
    add_sum(3, first_grad * first_normed)
    add_sum(4, first_grad)
    residual = norm_backward(first_grad * vector(1), first_normed, first_inverse)
    res_ref[...] = residual
    branch_low = residual.astype(BF16)
    add_sum(5, branch_low.astype(F32))
    acc_ref[0] += dot(mixed_ref[...], branch_low, 0, 0)
    mgrad_ref[...] = dot(branch_low, weight(0), 1, 1).astype(BF16)

    @pl.when(i == pl.num_programs(0) - 1)
    def _():
        def copy(k, slot):
            columns = pl.ds(pl.multiple_of(k * width, width), width)
            return pltpu.make_async_copy(stage_ref.at[slot], dw_ref.at[:, columns], sem.at[slot])

        def flush(k, carry):
            slot = lax.rem(k, 2)

            @pl.when(k >= 2)
            def _():
                copy(k - 2, slot).wait()

            @pl.when(k > parts)
            def _():
                stage_ref[slot] = acc_ref[k].astype(BF16).T

            @pl.when(k <= parts)
            def _():
                stage_ref[slot] = acc_ref[k].astype(BF16)

            copy(k, slot).start()
            return carry

        lax.fori_loop(0, 1 + 2 * parts, flush, 0)
        copy(2 * parts - 1, (2 * parts - 1) % 2).wait()
        copy(2 * parts, (2 * parts) % 2).wait()


def middle(mixed, rows, cotangent, w, vec, pad):
    count, width = mixed.shape
    tokens = 256
    parts = (w.shape[1] // width - 1) // 2
    block = pl.BlockSpec((tokens, width), lambda i, *_: (i, 0))
    return pl.pallas_call(
        functools.partial(middle_kernel, parts, width, tokens),
        grid_spec=pltpu.PrefetchScalarGridSpec(
            num_scalar_prefetch=1,
            grid=(count // tokens,),
            in_specs=[
                block,
                block,
                block,
                pl.BlockSpec(w.shape, lambda i, *_: (0, 0), pipeline_mode=pl.Buffered(1)),
                pl.BlockSpec(vec.shape, lambda i, *_: (0, 0)),
            ],
            out_specs=[
                block,
                block,
                block,
                pl.BlockSpec(memory_space=pl.ANY),
                pl.BlockSpec((16, width), lambda i, *_: (0, 0)),
                pl.BlockSpec((8, width), lambda i, *_: (0, 0)),
            ],
            scratch_shapes=[
                pltpu.VMEM((parts, tokens, width), BF16),
                pltpu.VMEM((parts, tokens, width), BF16),
                pltpu.VMEM((tokens, width), BF16),
                pltpu.VMEM((tokens, width), F32),
                pltpu.VMEM((tokens, width), BF16),
                pltpu.VMEM((tokens, width), F32),
                pltpu.VMEM((1 + 2 * parts, width, width), F32),
                pltpu.VMEM((2, width, width), BF16),
                pltpu.SemaphoreType.DMA((2,)),
            ],
        ),
        out_shape=[
            jax.ShapeDtypeStruct((count, width), BF16),
            jax.ShapeDtypeStruct((count, width), F32),
            jax.ShapeDtypeStruct((count, width), BF16),
            jax.ShapeDtypeStruct((width, (1 + 2 * parts) * width), BF16),
            jax.ShapeDtypeStruct((16, width), F32),
            jax.ShapeDtypeStruct((8, width), F32),
        ],
        compiler_params=pltpu.CompilerParams(vmem_limit_bytes=60 * 2**20),
        cost_estimate=cost(12 * count * width * w.shape[1], count * width * 14 + 4 * w.size),
        name="middle",
    )(pad, mixed, rows, cotangent, w, vec)


def gather(shard):
    return lax.all_gather(shard, AXES, axis=0, tiled=True)


def swap(values, axis, flip):
    return lax.ppermute(values, axis, [(d, d ^ flip) for d in range(lax.axis_size(axis))])


def place_kernel(columns, lines, where_ref, *refs):
    sources, target = refs[:lines], refs[lines]
    plane, column = where_ref[0], where_ref[1]
    for m, source in enumerate(sources):
        for k in range(columns):
            target[(plane ^ m) * columns + (column ^ k)] = source[k]


def quick_gather(shard):
    planes, columns = lax.axis_size("dp"), lax.axis_size("fsdp")
    rows, width = shard.shape
    if planes % 2 or rows % 8:
        return gather(shard)
    column = jnp.stack([shard] + [swap(shard, "fsdp", k) for k in range(1, columns)])
    even = [column] + [swap(column, "dp", m) for m in range(2, planes, 2)]
    odd = [swap(part, "dp", 1) for part in even]
    sources = [part for pair in zip(even, odd) for part in pair]
    where = jnp.stack([lax.axis_index("dp"), lax.axis_index("fsdp")]).astype(jnp.int32)
    whole = pl.pallas_call(
        functools.partial(place_kernel, columns, len(sources)),
        grid_spec=pltpu.PrefetchScalarGridSpec(
            num_scalar_prefetch=1,
            grid=(1,),
            in_specs=[pl.BlockSpec((columns, rows, width), lambda i, *_: (0, 0, 0))] * len(sources),
            out_specs=pl.BlockSpec((planes * columns, rows, width), lambda i, *_: (0, 0, 0)),
        ),
        out_shape=jax.ShapeDtypeStruct((planes * columns, rows, width), shard.dtype),
        compiler_params=pltpu.CompilerParams(vmem_limit_bytes=48 * 2**20),
        name="place",
    )(where, *sources)
    return whole.reshape(planes * columns * rows, width)


def quick_scatter(partial):
    planes, columns = lax.axis_size("dp"), lax.axis_size("fsdp")
    rows = partial.shape[0] // (planes * columns)
    if planes % 2 or rows % 8:
        return scatter(partial)
    plane, column = lax.axis_index("dp"), lax.axis_index("fsdp")
    core, chip = plane % 2, plane // 2

    def pick(values, index, axis=0):
        return lax.dynamic_index_in_dim(values, index, axis, keepdims=False)

    halves = partial.reshape(planes // 2, 2, columns * rows, -1)
    other = swap(pick(halves, 1 - core, 1), "dp", 1)
    chips = (pick(halves, core, 1).astype(F32) + other.astype(F32)).astype(partial.dtype)
    arrived = [swap(pick(chips, chip ^ m), "dp", 2 * m) for m in range(1, planes // 2)]
    own = pick(chips, chip).astype(F32)
    for part in arrived:
        own = own + part.astype(F32)
    own = own.astype(partial.dtype).reshape(columns, rows, -1)
    arrived = [swap(pick(own, column ^ k), "fsdp", k) for k in range(1, columns)]
    own = pick(own, column).astype(F32)
    for part in arrived:
        own = own + part.astype(F32)
    return own


def scatter(partial):
    partial = lax.psum_scatter(partial, "dp", scatter_dimension=0, tiled=True)
    return lax.psum_scatter(partial, "fsdp", scatter_dimension=0, tiled=True)


def total_over_devices(values):
    for axis, flips in (("dp", [1]), ("dp", range(2, lax.axis_size("dp"), 2)), ("fsdp", range(1, lax.axis_size("fsdp")))):
        parts = [values] + [swap(values, axis, flip) for flip in flips]
        while len(parts) > 1:
            parts = [a + b for a, b in zip(parts[::2], parts[1::2])]
        values = parts[0]
    return values


def per_device(
    layer_input, cotangent, doc_lengths, pad_tail,
    query_weight, query_bias, key_weight, value_weight, value_bias,
    merge_weight, merge_bias, first_gain, first_shift,
    inner_weight, inner_bias, outer_weight, outer_bias, second_gain, second_shift,
):
    seqs, _, width = layer_input.shape
    own = query_weight.shape[0]
    devices = width // own
    parts = inner_weight.shape[1] // width
    groups = width // GROUP

    vectors = [query_bias, value_bias, merge_bias, first_gain, first_shift, outer_bias, second_gain, second_shift]
    columns = jnp.concatenate([jnp.stack(vectors), inner_bias.reshape(parts, own)]).T
    columns = jnp.pad(columns, ((0, 0), (0, VEC - columns.shape[1])))
    triples = [
        mat[:, g * GROUP : (g + 1) * GROUP]
        for g in range(groups)
        for mat in (query_weight, key_weight, value_weight)
    ]
    near = quick_gather(jnp.concatenate(triples + [columns], axis=1))
    inner_own = inner_weight.reshape(own, devices, parts, own).transpose(0, 2, 1, 3).reshape(own, parts * width)
    outer_own = outer_weight.reshape(parts, own, width).transpose(1, 0, 2).reshape(own, parts * width)
    far = gather(jnp.concatenate([merge_weight, inner_own, outer_own], axis=1))

    segment, low, count = segments(doc_lengths, pad_tail)
    segc = jnp.broadcast_to(segment[:, :, None], (seqs, LEN, 128))
    segr = jnp.broadcast_to(segment[:, None, :], (seqs, 8, LEN))
    rowst = jnp.swapaxes(layer_input, 1, 2)

    vec_rows = near[:, 3 * width :].T.astype(F32)
    bias = jnp.stack([vec_rows[0], jnp.zeros((width,), F32), vec_rows[1]])
    bias = bias.reshape(3, groups, GROUP).transpose(1, 0, 2).reshape(1, 3 * width)
    bias = jnp.broadcast_to(bias, (8, 3 * width))
    vec = vec_rows[2:18]

    qkv, mixed, lse = attention_forward(layer_input, near, bias, segc, segr, low, count)
    tokens = seqs * LEN
    output, residual, mixed_grad, far_partial, sums, stats = middle(
        mixed.reshape(tokens, width), layer_input.reshape(tokens, width), cotangent.reshape(tokens, width), far, vec, pad_tail
    )
    far_grad = scatter(far_partial)
    valid_count = jnp.sum(LEN - pad_tail).astype(F32)
    stat_row = jnp.concatenate([jnp.sum(stats[:4], axis=1), valid_count[None], jnp.zeros((VEC - 5,), F32)])
    totals = total_over_devices(jnp.broadcast_to(stat_row, (8, VEC)))[0]
    dqkv, near_partial, near_columns = attention_backward(
        qkv, mixed, mixed_grad.reshape(mixed.shape), rowst, lse, segc, segr, sums, low, count
    )
    near_grad = quick_scatter(jnp.concatenate([near_partial, near_columns], axis=1)).astype(F32)
    input_gradient = residual + dot(dqkv.reshape(tokens, 3 * width), near[:, : 3 * width], 1, 1)

    mine = near_grad[:, 3 * width :].T
    inner_bias_gradient = mine[8 : 8 + parts].reshape(parts * own)
    triple = near_grad[:, : 3 * width].reshape(own, groups, 3, GROUP)
    query_grad, key_grad, value_grad = (triple[:, :, k].reshape(own, width) for k in range(3))
    far_grad = far_grad.astype(F32)
    inner_grad = far_grad[:, width : (1 + parts) * width]
    inner_grad = inner_grad.reshape(own, parts, devices, own).transpose(0, 2, 1, 3).reshape(own, parts * width)
    outer_grad = far_grad[:, (1 + parts) * width :].reshape(own, parts, width).transpose(1, 0, 2)
    all_tokens = tokens * devices
    valid_total = totals[4]
    share = jnp.reshape(valid_total / all_tokens, (1,))
    layer_stats = jnp.concatenate([share, jnp.sqrt(totals[:4] / (valid_total * width))])
    return (
        output.reshape(layer_input.shape),
        input_gradient.reshape(layer_input.shape),
        query_grad,
        mine[6],
        key_grad,
        value_grad,
        mine[7],
        far_grad[:, :width],
        mine[5],
        mine[3],
        mine[4],
        inner_grad,
        inner_bias_gradient,
        outer_grad.reshape(parts * own, width),
        mine[2],
        mine[0],
        mine[1],
        layer_stats,
    )


def solution(mesh):
    matrix, vector, cube = P(AXES, None), P(AXES), P(AXES, None, None)
    in_specs = (
        cube, cube, matrix, vector,
        matrix, vector, matrix, matrix, vector,
        matrix, vector, vector, vector,
        matrix, vector, matrix, vector, vector, vector,
    )
    out_specs = (
        cube, cube,
        matrix, vector, matrix, matrix, vector,
        matrix, vector, vector, vector,
        matrix, vector, matrix, vector, vector, vector,
        P(),
    )
    return jax.shard_map(per_device, mesh=mesh, in_specs=in_specs, out_specs=out_specs, check_vma=False)
```

```python
import functools

import jax
import jax.numpy as jnp
from jax import lax
from jax.experimental import pallas as pl
from jax.experimental.pallas import tpu as pltpu
from jax.sharding import PartitionSpec as P

HEAD_DIM = 64
LEN = 1024
DOCS = 8
EPSILON = 1e-12
NEGATIVE = -1e30
ROOT_HALF = 0.7071067811865476
INV_ROOT_TWO_PI = 0.3989422804014327
AXES = ("dp", "fsdp")
F32 = jnp.float32
BF16 = jnp.bfloat16

GROUP = 256
HEADS_IN = GROUP // HEAD_DIM
TRIPLE = 3 * GROUP
QB = 256
CHUNK = 256
VEC = 128
DIGITS = 8


def dot(left, right, left_dim=1, right_dim=0):
    return lax.dot_general(
        left, right, (((left_dim,), (right_dim,)), ((), ())), preferred_element_type=F32
    )


def head_masks():
    lane = lax.broadcasted_iota(jnp.int32, (1, GROUP), 1) // HEAD_DIM
    return [lane == h for h in range(HEADS_IN)]


def cost(flops, moved):
    return pl.CostEstimate(flops=int(flops), bytes_accessed=int(moved), transcendentals=0)


def segments(doc_lengths, pad_tail):
    ends = jnp.cumsum(doc_lengths, axis=1)
    limit = (LEN - pad_tail)[:, None]
    places = jnp.arange(LEN, dtype=jnp.int32)
    segment = jnp.sum((places[None, :, None] >= ends[:, None, :]).astype(jnp.int32), axis=2)
    segment = jnp.where(places[None] < limit, segment, DOCS)
    borders = jnp.concatenate(
        [jnp.zeros_like(limit), jnp.minimum(ends, limit), limit, jnp.full_like(limit, LEN)], axis=1
    )[:, None, :]
    first = (jnp.arange(LEN // QB, dtype=jnp.int32) * QB)[None, :, None]
    low = jnp.max(jnp.where(borders <= first, borders, 0), axis=2)
    high = jnp.min(jnp.where(borders > first + QB - 1, borders, LEN), axis=2)
    low = (low // 128) * 128
    count = (high - low + CHUNK - 1) // CHUNK
    low = jnp.minimum(low, LEN - CHUNK * count)
    return segment, low.astype(jnp.int32), count.astype(jnp.int32)


def forward_kernel(
    low_ref, count_ref, rows_ref, w_ref, bias_ref, segc_ref, segr_ref,
    qkv_ref, mixed_ref, lse_ref, keyt_ref,
):
    s = pl.program_id(0)
    qkv_ref[...] = (dot(rows_ref[...], w_ref[...]) + bias_ref[0:1, :]).astype(BF16)
    keyt_ref[...] = qkv_ref[:, GROUP : 2 * GROUP].T
    masks = head_masks()

    def block(i, carry):
        start = pl.multiple_of(i * QB, QB)
        queries = qkv_ref[pl.ds(start, QB), :GROUP] * BF16(HEAD_DIM**-0.5)
        zero = jnp.zeros_like(queries)
        own = segc_ref[pl.ds(start, QB), :][:, :1]
        low = pl.multiple_of(low_ref[s, i], 128)
        count = count_ref[s, i]
        for c in range(1, LEN // CHUNK + 1):

            @pl.when(count == c)
            def _():
                span = pl.ds(low, CHUNK * c)
                keys = keyt_ref[:, span]
                values = qkv_ref[span, 2 * GROUP :]
                allowed = own == segr_ref[0:1, span]
                lane = lax.broadcasted_iota(jnp.int32, (QB, 128), 1)
                mixed = None
                for h in range(HEADS_IN):
                    scores = dot(jnp.where(masks[h], queries, zero), keys)
                    scores = jnp.where(allowed, scores, NEGATIVE)
                    top = jnp.max(scores, axis=1, keepdims=True)
                    expo = jnp.exp(scores - top)
                    total = jnp.sum(expo, axis=1, keepdims=True)
                    part = dot(expo.astype(BF16), values) * (1.0 / total)
                    logsum = top + jnp.log(total)
                    if h == 0:
                        mixed, sums = part, jnp.broadcast_to(logsum, (QB, 128))
                    else:
                        mixed, sums = jnp.where(masks[h], part, mixed), jnp.where(lane == h, logsum, sums)
                mixed_ref[pl.ds(start, QB), :] = mixed.astype(BF16)
                lse_ref[:, pl.ds(start, QB)] = sums.T[:8]

        return carry

    lax.fori_loop(0, LEN // QB, block, 0)


def attention_forward(rows, w, bias, segc, segr, low, count):
    seqs, _, width = rows.shape
    groups = width // GROUP
    return pl.pallas_call(
        forward_kernel,
        grid_spec=pltpu.PrefetchScalarGridSpec(
            num_scalar_prefetch=2,
            grid=(seqs, groups),
            in_specs=[
                pl.BlockSpec((None, LEN, width), lambda s, g, *_: (s, 0, 0)),
                pl.BlockSpec((width, TRIPLE), lambda s, g, *_: (0, g)),
                pl.BlockSpec((8, TRIPLE), lambda s, g, *_: (0, g)),
                pl.BlockSpec((None, LEN, 128), lambda s, g, *_: (s, 0, 0)),
                pl.BlockSpec((None, 8, LEN), lambda s, g, *_: (s, 0, 0)),
            ],
            out_specs=[
                pl.BlockSpec((None, LEN, TRIPLE), lambda s, g, *_: (s, 0, g)),
                pl.BlockSpec((None, LEN, GROUP), lambda s, g, *_: (s, 0, g)),
                pl.BlockSpec((None, None, 8, LEN), lambda s, g, *_: (s, g, 0, 0)),
            ],
            scratch_shapes=[pltpu.VMEM((GROUP, LEN), BF16)],
        ),
        out_shape=[
            jax.ShapeDtypeStruct((seqs, LEN, 3 * width), BF16),
            jax.ShapeDtypeStruct((seqs, LEN, width), BF16),
            jax.ShapeDtypeStruct((seqs, groups, 8, LEN), F32),
        ],
        compiler_params=pltpu.CompilerParams(vmem_limit_bytes=48 * 2**20),
        cost_estimate=cost(2 * seqs * LEN * width * (3 * width + 16 * LEN), seqs * LEN * width * 10),
        name="attention_forward",
    )(low, count, rows, w, bias, segc, segr)


def backward_kernel(
    chips,
    low_ref, count_ref, pad_ref, plane_ref, qkv_ref, mixed_ref, grad_ref, rows_ref, lse_ref, segc_ref, segr_ref, vec_ref, stats_ref,
    dqkv_ref, keep_ref, send_ref,
    q_ref, qt_ref, gt_ref, kt_ref, dqt_ref, acc_ref, delta_ref, sums_ref, stage_ref, columns_ref, rowst_ref, sem,
):
    s, g = pl.program_id(0), pl.program_id(1)
    masks = head_masks()

    @pl.when(g == 0)
    def _():
        rowst_ref[...] = rows_ref[...].T

    @pl.when((g == 0) & (s == 0))
    def _():
        sums_ref[...] = jnp.zeros_like(sums_ref)
        sums_ref[:16, :] = vec_ref[...]

    grad = grad_ref[...]
    prod = grad.astype(F32) * mixed_ref[...].astype(F32)
    coarse = prod.astype(BF16)
    fine = (prod - coarse.astype(F32)).astype(BF16)
    pick = lax.broadcasted_iota(jnp.int32, (8, GROUP), 1) // HEAD_DIM
    pick = (pick == lax.broadcasted_iota(jnp.int32, (8, GROUP), 0)).astype(F32).astype(BF16)
    delta_ref[...] = dot(pick, coarse, 1, 1) + dot(pick, fine, 1, 1)
    queries = qkv_ref[:, :GROUP] * BF16(HEAD_DIM**-0.5)
    q_ref[...] = queries
    qt_ref[...] = queries.T
    gt_ref[...] = grad.T
    kt_ref[...] = qkv_ref[:, GROUP : 2 * GROUP].T
    dqt_ref[...] = jnp.zeros_like(dqt_ref)

    def block(i, carry):
        start = pl.multiple_of(i * QB, QB)
        mine = pl.ds(start, QB)
        keys = qkv_ref[mine, GROUP : 2 * GROUP]
        values = qkv_ref[mine, 2 * GROUP :]
        zero = jnp.zeros_like(keys)
        own = segc_ref[mine, :][:, :1]
        low = pl.multiple_of(low_ref[s, i], 128)
        count = count_ref[s, i]
        for c in range(1, LEN // CHUNK + 1):

            @pl.when(count == c)
            def _():
                span = pl.ds(low, CHUNK * c)
                allowed = own == segr_ref[0:1, span]
                dkey = dvalue = None
                for h in range(HEADS_IN):
                    scores = dot(jnp.where(masks[h], keys, zero), qt_ref[:, span])
                    probs = jnp.exp(jnp.where(allowed, scores, NEGATIVE) - lse_ref[h : h + 1, span])
                    pgrad = dot(jnp.where(masks[h], values, zero), gt_ref[:, span])
                    low_score = (probs * (pgrad - delta_ref[h : h + 1, span])).astype(BF16)
                    v_part = dot(probs.astype(BF16), grad_ref[span, :])
                    k_part = dot(low_score, q_ref[span, :])
                    head = slice(h * HEAD_DIM, (h + 1) * HEAD_DIM)
                    dqt_ref[head, span] += dot(kt_ref[head, mine], low_score)
                    if h == 0:
                        dkey, dvalue = k_part, v_part
                    else:
                        dkey, dvalue = jnp.where(masks[h], k_part, dkey), jnp.where(masks[h], v_part, dvalue)
                dqkv_ref[mine, GROUP : 2 * GROUP] = dkey.astype(BF16)
                dqkv_ref[mine, 2 * GROUP :] = dvalue.astype(BF16)

        return carry

    lax.fori_loop(0, LEN // QB, block, 0)
    dqkv_ref[:, :GROUP] = (dqt_ref[...] * HEAD_DIM**-0.5).astype(BF16).T
    dqkv = dqkv_ref[...]
    dw = dot(rowst_ref[...], dqkv)
    sums = jnp.sum(dqkv.astype(F32), axis=0, keepdims=True)
    lanes = pl.ds(pl.multiple_of(g * GROUP, GROUP), GROUP)
    sums_ref[6:7, lanes] += sums[:, :GROUP]
    sums_ref[7:8, lanes] += sums[:, 2 * GROUP :]

    @pl.when(s == 0)
    def _():
        acc_ref[g] = dw

    @pl.when(s > 0)
    def _():
        acc_ref[g] += dw

    last_s, last_g = pl.num_programs(0) - 1, pl.num_programs(1) - 1

    def copies(source, lanes, first_sem):
        if chips == 0:
            return [pltpu.make_async_copy(source, keep_ref.at[0, :, lanes], sem.at[first_sem])]
        rows = source.shape[0] // (2 * chips)
        core, chip = plane_ref[0] & 1, lax.shift_right_logical(plane_ref[0], 1)
        moves = []
        for m in range(chips):
            for side, target in enumerate((keep_ref, send_ref)):
                owner = 2 * (chip ^ m) + (core ^ side)
                piece = source.at[pl.ds(pl.multiple_of(owner * rows, rows), rows), :]
                moves.append(pltpu.make_async_copy(piece, target.at[m, :, lanes], sem.at[first_sem + 2 * m + side]))
        return moves

    def group_copies(group):
        return copies(stage_ref, pl.ds(pl.multiple_of(group * TRIPLE, TRIPLE), TRIPLE), 0)

    @pl.when(s == last_s)
    def _():
        @pl.when(g > 0)
        def _():
            for move in group_copies(g - 1):
                move.wait()

        stage_ref[...] = acc_ref[g].astype(BF16)
        for move in group_copies(g):
            move.start()

    @pl.when((g == last_g) & (s == last_s))
    def _():
        for row in range(4):
            value = jnp.sum(stats_ref[row : row + 1, :], axis=1, keepdims=True)
            sums_ref[16 + row : 17 + row, :] = jnp.broadcast_to(value, (1, sums_ref.shape[1]))
        tokens = pl.num_programs(0) * LEN
        for seq in range(pad_ref.shape[0]):
            tokens -= pad_ref[seq]
        for row in range(DIGITS):
            digit = (lax.shift_right_logical(tokens, 3 * row) & 7).astype(F32)
            sums_ref[20 + row : 21 + row, :] = jnp.full((1, sums_ref.shape[1]), digit)
        columns_ref[...] = sums_ref[...].T.astype(BF16)
        width = sums_ref.shape[1]
        moves = copies(columns_ref, slice(3 * width, 3 * width + VEC), max(1, 2 * chips))
        for move in moves:
            move.start()
        for move in group_copies(g) + moves:
            move.wait()


def attention_backward(qkv, mixed, grad, rows, lse, segc, segr, vec, stats, low, count, pad, chips):
    seqs, _, width = mixed.shape
    groups = width // GROUP
    plane = lax.axis_index("dp").astype(jnp.int32).reshape(1)
    packed = (max(1, chips), width // max(1, 2 * chips), 3 * width + VEC)
    return pl.pallas_call(
        functools.partial(backward_kernel, chips),
        grid_spec=pltpu.PrefetchScalarGridSpec(
            num_scalar_prefetch=4,
            grid=(seqs, groups),
            in_specs=[
                pl.BlockSpec((None, LEN, TRIPLE), lambda s, g, *_: (s, 0, g)),
                pl.BlockSpec((None, LEN, GROUP), lambda s, g, *_: (s, 0, g)),
                pl.BlockSpec((None, LEN, GROUP), lambda s, g, *_: (s, 0, g)),
                pl.BlockSpec((None, LEN, width), lambda s, g, *_: (s, 0, 0)),
                pl.BlockSpec((None, None, 8, LEN), lambda s, g, *_: (s, g, 0, 0)),
                pl.BlockSpec((None, LEN, 128), lambda s, g, *_: (s, 0, 0)),
                pl.BlockSpec((None, 8, LEN), lambda s, g, *_: (s, 0, 0)),
                pl.BlockSpec((16, width), lambda s, g, *_: (0, 0)),
                pl.BlockSpec((8, width), lambda s, g, *_: (0, 0)),
            ],
            out_specs=[
                pl.BlockSpec((None, LEN, TRIPLE), lambda s, g, *_: (s, 0, g)),
                pl.BlockSpec(memory_space=pl.ANY),
                pl.BlockSpec(memory_space=pl.ANY),
            ],
            scratch_shapes=[
                pltpu.VMEM((LEN, GROUP), BF16),
                pltpu.VMEM((GROUP, LEN), BF16),
                pltpu.VMEM((GROUP, LEN), BF16),
                pltpu.VMEM((GROUP, LEN), BF16),
                pltpu.VMEM((GROUP, LEN), F32),
                pltpu.VMEM((groups, width, TRIPLE), F32),
                pltpu.VMEM((8, LEN), F32),
                pltpu.VMEM((VEC, width), F32),
                pltpu.VMEM((width, TRIPLE), BF16),
                pltpu.VMEM((width, VEC), BF16),
                pltpu.VMEM((width, LEN), BF16),
                pltpu.SemaphoreType.DMA((2 * max(1, 2 * chips),)),
            ],
        ),
        out_shape=[
            jax.ShapeDtypeStruct((seqs, LEN, 3 * width), BF16),
            jax.ShapeDtypeStruct(packed, BF16),
            jax.ShapeDtypeStruct(packed if chips else (8, 128), BF16),
        ],
        compiler_params=pltpu.CompilerParams(vmem_limit_bytes=48 * 2**20),
        cost_estimate=cost(2 * seqs * LEN * width * (3 * width + 32 * LEN), seqs * LEN * width * 20),
        name="attention_backward",
    )(low, count, pad, plane, qkv, mixed, grad, rows, lse, segc, segr, vec, stats)


def mean(values):
    return jnp.mean(values, axis=1, keepdims=True)


def normed_of(values):
    centred = values - mean(values)
    inverse = lax.rsqrt(mean(centred * centred) + EPSILON)
    return centred * inverse, inverse


def norm_backward(scaled, normed, inverse):
    return inverse * (scaled - mean(scaled) - normed * mean(scaled * normed))


def add_rows(sums_ref, row, values):
    sums_ref[row] += jnp.sum(values.reshape(-1, 8, values.shape[1]), axis=0)


class Blocks:
    def __init__(self, wide_ref, held_ref, sem, first_step):
        self.wide_ref, self.held_ref, self.sem, self.first_step = wide_ref, held_ref, sem, first_step

    def copy(self, k):
        width = self.held_ref.shape[2]
        columns = pl.ds(pl.multiple_of(k * width, width), width)
        return pltpu.make_async_copy(self.wide_ref.at[:, columns], self.held_ref.at[k], self.sem.at[k])

    def start(self, order):
        @pl.when(self.first_step)
        def _():
            for k in order:
                self.copy(k).start()

    def wait(self, k):
        @pl.when(self.first_step)
        def _():
            self.copy(k).wait()


def send_block(acc_ref, stage_ref, dw_ref, sem, k, first, last_step, turned):
    width = stage_ref.shape[1]

    def copy(k):
        columns = pl.ds(pl.multiple_of(k * width, width), width)
        slot = lax.rem(k, 2)
        return pltpu.make_async_copy(stage_ref.at[slot], dw_ref.at[:, columns], sem.at[slot])

    @pl.when(last_step)
    def _():
        @pl.when(k >= first + 2)
        def _():
            copy(k - 2).wait()

        value = acc_ref[k].astype(BF16)
        stage_ref[lax.rem(k, 2)] = value.T if turned else value
        copy(k).start()


def upper_kernel(
    parts, width, tokens,
    pad_ref, mixed_ref, rows_ref, cot_ref, w_ref, vec_ref,
    out_ref, normed_ref, inverse_ref, upper_ref, slope_ref, dw_ref, sums_ref, stats_ref,
    held_ref, hidden_ref, low_ref, wide_ref, acc_ref, stage_ref, part_ref, w_sem, sem,
):
    i = pl.program_id(0)
    last = i == pl.num_programs(0) - 1
    per_seq = LEN // tokens
    weights = Blocks(w_ref, held_ref, w_sem, i == 0)
    weights.start([0] + [k + j for j in range(parts) for k in (1, 1 + parts)])

    @pl.when(i == 0)
    def _():
        acc_ref[...] = jnp.zeros_like(acc_ref)
        part_ref[...] = jnp.zeros_like(part_ref)

    def vector(row):
        return vec_ref[row : row + 1, :]

    def valid_of():
        place = (i % per_seq) * tokens + lax.broadcasted_iota(jnp.int32, (tokens, 1), 0)
        return (place < LEN - pad_ref[i // per_seq]).astype(F32)

    weights.wait(0)
    wide_ref[...] = dot(mixed_ref[...], held_ref[0])

    valid = valid_of()
    rows = rows_ref[...].astype(F32)
    branch = wide_ref[...] + vector(0)
    add_rows(part_ref, 3, valid * rows * rows)
    add_rows(part_ref, 4, valid * branch * branch)
    normed, inverse = normed_of(rows + branch)
    normed_ref[...] = normed
    inverse_ref[...] = jnp.broadcast_to(inverse, (tokens, 128))
    first = normed * vector(1) + vector(2)
    low_ref[...] = first.astype(BF16)
    wide_ref[...] = first + vector(3)

    def feed(j, carry):
        weights.wait(1 + j)
        weights.wait(1 + parts + j)
        inner = dot(low_ref[...], held_ref[1 + j]) + vec_ref[pl.ds(6 + j, 1), :]
        half = 0.5 * (1.0 + lax.erf(inner * ROOT_HALF))
        hidden = (inner * half).astype(BF16)
        hidden_ref[j] = hidden
        slope = half + inner * jnp.exp(-0.5 * inner * inner) * INV_ROOT_TWO_PI
        slope_ref[:, pl.ds(pl.multiple_of(j * width, width), width)] = slope.astype(BF16)
        wide_ref[...] += dot(hidden, held_ref[1 + parts + j])
        return carry

    lax.fori_loop(0, parts, feed, 0)

    valid = valid_of()
    total = wide_ref[...]
    second = total - (normed_ref[...] * vector(1) + vector(2))
    add_rows(part_ref, 5, valid * second * second)
    normed, inverse = normed_of(total)
    result = normed * vector(4) + vector(5)
    add_rows(part_ref, 6, valid * result * result)
    out_ref[...] = result.astype(BF16)
    upstream = cot_ref[...].astype(F32) * valid
    add_rows(part_ref, 0, upstream * normed)
    add_rows(part_ref, 1, upstream)
    upper = norm_backward(upstream * vector(4), normed, inverse)
    upper_ref[...] = upper
    upper_low = upper.astype(BF16)
    add_rows(part_ref, 2, upper_low.astype(F32))
    low_ref[...] = upper_low

    upper_t = low_ref[...].T

    def back(j, carry):
        acc_ref[j] += dot(upper_t, hidden_ref[j])
        send_block(acc_ref, stage_ref, dw_ref, sem, j, 0, last, True)
        return carry

    lax.fori_loop(0, parts, back, 0)

    @pl.when(last)
    def _():
        sums_ref[...] = jnp.zeros_like(sums_ref)
        for row in range(3):
            sums_ref[row : row + 1, :] = jnp.sum(part_ref[row], axis=0, keepdims=True)
        for row in range(4):
            stats_ref[row : row + 1, :] = jnp.sum(part_ref[3 + row], axis=0, keepdims=True)
        stats_ref[4:, :] = jnp.zeros_like(stats_ref[4:, :])
        for k in (parts - 2, parts - 1):
            out_copy(stage_ref, dw_ref, sem, k).wait()


def lower_kernel(
    parts, width, tokens,
    mixed_ref, normed_ref, inverse_ref, upper_ref, slope_ref, w_ref, vec_ref, sums_in_ref,
    res_ref, mgrad_ref, dw_ref, sums_ref,
    held_ref, low_ref, first_ref, wide_ref, acc_ref, stage_ref, part_ref, w_sem, sem,
):
    i = pl.program_id(0)
    last = i == pl.num_programs(0) - 1
    weights = Blocks(w_ref, held_ref, w_sem, i == 0)
    weights.start([k + j for j in range(parts) for k in (1 + parts, 1)] + [0])

    @pl.when(i == 0)
    def _():
        acc_ref[...] = jnp.zeros_like(acc_ref)
        part_ref[...] = jnp.zeros_like(part_ref)

    def vector(row):
        return vec_ref[row : row + 1, :]

    upper = upper_ref[...]
    wide_ref[...] = upper
    low_ref[...] = upper.astype(BF16)
    first_ref[...] = (normed_ref[...] * vector(1) + vector(2)).astype(BF16)

    first_t = first_ref[...].T

    def back(j, carry):
        weights.wait(1 + parts + j)
        weights.wait(1 + j)
        slope = slope_ref[:, pl.ds(pl.multiple_of(j * width, width), width)].astype(F32)
        inner_low = (dot(low_ref[...], held_ref[1 + parts + j], 1, 1) * slope).astype(BF16)
        add_rows(part_ref, 3 + j, inner_low.astype(F32))
        acc_ref[1 + j] += dot(first_t, inner_low)
        wide_ref[...] += dot(inner_low, held_ref[1 + j], 1, 1)
        send_block(acc_ref, stage_ref, dw_ref, sem, 1 + j, 1, last, False)
        return carry

    lax.fori_loop(0, parts, back, 0)

    first_grad = wide_ref[...]
    normed = normed_ref[...]
    add_rows(part_ref, 0, first_grad * normed)
    add_rows(part_ref, 1, first_grad)
    residual = norm_backward(first_grad * vector(1), normed, inverse_ref[:, :1])
    res_ref[...] = residual
    branch_low = residual.astype(BF16)
    add_rows(part_ref, 2, branch_low.astype(F32))
    low_ref[...] = branch_low

    weights.wait(0)
    acc_ref[0] += dot(mixed_ref[...], low_ref[...], 0, 0)
    mgrad_ref[...] = dot(low_ref[...], held_ref[0], 1, 1).astype(BF16)

    @pl.when(last)
    def _():
        sums_ref[...] = sums_in_ref[...]
        for row in range(3):
            sums_ref[3 + row : 4 + row, :] = jnp.sum(part_ref[row], axis=0, keepdims=True)
        for j in range(parts):
            sums_ref[8 + j : 9 + j, :] = jnp.sum(part_ref[3 + j], axis=0, keepdims=True)
        for k in (parts - 1, parts):
            out_copy(stage_ref, dw_ref, sem, k).wait()
        stage_ref[0] = acc_ref[0].astype(BF16)
        out_copy(stage_ref, dw_ref, sem, 0).start()
        out_copy(stage_ref, dw_ref, sem, 0).wait()


def out_copy(stage_ref, dw_ref, sem, k):
    width = stage_ref.shape[1]
    return pltpu.make_async_copy(stage_ref.at[k % 2], dw_ref.at[:, k * width : (k + 1) * width], sem.at[k % 2])


def upper_half(mixed, rows, cotangent, w, vec, pad, tokens=512):
    count, width = mixed.shape
    parts = (w.shape[1] // width - 1) // 2

    def block(columns):
        return pl.BlockSpec((tokens, columns), lambda i, *_: (i, 0))

    def fixed(*shape):
        return pl.BlockSpec(shape, lambda i, *_: (0, 0))

    anywhere = pl.BlockSpec(memory_space=pl.ANY)
    return pl.pallas_call(
        functools.partial(upper_kernel, parts, width, tokens),
        grid_spec=pltpu.PrefetchScalarGridSpec(
            num_scalar_prefetch=1,
            grid=(count // tokens,),
            in_specs=[block(width), block(width), block(width), anywhere, fixed(16, width)],
            out_specs=[
                block(width), block(width), block(128), block(width), block(parts * width), anywhere,
                fixed(16, width), fixed(8, width),
            ],
            scratch_shapes=[
                pltpu.VMEM((1 + 2 * parts, width, width), BF16),
                pltpu.VMEM((parts, tokens, width), BF16),
                pltpu.VMEM((tokens, width), BF16),
                pltpu.VMEM((tokens, width), F32),
                pltpu.VMEM((parts, width, width), F32),
                pltpu.VMEM((2, width, width), BF16),
                pltpu.VMEM((8, 8, width), F32),
                pltpu.SemaphoreType.DMA((1 + 2 * parts,)),
                pltpu.SemaphoreType.DMA((2,)),
            ],
        ),
        out_shape=[
            jax.ShapeDtypeStruct((count, width), BF16),
            jax.ShapeDtypeStruct((count, width), F32),
            jax.ShapeDtypeStruct((count, 128), F32),
            jax.ShapeDtypeStruct((count, width), F32),
            jax.ShapeDtypeStruct((count, parts * width), BF16),
            jax.ShapeDtypeStruct((width, parts * width), BF16),
            jax.ShapeDtypeStruct((16, width), F32),
            jax.ShapeDtypeStruct((8, width), F32),
        ],
        compiler_params=pltpu.CompilerParams(vmem_limit_bytes=60 * 2**20),
        cost_estimate=cost(2 * count * width * width * (1 + 3 * parts), count * width * 40 + 4 * w.size),
        name="upper_half",
    )(pad, mixed, rows, cotangent, w, vec)


def lower_half(mixed, normed, inverse, upper, slope, w, vec, sums, tokens=512):
    count, width = mixed.shape
    parts = (w.shape[1] // width - 1) // 2

    def block(columns):
        return pl.BlockSpec((tokens, columns), lambda i: (i, 0))

    def fixed(*shape):
        return pl.BlockSpec(shape, lambda i: (0, 0))

    anywhere = pl.BlockSpec(memory_space=pl.ANY)
    return pl.pallas_call(
        functools.partial(lower_kernel, parts, width, tokens),
        grid=(count // tokens,),
        in_specs=[
            block(width), block(width), block(128), block(width), block(parts * width), anywhere,
            fixed(16, width), fixed(16, width),
        ],
        out_specs=[block(width), block(width), anywhere, fixed(16, width)],
        scratch_shapes=[
            pltpu.VMEM((1 + 2 * parts, width, width), BF16),
            pltpu.VMEM((tokens, width), BF16),
            pltpu.VMEM((tokens, width), BF16),
            pltpu.VMEM((tokens, width), F32),
            pltpu.VMEM((1 + parts, width, width), F32),
            pltpu.VMEM((2, width, width), BF16),
            pltpu.VMEM((3 + parts, 8, width), F32),
            pltpu.SemaphoreType.DMA((1 + 2 * parts,)),
            pltpu.SemaphoreType.DMA((2,)),
        ],
        out_shape=[
            jax.ShapeDtypeStruct((count, width), F32),
            jax.ShapeDtypeStruct((count, width), BF16),
            jax.ShapeDtypeStruct((width, (1 + parts) * width), BF16),
            jax.ShapeDtypeStruct((16, width), F32),
        ],
        compiler_params=pltpu.CompilerParams(vmem_limit_bytes=60 * 2**20),
        cost_estimate=cost(2 * count * width * width * (2 + 3 * parts), count * width * 40 + 4 * w.size),
        name="lower_half",
    )(mixed, normed, inverse, upper, slope, w, vec, sums)


def gather(shard):
    return lax.all_gather(shard, AXES, axis=0, tiled=True)


def swap(values, axis, flip):
    return lax.ppermute(values, axis, [(d, d ^ flip) for d in range(lax.axis_size(axis))])


def place_kernel(columns, lines, where_ref, *refs):
    sources, target = refs[:lines], refs[lines]
    plane, column = where_ref[0], where_ref[1]
    for m, source in enumerate(sources):
        for k in range(columns):
            target[(plane ^ m) * columns + (column ^ k)] = source[k]


def quick_gather(shard):
    planes, columns = lax.axis_size("dp"), lax.axis_size("fsdp")
    rows, width = shard.shape
    if not quick(rows):
        return gather(shard)
    column = jnp.stack([shard] + [swap(shard, "fsdp", k) for k in range(1, columns)])
    even = [column] + [swap(column, "dp", m) for m in range(2, planes, 2)]
    odd = [swap(part, "dp", 1) for part in even]
    sources = [part for pair in zip(even, odd) for part in pair]
    where = jnp.stack([lax.axis_index("dp"), lax.axis_index("fsdp")]).astype(jnp.int32)
    whole = pl.pallas_call(
        functools.partial(place_kernel, columns, len(sources)),
        grid_spec=pltpu.PrefetchScalarGridSpec(
            num_scalar_prefetch=1,
            grid=(1,),
            in_specs=[pl.BlockSpec((columns, rows, width), lambda i, *_: (0, 0, 0))] * len(sources),
            out_specs=pl.BlockSpec((planes * columns, rows, width), lambda i, *_: (0, 0, 0)),
        ),
        out_shape=jax.ShapeDtypeStruct((planes * columns, rows, width), shard.dtype),
        compiler_params=pltpu.CompilerParams(vmem_limit_bytes=48 * 2**20),
        name="place",
    )(where, *sources)
    return whole.reshape(planes * columns * rows, width)


def tree_sum(parts):
    parts = [part.astype(F32) for part in parts]
    while len(parts) > 1:
        parts = [a + b for a, b in zip(parts[::2], parts[1::2])]
    return parts[0]


def quick(rows):
    return lax.axis_size("dp") % 2 == 0 and rows % 8 == 0


def pick(values, index):
    return lax.dynamic_index_in_dim(values, index, 0, keepdims=False)


def over_planes(partial):
    return lax.psum_scatter(partial, "dp", scatter_dimension=0, tiled=True)


def over_columns(partial):
    return lax.psum_scatter(partial, "fsdp", scatter_dimension=0, tiled=True)


def join_planes(keep, send):
    other = swap(send, "dp", 1)
    parts = [tree_sum([keep[m], other[m]]).astype(keep.dtype) for m in range(keep.shape[0])]
    return tree_sum(parts[:1] + [swap(parts[m], "dp", 2 * m) for m in range(1, len(parts))]).astype(keep.dtype)


def blocks_for_columns(partial):
    columns = lax.axis_size("fsdp")
    blocks = partial.reshape(columns, partial.shape[0] // columns, partial.shape[1])
    return [pick(blocks, lax.axis_index("fsdp") ^ k) for k in range(columns)]


def join_blocks(blocks):
    return tree_sum(blocks[:1] + [swap(block, "fsdp", k) for k, block in enumerate(blocks) if k])


def per_device(
    layer_input, cotangent, doc_lengths, pad_tail,
    query_weight, query_bias, key_weight, value_weight, value_bias,
    merge_weight, merge_bias, first_gain, first_shift,
    inner_weight, inner_bias, outer_weight, outer_bias, second_gain, second_shift,
):
    seqs, _, width = layer_input.shape
    own = query_weight.shape[0]
    devices = width // own
    parts = inner_weight.shape[1] // width
    groups = width // GROUP

    vectors = [query_bias, value_bias, merge_bias, first_gain, first_shift, outer_bias, second_gain, second_shift]
    columns = jnp.concatenate([jnp.stack(vectors), inner_bias.reshape(parts, own)]).T
    columns = jnp.pad(columns, ((0, 0), (0, VEC - columns.shape[1])))
    triples = [
        mat[:, g * GROUP : (g + 1) * GROUP]
        for g in range(groups)
        for mat in (query_weight, key_weight, value_weight)
    ]
    segment, low, count = segments(doc_lengths, pad_tail)
    segc = jnp.broadcast_to(segment[:, :, None], (seqs, LEN, 128))
    segr = jnp.broadcast_to(segment[:, None, :], (seqs, 8, LEN))
    near = quick_gather(jnp.concatenate(triples + [columns], axis=1))
    inner_own = inner_weight.reshape(own, devices, parts, own).transpose(0, 2, 1, 3).reshape(own, parts * width)
    outer_own = outer_weight.reshape(parts, own, width).transpose(1, 0, 2).reshape(own, parts * width)
    far = gather(jnp.concatenate([merge_weight, inner_own, outer_own], axis=1))

    vec_rows = near[:, 3 * width :].T.astype(F32)
    bias = jnp.stack([vec_rows[0], jnp.zeros((width,), F32), vec_rows[1]])
    bias = bias.reshape(3, groups, GROUP).transpose(1, 0, 2).reshape(1, 3 * width)
    bias = jnp.broadcast_to(bias, (8, 3 * width))
    vec = vec_rows[2:18]

    qkv, mixed, lse = attention_forward(layer_input, near, bias, segc, segr, low, count)
    tokens = seqs * LEN
    flat_mixed = mixed.reshape(tokens, width)
    output, normed, inverse, upper, slope, outer_partial, sums, stats = upper_half(
        flat_mixed, layer_input.reshape(tokens, width), cotangent.reshape(tokens, width), far, vec, pad_tail
    )
    outer_grad = over_planes(outer_partial)
    residual, mixed_grad, inner_partial, sums = lower_half(flat_mixed, normed, inverse, upper, slope, far, vec, sums)
    inner_grad = over_planes(inner_partial)
    chips = lax.axis_size("dp") // 2 if quick(own) else 0
    dqkv, keep, send = attention_backward(
        qkv, mixed, mixed_grad.reshape(mixed.shape), layer_input, lse, segc, segr, sums, stats, low, count, pad_tail, chips
    )
    if chips:
        far_blocks = blocks_for_columns(jnp.concatenate([inner_grad, outer_grad], axis=1))
        keep, send, far_blocks = lax.optimization_barrier((keep, send, far_blocks))
        far_grad = join_blocks(far_blocks)
        near_grad = join_blocks(blocks_for_columns(join_planes(keep, send)))
    else:
        far_grad = over_columns(jnp.concatenate([inner_grad, outer_grad], axis=1)).astype(F32)
        near_grad = over_columns(over_planes(keep[0])).astype(F32)
    residual, far_grad = lax.optimization_barrier((residual, far_grad))
    input_gradient = residual + dot(dqkv.reshape(tokens, 3 * width), near[:, : 3 * width], 1, 1)

    mine = near_grad[:, 3 * width :].T
    inner_bias_gradient = mine[8 : 8 + parts].reshape(parts * own)
    triple = near_grad[:, : 3 * width].reshape(own, groups, 3, GROUP)
    query_grad, key_grad, value_grad = (triple[:, :, k].reshape(own, width) for k in range(3))
    inner_grad = far_grad[:, width : (1 + parts) * width]
    inner_grad = inner_grad.reshape(own, parts, devices, own).transpose(0, 2, 1, 3).reshape(own, parts * width)
    outer_grad = far_grad[:, (1 + parts) * width :].reshape(own, parts, width).transpose(1, 0, 2)
    all_tokens = tokens * devices
    if quick(own):
        totals = mine[16 : 20 + DIGITS, 0]
        valid_total = sum(totals[4 + digit] * 8.0**digit for digit in range(DIGITS))
    else:
        valid_own = jnp.sum(LEN - pad_tail).astype(F32)
        totals = lax.psum(jnp.concatenate([jnp.sum(stats[:4], axis=1), valid_own[None]]), AXES)
        valid_total = totals[4]
    share = jnp.reshape(valid_total / all_tokens, (1,))
    layer_stats = jnp.concatenate([share, jnp.sqrt(totals[:4] / (valid_total * width))])
    return (
        output.reshape(layer_input.shape),
        input_gradient.reshape(layer_input.shape),
        query_grad,
        mine[6],
        key_grad,
        value_grad,
        mine[7],
        far_grad[:, :width],
        mine[5],
        mine[3],
        mine[4],
        inner_grad,
        inner_bias_gradient,
        outer_grad.reshape(parts * own, width),
        mine[2],
        mine[0],
        mine[1],
        layer_stats,
    )


def solution(mesh):
    matrix, vector, cube = P(AXES, None), P(AXES), P(AXES, None, None)
    in_specs = (
        cube, cube, matrix, vector,
        matrix, vector, matrix, matrix, vector,
        matrix, vector, vector, vector,
        matrix, vector, matrix, vector, vector, vector,
    )
    out_specs = (
        cube, cube,
        matrix, vector, matrix, matrix, vector,
        matrix, vector, vector, vector,
        matrix, vector, matrix, vector, vector, vector,
        P(),
    )
    return jax.shard_map(per_device, mesh=mesh, in_specs=in_specs, out_specs=out_specs, check_vma=False)
```

```python
import functools

import jax
import jax.numpy as jnp
from jax import lax
from jax.experimental import pallas as pl
from jax.experimental.pallas import tpu as pltpu
from jax.sharding import PartitionSpec as P

HEAD_DIM = 64
LEN = 1024
DOCS = 8
EPSILON = 1e-12
NEGATIVE = -1e30
ROOT_HALF = 0.7071067811865476
INV_ROOT_TWO_PI = 0.3989422804014327
AXES = ("dp", "fsdp")
F32 = jnp.float32
BF16 = jnp.bfloat16

GROUP = 256
HEADS_IN = GROUP // HEAD_DIM
PAIR = 128
TRIPLE = 3 * GROUP
QB = 256
CHUNK = 256
VEC = 128
DIGITS = 8


def dot(left, right, left_dim=1, right_dim=0):
    return lax.dot_general(
        left, right, (((left_dim,), (right_dim,)), ((), ())), preferred_element_type=F32
    )


def head_masks(columns):
    lane = lax.broadcasted_iota(jnp.int32, (1, columns), 1) // HEAD_DIM
    return [lane == h for h in range(columns // HEAD_DIM)]


def cost(flops, moved):
    return pl.CostEstimate(flops=int(flops), bytes_accessed=int(moved), transcendentals=0)


def segments(doc_lengths, pad_tail):
    ends = jnp.cumsum(doc_lengths, axis=1)
    limit = (LEN - pad_tail)[:, None]
    places = jnp.arange(LEN, dtype=jnp.int32)
    segment = jnp.sum((places[None, :, None] >= ends[:, None, :]).astype(jnp.int32), axis=2)
    segment = jnp.where(places[None] < limit, segment, DOCS)
    borders = jnp.concatenate(
        [jnp.zeros_like(limit), jnp.minimum(ends, limit), limit, jnp.full_like(limit, LEN)], axis=1
    )[:, None, :]
    first = (jnp.arange(LEN // QB, dtype=jnp.int32) * QB)[None, :, None]
    low = jnp.max(jnp.where(borders <= first, borders, 0), axis=2)
    high = jnp.min(jnp.where(borders > first + QB - 1, borders, LEN), axis=2)
    low = (low // 128) * 128
    count = (high - low + CHUNK - 1) // CHUNK
    low = jnp.minimum(low, LEN - CHUNK * count)
    return segment, low.astype(jnp.int32), count.astype(jnp.int32)


def forward_kernel(
    low_ref, count_ref, rows_ref, w_ref, bias_ref, segc_ref, segr_ref,
    qkv_ref, mixed_ref, lse_ref, keyt_ref,
):
    s = pl.program_id(0)
    qkv_ref[...] = (dot(rows_ref[...], w_ref[...]) + bias_ref[0:1, :]).astype(BF16)
    keyt_ref[...] = qkv_ref[:, GROUP : 2 * GROUP].T
    masks = head_masks(GROUP)

    def block(i, carry):
        start = pl.multiple_of(i * QB, QB)
        queries = qkv_ref[pl.ds(start, QB), :GROUP] * BF16(HEAD_DIM**-0.5)
        zero = jnp.zeros_like(queries)
        own = segc_ref[pl.ds(start, QB), :][:, :1]
        low = pl.multiple_of(low_ref[s, i], 128)
        count = count_ref[s, i]
        for c in range(1, LEN // CHUNK + 1):

            @pl.when(count == c)
            def _():
                span = pl.ds(low, CHUNK * c)
                keys = keyt_ref[:, span]
                values = qkv_ref[span, 2 * GROUP :]
                allowed = own == segr_ref[0:1, span]
                lane = lax.broadcasted_iota(jnp.int32, (QB, 128), 1)
                mixed = None
                for h in range(HEADS_IN):
                    scores = dot(jnp.where(masks[h], queries, zero), keys)
                    scores = jnp.where(allowed, scores, NEGATIVE)
                    top = jnp.max(scores, axis=1, keepdims=True)
                    expo = jnp.exp(scores - top)
                    total = jnp.sum(expo, axis=1, keepdims=True)
                    part = dot(expo.astype(BF16), values) * (1.0 / total)
                    logsum = top + jnp.log(total)
                    if h == 0:
                        mixed, sums = part, jnp.broadcast_to(logsum, (QB, 128))
                    else:
                        mixed, sums = jnp.where(masks[h], part, mixed), jnp.where(lane == h, logsum, sums)
                mixed_ref[pl.ds(start, QB), :] = mixed.astype(BF16)
                lse_ref[:, pl.ds(start, QB)] = sums.T[:8]

        return carry

    lax.fori_loop(0, LEN // QB, block, 0)


def attention_forward(rows, w, bias, segc, segr, low, count):
    seqs, _, width = rows.shape
    groups = width // GROUP
    return pl.pallas_call(
        forward_kernel,
        grid_spec=pltpu.PrefetchScalarGridSpec(
            num_scalar_prefetch=2,
            grid=(seqs, groups),
            in_specs=[
                pl.BlockSpec((None, LEN, width), lambda s, g, *_: (s, 0, 0)),
                pl.BlockSpec((width, TRIPLE), lambda s, g, *_: (0, g)),
                pl.BlockSpec((8, TRIPLE), lambda s, g, *_: (0, g)),
                pl.BlockSpec((None, LEN, 128), lambda s, g, *_: (s, 0, 0)),
                pl.BlockSpec((None, 8, LEN), lambda s, g, *_: (s, 0, 0)),
            ],
            out_specs=[
                pl.BlockSpec((None, LEN, TRIPLE), lambda s, g, *_: (s, 0, g)),
                pl.BlockSpec((None, LEN, GROUP), lambda s, g, *_: (s, 0, g)),
                pl.BlockSpec((None, None, 8, LEN), lambda s, g, *_: (s, g, 0, 0)),
            ],
            scratch_shapes=[pltpu.VMEM((GROUP, LEN), BF16)],
        ),
        out_shape=[
            jax.ShapeDtypeStruct((seqs, LEN, 3 * width), BF16),
            jax.ShapeDtypeStruct((seqs, LEN, width), BF16),
            jax.ShapeDtypeStruct((seqs, groups, 8, LEN), F32),
        ],
        compiler_params=pltpu.CompilerParams(vmem_limit_bytes=48 * 2**20),
        cost_estimate=cost(2 * seqs * LEN * width * (3 * width + 16 * LEN), seqs * LEN * width * 10),
        name="attention_forward",
    )(low, count, rows, w, bias, segc, segr)


def backward_kernel(
    chips,
    low_ref, count_ref, pad_ref, plane_ref, qkv_ref, mixed_ref, grad_ref, rows_ref, lse_ref, segc_ref, segr_ref, vec_ref, stats_ref,
    dqkv_ref, keep_ref, send_ref,
    q_ref, qt_ref, gt_ref, kt_ref, dqt_ref, acc_ref, delta_ref, sums_ref, stage_ref, columns_ref, rowst_ref, sem,
):
    s, g = pl.program_id(0), pl.program_id(1)
    masks = head_masks(PAIR)

    @pl.when(g == 0)
    def _():
        rowst_ref[...] = rows_ref[...].T

    @pl.when((g == 0) & (s == 0))
    def _():
        sums_ref[...] = jnp.zeros_like(sums_ref)
        sums_ref[:16, :] = vec_ref[...]

    grad = grad_ref[...]
    prod = grad.astype(F32) * mixed_ref[...].astype(F32)
    coarse = prod.astype(BF16)
    fine = (prod - coarse.astype(F32)).astype(BF16)
    pick = lax.broadcasted_iota(jnp.int32, (8, GROUP), 1) // HEAD_DIM
    pick = (pick == lax.broadcasted_iota(jnp.int32, (8, GROUP), 0)).astype(F32).astype(BF16)
    delta_ref[...] = dot(pick, coarse, 1, 1) + dot(pick, fine, 1, 1)
    queries = qkv_ref[:, :GROUP] * BF16(HEAD_DIM**-0.5)
    q_ref[...] = queries
    qt_ref[...] = queries.T
    gt_ref[...] = grad.T
    kt_ref[...] = qkv_ref[:, GROUP : 2 * GROUP].T
    dqt_ref[...] = jnp.zeros_like(dqt_ref)

    def block(i, carry):
        start = pl.multiple_of(i * QB, QB)
        mine = pl.ds(start, QB)
        keys = qkv_ref[mine, GROUP : 2 * GROUP]
        values = qkv_ref[mine, 2 * GROUP :]
        zero = jnp.zeros((QB, PAIR), BF16)
        own = segc_ref[mine, :][:, :1]
        low = pl.multiple_of(low_ref[s, i], 128)
        count = count_ref[s, i]
        for c in range(1, LEN // CHUNK + 1):

            @pl.when(count == c)
            def _():
                span = pl.ds(low, CHUNK * c)
                allowed = own == segr_ref[0:1, span]
                for h in range(HEADS_IN):
                    mask, lanes = masks[h % 2], slice(h // 2 * PAIR, (h // 2 + 1) * PAIR)
                    scores = dot(jnp.where(mask, keys[:, lanes], zero), qt_ref[lanes, span])
                    probs = jnp.exp(jnp.where(allowed, scores, NEGATIVE) - lse_ref[h : h + 1, span])
                    pgrad = dot(jnp.where(mask, values[:, lanes], zero), gt_ref[lanes, span])
                    low_score = (probs * (pgrad - delta_ref[h : h + 1, span])).astype(BF16)
                    v_part = dot(probs.astype(BF16), grad_ref[span, lanes])
                    k_part = dot(low_score, q_ref[span, lanes])
                    head = slice(h * HEAD_DIM, (h + 1) * HEAD_DIM)
                    dqt_ref[head, span] += dot(kt_ref[head, mine], low_score)
                    if h % 2 == 0:
                        dkey, dvalue = k_part, v_part
                    else:
                        first = h // 2 * PAIR
                        dkey, dvalue = jnp.where(mask, k_part, dkey), jnp.where(mask, v_part, dvalue)
                        dqkv_ref[mine, GROUP + first : GROUP + first + PAIR] = dkey.astype(BF16)
                        dqkv_ref[mine, 2 * GROUP + first : 2 * GROUP + first + PAIR] = dvalue.astype(BF16)

        return carry

    lax.fori_loop(0, LEN // QB, block, 0)
    dqkv_ref[:, :GROUP] = (dqt_ref[...] * HEAD_DIM**-0.5).astype(BF16).T
    dqkv = dqkv_ref[...]
    dw = dot(rowst_ref[...], dqkv)
    sums = jnp.sum(dqkv.astype(F32), axis=0, keepdims=True)
    lanes = pl.ds(pl.multiple_of(g * GROUP, GROUP), GROUP)
    sums_ref[6:7, lanes] += sums[:, :GROUP]
    sums_ref[7:8, lanes] += sums[:, 2 * GROUP :]

    @pl.when(s == 0)
    def _():
        acc_ref[g] = dw

    @pl.when(s > 0)
    def _():
        acc_ref[g] += dw

    last_s, last_g = pl.num_programs(0) - 1, pl.num_programs(1) - 1

    def copies(source, lanes, first_sem):
        if chips == 0:
            return [pltpu.make_async_copy(source, keep_ref.at[0, :, lanes], sem.at[first_sem])]
        rows = source.shape[0] // (2 * chips)
        core, chip = plane_ref[0] & 1, lax.shift_right_logical(plane_ref[0], 1)
        moves = []
        for m in range(chips):
            for side, target in enumerate((keep_ref, send_ref)):
                owner = 2 * (chip ^ m) + (core ^ side)
                piece = source.at[pl.ds(pl.multiple_of(owner * rows, rows), rows), :]
                moves.append(pltpu.make_async_copy(piece, target.at[m, :, lanes], sem.at[first_sem + 2 * m + side]))
        return moves

    def group_copies(group):
        return copies(stage_ref, pl.ds(pl.multiple_of(group * TRIPLE, TRIPLE), TRIPLE), 0)

    @pl.when(s == last_s)
    def _():
        @pl.when(g > 0)
        def _():
            for move in group_copies(g - 1):
                move.wait()

        stage_ref[...] = acc_ref[g].astype(BF16)
        for move in group_copies(g):
            move.start()

    @pl.when((g == last_g) & (s == last_s))
    def _():
        for row in range(4):
            value = jnp.sum(stats_ref[row : row + 1, :], axis=1, keepdims=True)
            sums_ref[16 + row : 17 + row, :] = jnp.broadcast_to(value, (1, sums_ref.shape[1]))
        tokens = pl.num_programs(0) * LEN
        for seq in range(pad_ref.shape[0]):
            tokens -= pad_ref[seq]
        for row in range(DIGITS):
            digit = (lax.shift_right_logical(tokens, 3 * row) & 7).astype(F32)
            sums_ref[20 + row : 21 + row, :] = jnp.full((1, sums_ref.shape[1]), digit)
        columns_ref[...] = sums_ref[...].T.astype(BF16)
        width = sums_ref.shape[1]
        moves = copies(columns_ref, slice(3 * width, 3 * width + VEC), max(1, 2 * chips))
        for move in moves:
            move.start()
        for move in group_copies(g) + moves:
            move.wait()


def attention_backward(qkv, mixed, grad, rows, lse, segc, segr, vec, stats, low, count, pad, chips):
    seqs, _, width = mixed.shape
    groups = width // GROUP
    plane = lax.axis_index("dp").astype(jnp.int32).reshape(1)
    packed = (max(1, chips), width // max(1, 2 * chips), 3 * width + VEC)
    return pl.pallas_call(
        functools.partial(backward_kernel, chips),
        grid_spec=pltpu.PrefetchScalarGridSpec(
            num_scalar_prefetch=4,
            grid=(seqs, groups),
            in_specs=[
                pl.BlockSpec((None, LEN, TRIPLE), lambda s, g, *_: (s, 0, g)),
                pl.BlockSpec((None, LEN, GROUP), lambda s, g, *_: (s, 0, g)),
                pl.BlockSpec((None, LEN, GROUP), lambda s, g, *_: (s, 0, g)),
                pl.BlockSpec((None, LEN, width), lambda s, g, *_: (s, 0, 0)),
                pl.BlockSpec((None, None, 8, LEN), lambda s, g, *_: (s, g, 0, 0)),
                pl.BlockSpec((None, LEN, 128), lambda s, g, *_: (s, 0, 0)),
                pl.BlockSpec((None, 8, LEN), lambda s, g, *_: (s, 0, 0)),
                pl.BlockSpec((16, width), lambda s, g, *_: (0, 0)),
                pl.BlockSpec((8, width), lambda s, g, *_: (0, 0)),
            ],
            out_specs=[
                pl.BlockSpec((None, LEN, TRIPLE), lambda s, g, *_: (s, 0, g)),
                pl.BlockSpec(memory_space=pl.ANY),
                pl.BlockSpec(memory_space=pl.ANY),
            ],
            scratch_shapes=[
                pltpu.VMEM((LEN, GROUP), BF16),
                pltpu.VMEM((GROUP, LEN), BF16),
                pltpu.VMEM((GROUP, LEN), BF16),
                pltpu.VMEM((GROUP, LEN), BF16),
                pltpu.VMEM((GROUP, LEN), F32),
                pltpu.VMEM((groups, width, TRIPLE), F32),
                pltpu.VMEM((8, LEN), F32),
                pltpu.VMEM((VEC, width), F32),
                pltpu.VMEM((width, TRIPLE), BF16),
                pltpu.VMEM((width, VEC), BF16),
                pltpu.VMEM((width, LEN), BF16),
                pltpu.SemaphoreType.DMA((2 * max(1, 2 * chips),)),
            ],
        ),
        out_shape=[
            jax.ShapeDtypeStruct((seqs, LEN, 3 * width), BF16),
            jax.ShapeDtypeStruct(packed, BF16),
            jax.ShapeDtypeStruct(packed if chips else (8, 128), BF16),
        ],
        compiler_params=pltpu.CompilerParams(vmem_limit_bytes=48 * 2**20),
        cost_estimate=cost(2 * seqs * LEN * width * (3 * width + 32 * LEN), seqs * LEN * width * 20),
        name="attention_backward",
    )(low, count, pad, plane, qkv, mixed, grad, rows, lse, segc, segr, vec, stats)


def mean(values):
    return jnp.mean(values, axis=1, keepdims=True)


def normed_of(values):
    centred = values - mean(values)
    inverse = lax.rsqrt(mean(centred * centred) + EPSILON)
    return centred * inverse, inverse


def norm_backward(scaled, normed, inverse):
    return inverse * (scaled - mean(scaled) - normed * mean(scaled * normed))


def add_rows(sums_ref, row, values):
    sums_ref[row] += jnp.sum(values.reshape(-1, 8, values.shape[1]), axis=0)


class Blocks:
    def __init__(self, wide_ref, held_ref, sem, first_step):
        self.wide_ref, self.held_ref, self.sem, self.first_step = wide_ref, held_ref, sem, first_step

    def copy(self, k):
        width = self.held_ref.shape[2]
        columns = pl.ds(pl.multiple_of(k * width, width), width)
        return pltpu.make_async_copy(self.wide_ref.at[:, columns], self.held_ref.at[k], self.sem.at[k])

    def start(self, order):
        @pl.when(self.first_step)
        def _():
            for k in order:
                self.copy(k).start()

    def wait(self, k):
        @pl.when(self.first_step)
        def _():
            self.copy(k).wait()


def out_copy(stage_ref, dw_ref, sem, k):
    width = stage_ref.shape[1]
    columns = pl.ds(pl.multiple_of(k * width, width), width)
    slot = lax.rem(k, 2)
    return pltpu.make_async_copy(stage_ref.at[slot], dw_ref.at[:, columns], sem.at[slot])


def send_blocks(gradient, first, amount, stage_ref, dw_ref, sem):
    def step(j, carry):
        k = first + j

        @pl.when(j >= 2)
        def _():
            out_copy(stage_ref, dw_ref, sem, k - 2).wait()

        stage_ref[lax.rem(k, 2)] = gradient(j)
        out_copy(stage_ref, dw_ref, sem, k).start()
        return carry

    lax.fori_loop(0, amount, step, 0)


def upper_kernel(
    parts, width, tokens,
    pad_ref, mixed_ref, rows_ref, cot_ref, w_ref, vec_ref,
    out_ref, normed_ref, inverse_ref, upper_ref, slope_ref, dw_ref, sums_ref, stats_ref,
    held_ref, hidden_ref, low_ref, uppert_ref, stage_ref, part_ref, w_sem, sem,
):
    i = pl.program_id(0)
    last = i == pl.num_programs(0) - 1
    per_seq = LEN // tokens
    weights = Blocks(w_ref, held_ref, w_sem, i == 0)
    weights.start([0] + [k + j for j in range(parts) for k in (1, 1 + parts)])

    @pl.when(i == 0)
    def _():
        part_ref[...] = jnp.zeros_like(part_ref)

    def vector(row):
        return vec_ref[row : row + 1, :]

    def valid_of():
        place = (i % per_seq) * tokens + lax.broadcasted_iota(jnp.int32, (tokens, 1), 0)
        return (place < LEN - pad_ref[i // per_seq]).astype(F32)

    mine = pl.ds(pl.multiple_of(i * tokens, tokens), tokens)
    weights.wait(0)
    upper_ref[...] = dot(mixed_ref[...], held_ref[0])

    valid = valid_of()
    rows = rows_ref[...].astype(F32)
    branch = upper_ref[...] + vector(0)
    add_rows(part_ref, 3, valid * rows * rows)
    add_rows(part_ref, 4, valid * branch * branch)
    normed, inverse = normed_of(rows + branch)
    normed_ref[...] = normed
    inverse_ref[...] = jnp.broadcast_to(inverse, (tokens, 128))
    first = normed * vector(1) + vector(2)
    low_ref[...] = first.astype(BF16)
    upper_ref[...] = first + vector(3)

    def feed(j, carry):
        weights.wait(1 + j)
        weights.wait(1 + parts + j)
        inner = dot(low_ref[...], held_ref[1 + j]) + vec_ref[pl.ds(6 + j, 1), :]
        half = 0.5 * (1.0 + lax.erf(inner * ROOT_HALF))
        hidden = (inner * half).astype(BF16)
        hidden_ref[j, mine, :] = hidden
        slope = half + inner * jnp.exp(-0.5 * inner * inner) * INV_ROOT_TWO_PI
        slope_ref[:, pl.ds(pl.multiple_of(j * width, width), width)] = slope.astype(BF16)
        upper_ref[...] += dot(hidden, held_ref[1 + parts + j])
        return carry

    lax.fori_loop(0, parts, feed, 0)

    valid = valid_of()
    total = upper_ref[...]
    second = total - (normed_ref[...] * vector(1) + vector(2))
    add_rows(part_ref, 5, valid * second * second)
    normed, inverse = normed_of(total)
    result = normed * vector(4) + vector(5)
    add_rows(part_ref, 6, valid * result * result)
    out_ref[...] = result.astype(BF16)
    upstream = cot_ref[...].astype(F32) * valid
    add_rows(part_ref, 0, upstream * normed)
    add_rows(part_ref, 1, upstream)
    upper = norm_backward(upstream * vector(4), normed, inverse)
    upper_ref[...] = upper
    upper_low = upper.astype(BF16)
    add_rows(part_ref, 2, upper_low.astype(F32))
    uppert_ref[:, mine] = upper_low.T

    @pl.when(last)
    def _():
        sums_ref[...] = jnp.zeros_like(sums_ref)
        for row in range(3):
            sums_ref[row : row + 1, :] = jnp.sum(part_ref[row], axis=0, keepdims=True)
        for row in range(4):
            stats_ref[row : row + 1, :] = jnp.sum(part_ref[3 + row], axis=0, keepdims=True)
        stats_ref[4:, :] = jnp.zeros_like(stats_ref[4:, :])
        send_blocks(
            lambda j: dot(uppert_ref[...], hidden_ref[j]).astype(BF16).T, 0, parts, stage_ref, dw_ref, sem
        )
        for k in (parts - 2, parts - 1):
            out_copy(stage_ref, dw_ref, sem, k).wait()


def lower_kernel(
    parts, width, tokens,
    mixed_ref, normed_ref, inverse_ref, upper_ref, slope_ref, w_ref, vec_ref, sums_in_ref,
    res_ref, mgrad_ref, dw_ref, sums_ref,
    held_ref, low_ref, first_ref, acc_ref, stage_ref, part_ref, w_sem, sem,
):
    i = pl.program_id(0)
    last = i == pl.num_programs(0) - 1
    weights = Blocks(w_ref, held_ref, w_sem, i == 0)
    weights.start([k + j for j in range(parts) for k in (1 + parts, 1)] + [0])

    @pl.when(i == 0)
    def _():
        acc_ref[...] = jnp.zeros_like(acc_ref)
        part_ref[...] = jnp.zeros_like(part_ref)

    def vector(row):
        return vec_ref[row : row + 1, :]

    upper = upper_ref[...]
    res_ref[...] = upper
    low_ref[...] = upper.astype(BF16)
    first_ref[...] = (normed_ref[...] * vector(1) + vector(2)).astype(BF16)

    first_t = first_ref[...].T

    def back(j, carry):
        weights.wait(1 + parts + j)
        weights.wait(1 + j)
        slope = slope_ref[:, pl.ds(pl.multiple_of(j * width, width), width)].astype(F32)
        inner_low = (dot(low_ref[...], held_ref[1 + parts + j], 1, 1) * slope).astype(BF16)
        add_rows(part_ref, 3 + j, inner_low.astype(F32))
        acc_ref[1 + j] += dot(first_t, inner_low)
        res_ref[...] += dot(inner_low, held_ref[1 + j], 1, 1)

        @pl.when(last)
        def _():
            @pl.when(j >= 2)
            def _():
                out_copy(stage_ref, dw_ref, sem, j - 1).wait()

            stage_ref[lax.rem(1 + j, 2)] = acc_ref[1 + j].astype(BF16)
            out_copy(stage_ref, dw_ref, sem, 1 + j).start()

        return carry

    lax.fori_loop(0, parts, back, 0)

    first_grad = res_ref[...]
    normed = normed_ref[...]
    add_rows(part_ref, 0, first_grad * normed)
    add_rows(part_ref, 1, first_grad)
    residual = norm_backward(first_grad * vector(1), normed, inverse_ref[:, :1])
    res_ref[...] = residual
    branch_low = residual.astype(BF16)
    add_rows(part_ref, 2, branch_low.astype(F32))
    low_ref[...] = branch_low

    weights.wait(0)
    acc_ref[0] += dot(mixed_ref[...], low_ref[...], 0, 0)
    mgrad_ref[...] = dot(low_ref[...], held_ref[0], 1, 1).astype(BF16)

    @pl.when(last)
    def _():
        sums_ref[...] = sums_in_ref[...]
        for row in range(3):
            sums_ref[3 + row : 4 + row, :] = jnp.sum(part_ref[row], axis=0, keepdims=True)
        for j in range(parts):
            sums_ref[8 + j : 9 + j, :] = jnp.sum(part_ref[3 + j], axis=0, keepdims=True)
        for k in (parts - 1, parts):
            out_copy(stage_ref, dw_ref, sem, k).wait()
        stage_ref[0] = acc_ref[0].astype(BF16)
        out_copy(stage_ref, dw_ref, sem, 0).start()
        out_copy(stage_ref, dw_ref, sem, 0).wait()


def upper_half(mixed, rows, cotangent, w, vec, pad, tokens=512):
    count, width = mixed.shape
    parts = (w.shape[1] // width - 1) // 2

    def block(columns):
        return pl.BlockSpec((tokens, columns), lambda i, *_: (i, 0))

    def fixed(*shape):
        return pl.BlockSpec(shape, lambda i, *_: (0, 0))

    anywhere = pl.BlockSpec(memory_space=pl.ANY)
    return pl.pallas_call(
        functools.partial(upper_kernel, parts, width, tokens),
        grid_spec=pltpu.PrefetchScalarGridSpec(
            num_scalar_prefetch=1,
            grid=(count // tokens,),
            in_specs=[block(width), block(width), block(width), anywhere, fixed(16, width)],
            out_specs=[
                block(width), block(width), block(128), block(width), block(parts * width), anywhere,
                fixed(16, width), fixed(8, width),
            ],
            scratch_shapes=[
                pltpu.VMEM((1 + 2 * parts, width, width), BF16),
                pltpu.VMEM((parts, count, width), BF16),
                pltpu.VMEM((tokens, width), BF16),
                pltpu.VMEM((width, count), BF16),
                pltpu.VMEM((2, width, width), BF16),
                pltpu.VMEM((8, 8, width), F32),
                pltpu.SemaphoreType.DMA((1 + 2 * parts,)),
                pltpu.SemaphoreType.DMA((2,)),
            ],
        ),
        out_shape=[
            jax.ShapeDtypeStruct((count, width), BF16),
            jax.ShapeDtypeStruct((count, width), F32),
            jax.ShapeDtypeStruct((count, 128), F32),
            jax.ShapeDtypeStruct((count, width), F32),
            jax.ShapeDtypeStruct((count, parts * width), BF16),
            jax.ShapeDtypeStruct((width, parts * width), BF16),
            jax.ShapeDtypeStruct((16, width), F32),
            jax.ShapeDtypeStruct((8, width), F32),
        ],
        compiler_params=pltpu.CompilerParams(vmem_limit_bytes=60 * 2**20),
        cost_estimate=cost(2 * count * width * width * (1 + 3 * parts), count * width * 40 + 4 * w.size),
        name="upper_half",
    )(pad, mixed, rows, cotangent, w, vec)


def lower_half(mixed, normed, inverse, upper, slope, w, vec, sums, tokens=512):
    count, width = mixed.shape
    parts = (w.shape[1] // width - 1) // 2

    def block(columns):
        return pl.BlockSpec((tokens, columns), lambda i: (i, 0))

    def fixed(*shape):
        return pl.BlockSpec(shape, lambda i: (0, 0))

    anywhere = pl.BlockSpec(memory_space=pl.ANY)
    return pl.pallas_call(
        functools.partial(lower_kernel, parts, width, tokens),
        grid=(count // tokens,),
        in_specs=[
            block(width), block(width), block(128), block(width), block(parts * width), anywhere,
            fixed(16, width), fixed(16, width),
        ],
        out_specs=[block(width), block(width), anywhere, fixed(16, width)],
        scratch_shapes=[
            pltpu.VMEM((1 + 2 * parts, width, width), BF16),
            pltpu.VMEM((tokens, width), BF16),
            pltpu.VMEM((tokens, width), BF16),
            pltpu.VMEM((1 + parts, width, width), F32),
            pltpu.VMEM((2, width, width), BF16),
            pltpu.VMEM((3 + parts, 8, width), F32),
            pltpu.SemaphoreType.DMA((1 + 2 * parts,)),
            pltpu.SemaphoreType.DMA((2,)),
        ],
        out_shape=[
            jax.ShapeDtypeStruct((count, width), F32),
            jax.ShapeDtypeStruct((count, width), BF16),
            jax.ShapeDtypeStruct((width, (1 + parts) * width), BF16),
            jax.ShapeDtypeStruct((16, width), F32),
        ],
        compiler_params=pltpu.CompilerParams(vmem_limit_bytes=60 * 2**20),
        cost_estimate=cost(2 * count * width * width * (2 + 3 * parts), count * width * 40 + 4 * w.size),
        name="lower_half",
    )(mixed, normed, inverse, upper, slope, w, vec, sums)


def gather(shard):
    return lax.all_gather(shard, AXES, axis=0, tiled=True)


def swap(values, axis, flip):
    return lax.ppermute(values, axis, [(d, d ^ flip) for d in range(lax.axis_size(axis))])


def place_kernel(columns, lines, where_ref, *refs):
    sources, target = refs[:lines], refs[lines]
    plane, column = where_ref[0], where_ref[1]
    for m, source in enumerate(sources):
        for k in range(columns):
            target[(plane ^ m) * columns + (column ^ k)] = source[k]


def quick_gather(shard):
    planes, columns = lax.axis_size("dp"), lax.axis_size("fsdp")
    rows, width = shard.shape
    if not quick(rows):
        return gather(shard)
    column = jnp.stack([shard] + [swap(shard, "fsdp", k) for k in range(1, columns)])
    even = [column] + [swap(column, "dp", m) for m in range(2, planes, 2)]
    odd = [swap(part, "dp", 1) for part in even]
    sources = [part for pair in zip(even, odd) for part in pair]
    where = jnp.stack([lax.axis_index("dp"), lax.axis_index("fsdp")]).astype(jnp.int32)
    whole = pl.pallas_call(
        functools.partial(place_kernel, columns, len(sources)),
        grid_spec=pltpu.PrefetchScalarGridSpec(
            num_scalar_prefetch=1,
            grid=(1,),
            in_specs=[pl.BlockSpec((columns, rows, width), lambda i, *_: (0, 0, 0))] * len(sources),
            out_specs=pl.BlockSpec((planes * columns, rows, width), lambda i, *_: (0, 0, 0)),
        ),
        out_shape=jax.ShapeDtypeStruct((planes * columns, rows, width), shard.dtype),
        compiler_params=pltpu.CompilerParams(vmem_limit_bytes=24 * 2**20),
        name="place",
    )(where, *sources)
    return whole.reshape(planes * columns * rows, width)


def tree_sum(parts):
    parts = [part.astype(F32) for part in parts]
    while len(parts) > 1:
        parts = [a + b for a, b in zip(parts[::2], parts[1::2])]
    return parts[0]


def quick(rows):
    return lax.axis_size("dp") % 2 == 0 and rows % 8 == 0


def pick(values, index):
    return lax.dynamic_index_in_dim(values, index, 0, keepdims=False)


def over_planes(partial):
    return lax.psum_scatter(partial, "dp", scatter_dimension=0, tiled=True)


def over_columns(partial):
    return lax.psum_scatter(partial, "fsdp", scatter_dimension=0, tiled=True)


def join_cores(keep, send):
    other = swap(send, "dp", 1)
    return [tree_sum([keep[m], other[m]]).astype(keep.dtype) for m in range(keep.shape[0])]


def join_chips(parts):
    return tree_sum(parts[:1] + [swap(part, "dp", 2 * m) for m, part in enumerate(parts) if m]).astype(parts[0].dtype)


def blocks_for_columns(partial):
    columns = lax.axis_size("fsdp")
    blocks = partial.reshape(columns, partial.shape[0] // columns, partial.shape[1])
    return [pick(blocks, lax.axis_index("fsdp") ^ k) for k in range(columns)]


def swap_blocks(blocks):
    return blocks[:1] + [swap(block, "fsdp", k) for k, block in enumerate(blocks) if k]


def small_call(kernel, shapes, name, room=6, **options):
    params = pltpu.CompilerParams(vmem_limit_bytes=room * 2**20)
    return pl.pallas_call(kernel, out_shape=shapes, compiler_params=params, name=name, **options)


def fetching_call(kernel, shape, name, arrays, fetched, scratch=()):
    held = [pltpu.VMEM(array.shape, array.dtype) for array in arrays[:fetched]]
    return small_call(
        kernel,
        shape,
        name,
        room=60,
        in_specs=[pl.BlockSpec(memory_space=pltpu.MemorySpace.HBM)] * len(arrays),
        scratch_shapes=held + list(scratch) + [pltpu.SemaphoreType.DMA((fetched,))],
    )(*arrays)


def fetch(sources, targets, sem):
    copies = [pltpu.make_async_copy(s, t, sem.at[k]) for k, (s, t) in enumerate(zip(sources, targets))]
    for copy in copies:
        copy.start()
    return copies


def pack_far_kernel(merge_hbm, inner_hbm, outer_hbm, after_ref, far_ref, merge_ref, inner_ref, outer_ref, sem):
    for copy in fetch((merge_hbm, inner_hbm, outer_hbm), (merge_ref, inner_ref, outer_ref), sem):
        copy.wait()
    own, width = merge_ref.shape
    parts = inner_ref.shape[1] // width
    far_ref[:, :width] = merge_ref[...]
    for j in range(parts):
        for d in range(width // own):
            first, source = (1 + j) * width + d * own, (d * parts + j) * own
            far_ref[:, first : first + own] = inner_ref[:, source : source + own]
        first = (1 + parts + j) * width
        far_ref[:, first : first + width] = outer_ref[j * own : (j + 1) * own, :]


def pack_near_kernel(vectors, *refs):
    sources, near_ref, held = refs[: 3 + vectors], refs[3 + vectors], refs[4 + vectors : 7 + 2 * vectors]
    rows_ref, sem = refs[-2:]
    for copy in fetch(sources, held, sem):
        copy.wait()
    lines = held[3:]
    own, width = held[0].shape
    for g in range(width // GROUP):
        for k, source in enumerate(held[:3]):
            first = (3 * g + k) * GROUP
            near_ref[:, first : first + GROUP] = source[:, g * GROUP : (g + 1) * GROUP]
    rows_ref[...] = jnp.zeros_like(rows_ref)
    row = 0
    for line in lines:
        values = line[...].astype(F32)
        for j in range(line.shape[0] // own):
            rows_ref[row : row + 1, :own] = values[j * own : (j + 1) * own].reshape(1, own)
            row += 1
    near_ref[:, 3 * width :] = rows_ref[...].T[:own].astype(BF16)


def unpack_kernel(far_ref, merge_ref, inner_ref, outer_ref):
    own, width = merge_ref.shape
    parts = inner_ref.shape[1] // width
    merge_ref[...] = far_ref[:, :width].astype(F32)
    for j in range(parts):
        block = far_ref[:, (1 + j) * width : (2 + j) * width].astype(F32)
        for d in range(width // own):
            target = (d * parts + j) * own
            inner_ref[:, target : target + own] = block[:, d * own : (d + 1) * own]
        outer_ref[j * own : (j + 1) * own, :] = far_ref[:, (1 + parts + j) * width : (2 + parts + j) * width].astype(F32)


def finish_kernel(*refs):
    blocks, (query_ref, key_ref, value_ref, vectors_ref) = refs[:-4], refs[-4:]
    total = tree_sum([block[...] for block in blocks])
    width = query_ref.shape[1]
    for g in range(width // GROUP):
        for k, target in enumerate((query_ref, key_ref, value_ref)):
            first = (3 * g + k) * GROUP
            target[:, g * GROUP : (g + 1) * GROUP] = total[:, first : first + GROUP]
    vectors_ref[...] = total[:, 3 * width :].T


def pack_near(query, key, value, vectors):
    own, width = query.shape
    if quick(own):
        shape = jax.ShapeDtypeStruct((own, 3 * width + VEC), query.dtype)
        kernel = functools.partial(pack_near_kernel, len(vectors))
        arrays = (query, key, value, *vectors)
        return fetching_call(kernel, shape, "pack_near", arrays, len(arrays), [pltpu.VMEM((VEC, VEC), F32)])
    columns = jnp.concatenate([vector.reshape(-1, own) for vector in vectors]).T
    columns = jnp.pad(columns, ((0, 0), (0, VEC - columns.shape[1])))
    groups = range(0, width, GROUP)
    triples = [mat[:, first : first + GROUP] for first in groups for mat in (query, key, value)]
    return jnp.concatenate(triples + [columns], axis=1)


def pack_far(merge, inner, outer, after):
    own, width = merge.shape
    parts = inner.shape[1] // width
    if quick(own):
        shape = jax.ShapeDtypeStruct((own, (1 + 2 * parts) * width), merge.dtype)
        return fetching_call(pack_far_kernel, shape, "pack_far", (merge, inner, outer, after), 3)
    inner = inner.reshape(own, width // own, parts, own).transpose(0, 2, 1, 3).reshape(own, parts * width)
    outer = outer.reshape(parts, own, width).transpose(1, 0, 2).reshape(own, parts * width)
    return jnp.concatenate([merge, inner, outer], axis=1)


def unpack_far(far, parts):
    own, width = far.shape[0], far.shape[1] // (1 + 2 * parts)
    if quick(own):
        shapes = [(own, width), (own, parts * width), (parts * own, width)]
        shapes = [jax.ShapeDtypeStruct(shape, F32) for shape in shapes]
        return small_call(unpack_kernel, shapes, "unpack_far")(far)
    far = far.astype(F32)
    inner = far[:, width : (1 + parts) * width].reshape(own, parts, width // own, own)
    outer = far[:, (1 + parts) * width :].reshape(own, parts, width)
    return (
        far[:, :width],
        inner.transpose(0, 2, 1, 3).reshape(own, parts * width),
        outer.transpose(1, 0, 2).reshape(parts * own, width),
    )


def finish_near(blocks):
    own = blocks[0].shape[0]
    width = (blocks[0].shape[1] - VEC) // 3
    if quick(own):
        shapes = [jax.ShapeDtypeStruct(shape, F32) for shape in [(own, width)] * 3 + [(VEC, own)]]
        return small_call(finish_kernel, shapes, "finish_near")(*blocks)
    total = tree_sum(blocks)
    triple = total[:, : 3 * width].reshape(own, width // GROUP, 3, GROUP)
    return [triple[:, :, k].reshape(own, width) for k in range(3)] + [total[:, 3 * width :].T]


def per_device(
    layer_input, cotangent, doc_lengths, pad_tail,
    query_weight, query_bias, key_weight, value_weight, value_bias,
    merge_weight, merge_bias, first_gain, first_shift,
    inner_weight, inner_bias, outer_weight, outer_bias, second_gain, second_shift,
):
    seqs, _, width = layer_input.shape
    own = query_weight.shape[0]
    devices = width // own
    parts = inner_weight.shape[1] // width
    groups = width // GROUP

    vectors = (query_bias, value_bias, merge_bias, first_gain, first_shift, outer_bias, second_gain, second_shift, inner_bias)
    near_own = pack_near(query_weight, key_weight, value_weight, vectors)
    near = quick_gather(near_own)
    far = gather(pack_far(merge_weight, inner_weight, outer_weight, near_own))
    segment, low, count = segments(doc_lengths, pad_tail)
    segc = jnp.broadcast_to(segment[:, :, None], (seqs, LEN, 128))
    segr = jnp.broadcast_to(segment[:, None, :], (seqs, 8, LEN))

    vec_rows = near[:, 3 * width :].T.astype(F32)
    bias = jnp.stack([vec_rows[0], jnp.zeros((width,), F32), vec_rows[1]])
    bias = bias.reshape(3, groups, GROUP).transpose(1, 0, 2).reshape(1, 3 * width)
    bias = jnp.broadcast_to(bias, (8, 3 * width))
    vec = vec_rows[2:18]

    qkv, mixed, lse = attention_forward(layer_input, near, bias, segc, segr, low, count)
    tokens = seqs * LEN
    flat_mixed = mixed.reshape(tokens, width)
    output, normed, inverse, upper, slope, outer_partial, sums, stats = upper_half(
        flat_mixed, layer_input.reshape(tokens, width), cotangent.reshape(tokens, width), far, vec, pad_tail
    )
    outer_grad = over_planes(outer_partial)
    residual, mixed_grad, inner_partial, sums = lower_half(flat_mixed, normed, inverse, upper, slope, far, vec, sums)
    inner_grad = over_planes(inner_partial)
    chips = lax.axis_size("dp") // 2 if quick(own) else 0
    dqkv, keep, send = attention_backward(
        qkv, mixed, mixed_grad.reshape(mixed.shape), layer_input, lse, segc, segr, sums, stats, low, count, pad_tail, chips
    )
    far_planes = jnp.concatenate([inner_grad, outer_grad], axis=1)
    if chips:
        keep, far_planes = lax.optimization_barrier((keep, far_planes))
        far_grad = over_columns(far_planes)
        parts_own = join_cores(keep, send)
        parts_own, residual = lax.optimization_barrier((parts_own, residual))
        near_planes = join_chips(parts_own)
    else:
        far_grad = over_columns(far_planes)
        near_planes = over_planes(keep[0])
    input_gradient = residual + dot(dqkv.reshape(tokens, 3 * width), near[:, : 3 * width], 1, 1)
    if chips:
        near_planes, input_gradient, far_grad = lax.optimization_barrier((near_planes, input_gradient, far_grad))
        near_blocks = swap_blocks(blocks_for_columns(near_planes))
    else:
        near_blocks = [over_columns(near_planes)]
    query_grad, key_grad, value_grad, mine = finish_near(near_blocks)
    merge_grad, inner_grad, outer_grad = unpack_far(far_grad, parts)
    inner_bias_gradient = mine[8 : 8 + parts].reshape(parts * own)
    all_tokens = tokens * devices
    if quick(own):
        totals = mine[16 : 20 + DIGITS, 0]
        valid_total = sum(totals[4 + digit] * 8.0**digit for digit in range(DIGITS))
    else:
        valid_own = jnp.sum(LEN - pad_tail).astype(F32)
        totals = lax.psum(jnp.concatenate([jnp.sum(stats[:4], axis=1), valid_own[None]]), AXES)
        valid_total = totals[4]
    share = jnp.reshape(valid_total / all_tokens, (1,))
    layer_stats = jnp.concatenate([share, jnp.sqrt(totals[:4] / (valid_total * width))])
    return (
        output.reshape(layer_input.shape),
        input_gradient.reshape(layer_input.shape),
        query_grad,
        mine[6],
        key_grad,
        value_grad,
        mine[7],
        merge_grad,
        mine[5],
        mine[3],
        mine[4],
        inner_grad,
        inner_bias_gradient,
        outer_grad,
        mine[2],
        mine[0],
        mine[1],
        layer_stats,
    )


def solution(mesh):
    matrix, vector, cube = P(AXES, None), P(AXES), P(AXES, None, None)
    in_specs = (
        cube, cube, matrix, vector,
        matrix, vector, matrix, matrix, vector,
        matrix, vector, vector, vector,
        matrix, vector, matrix, vector, vector, vector,
    )
    out_specs = (
        cube, cube,
        matrix, vector, matrix, matrix, vector,
        matrix, vector, vector, vector,
        matrix, vector, matrix, vector, vector, vector,
        P(),
    )
    return jax.shard_map(per_device, mesh=mesh, in_specs=in_specs, out_specs=out_specs, check_vma=False)
```

```python
import functools

import jax
import jax.numpy as jnp
from jax import lax
from jax.experimental import pallas as pl
from jax.experimental.pallas import tpu as pltpu
from jax.sharding import PartitionSpec as P

HEAD_DIM = 64
LEN = 1024
DOCS = 8
EPSILON = 1e-12
NEGATIVE = -1e30
ROOT_HALF = 0.7071067811865476
INV_ROOT_TWO_PI = 0.3989422804014327
AXES = ("dp", "fsdp")
F32 = jnp.float32
BF16 = jnp.bfloat16

GROUP = 256
HEADS_IN = GROUP // HEAD_DIM
PAIR = 128
TRIPLE = 3 * GROUP
QB = 256
CHUNK = 256
VEC = 128
DIGITS = 8


def dot(left, right, left_dim=1, right_dim=0):
    return lax.dot_general(
        left, right, (((left_dim,), (right_dim,)), ((), ())), preferred_element_type=F32
    )


def head_masks(columns):
    lane = lax.broadcasted_iota(jnp.int32, (1, columns), 1) // HEAD_DIM
    return [lane == h for h in range(columns // HEAD_DIM)]


def cost(flops, moved):
    return pl.CostEstimate(flops=int(flops), bytes_accessed=int(moved), transcendentals=0)


def segments(doc_lengths, pad_tail):
    ends = jnp.cumsum(doc_lengths, axis=1)
    limit = (LEN - pad_tail)[:, None]
    places = jnp.arange(LEN, dtype=jnp.int32)
    segment = jnp.sum((places[None, :, None] >= ends[:, None, :]).astype(jnp.int32), axis=2)
    segment = jnp.where(places[None] < limit, segment, DOCS)
    borders = jnp.concatenate(
        [jnp.zeros_like(limit), jnp.minimum(ends, limit), limit, jnp.full_like(limit, LEN)], axis=1
    )[:, None, :]
    first = (jnp.arange(LEN // QB, dtype=jnp.int32) * QB)[None, :, None]
    low = jnp.max(jnp.where(borders <= first, borders, 0), axis=2)
    high = jnp.min(jnp.where(borders > first + QB - 1, borders, LEN), axis=2)
    low = (low // 128) * 128
    count = (high - low + CHUNK - 1) // CHUNK
    low = jnp.minimum(low, LEN - CHUNK * count)
    return segment, low.astype(jnp.int32), count.astype(jnp.int32)


def forward_kernel(
    low_ref, count_ref, rows_ref, w_ref, bias_ref, segr_ref,
    qkv_ref, mixed_ref, lse_ref, keyt_ref, segc_ref,
):
    s = pl.program_id(0)
    qkv_ref[...] = (dot(rows_ref[...], w_ref[...]) + bias_ref[0:1, :]).astype(BF16)
    keyt_ref[...] = qkv_ref[:, GROUP : 2 * GROUP].T

    @pl.when(pl.program_id(1) == 0)
    def _():
        segc_ref[...] = jnp.broadcast_to(segr_ref[...], (128, LEN)).T

    masks = head_masks(GROUP)

    def block(i, carry):
        start = pl.multiple_of(i * QB, QB)
        queries = qkv_ref[pl.ds(start, QB), :GROUP] * BF16(HEAD_DIM**-0.5)
        zero = jnp.zeros_like(queries)
        own = segc_ref[pl.ds(start, QB), :][:, :1]
        low = pl.multiple_of(low_ref[s, i], 128)
        count = count_ref[s, i]
        for c in range(1, LEN // CHUNK + 1):

            @pl.when(count == c)
            def _():
                span = pl.ds(low, CHUNK * c)
                keys = keyt_ref[:, span]
                values = qkv_ref[span, 2 * GROUP :]
                allowed = own == segr_ref[0:1, span]
                lane = lax.broadcasted_iota(jnp.int32, (QB, 128), 1)
                mixed = None
                for h in range(HEADS_IN):
                    scores = dot(jnp.where(masks[h], queries, zero), keys)
                    scores = jnp.where(allowed, scores, NEGATIVE)
                    top = jnp.max(scores, axis=1, keepdims=True)
                    expo = jnp.exp(scores - top)
                    total = jnp.sum(expo, axis=1, keepdims=True)
                    part = dot(expo.astype(BF16), values) * (1.0 / total)
                    logsum = top + jnp.log(total)
                    if h == 0:
                        mixed, sums = part, jnp.broadcast_to(logsum, (QB, 128))
                    else:
                        mixed, sums = jnp.where(masks[h], part, mixed), jnp.where(lane == h, logsum, sums)
                mixed_ref[pl.ds(start, QB), :] = mixed.astype(BF16)
                lse_ref[:, pl.ds(start, QB)] = sums.T[:8]

        return carry

    lax.fori_loop(0, LEN // QB, block, 0)


def attention_forward(rows, w, bias, segment, low, count):
    seqs, _, width = rows.shape
    groups = width // GROUP
    return pl.pallas_call(
        forward_kernel,
        grid_spec=pltpu.PrefetchScalarGridSpec(
            num_scalar_prefetch=2,
            grid=(seqs, groups),
            in_specs=[
                pl.BlockSpec((None, LEN, width), lambda s, g, *_: (s, 0, 0)),
                pl.BlockSpec((width, TRIPLE), lambda s, g, *_: (0, g)),
                pl.BlockSpec((1, TRIPLE), lambda s, g, *_: (0, g)),
                pl.BlockSpec((None, 1, LEN), lambda s, g, *_: (s, 0, 0)),
            ],
            out_specs=[
                pl.BlockSpec((None, LEN, TRIPLE), lambda s, g, *_: (s, 0, g)),
                pl.BlockSpec((None, LEN, GROUP), lambda s, g, *_: (s, 0, g)),
                pl.BlockSpec((None, None, 8, LEN), lambda s, g, *_: (s, g, 0, 0)),
            ],
            scratch_shapes=[pltpu.VMEM((GROUP, LEN), BF16), pltpu.VMEM((LEN, 128), jnp.int32)],
        ),
        out_shape=[
            jax.ShapeDtypeStruct((seqs, LEN, 3 * width), BF16),
            jax.ShapeDtypeStruct((seqs, LEN, width), BF16),
            jax.ShapeDtypeStruct((seqs, groups, 8, LEN), F32),
        ],
        compiler_params=pltpu.CompilerParams(vmem_limit_bytes=60 * 2**20),
        cost_estimate=cost(2 * seqs * LEN * width * (3 * width + 16 * LEN), seqs * LEN * width * 10),
        name="attention_forward",
    )(low, count, rows, w, bias, segment)


def backward_kernel(
    chips,
    low_ref, count_ref, pad_ref, plane_ref, qkv_ref, mixed_ref, grad_ref, rows_ref, lse_ref, segr_ref, vec_ref, stats_ref,
    dqkv_ref, keep_ref, send_ref,
    q_ref, qt_ref, gt_ref, kt_ref, dqt_ref, acc_ref, delta_ref, sums_ref, stage_ref, columns_ref, rowst_ref, segc_ref, sem,
):
    s, g = pl.program_id(0), pl.program_id(1)
    masks = head_masks(PAIR)

    @pl.when(g == 0)
    def _():
        rowst_ref[...] = rows_ref[...].T
        segc_ref[...] = jnp.broadcast_to(segr_ref[...], (128, LEN)).T

    @pl.when((g == 0) & (s == 0))
    def _():
        sums_ref[...] = jnp.zeros_like(sums_ref)
        sums_ref[:16, :] = vec_ref[...]

    grad = grad_ref[...]
    prod = grad.astype(F32) * mixed_ref[...].astype(F32)
    coarse = prod.astype(BF16)
    fine = (prod - coarse.astype(F32)).astype(BF16)
    pick = lax.broadcasted_iota(jnp.int32, (8, GROUP), 1) // HEAD_DIM
    pick = (pick == lax.broadcasted_iota(jnp.int32, (8, GROUP), 0)).astype(F32).astype(BF16)
    delta_ref[...] = dot(pick, coarse, 1, 1) + dot(pick, fine, 1, 1)
    queries = qkv_ref[:, :GROUP] * BF16(HEAD_DIM**-0.5)
    q_ref[...] = queries
    qt_ref[...] = queries.T
    gt_ref[...] = grad.T
    kt_ref[...] = qkv_ref[:, GROUP : 2 * GROUP].T
    dqt_ref[...] = jnp.zeros_like(dqt_ref)

    def block(i, carry):
        start = pl.multiple_of(i * QB, QB)
        mine = pl.ds(start, QB)
        keys = qkv_ref[mine, GROUP : 2 * GROUP]
        values = qkv_ref[mine, 2 * GROUP :]
        zero = jnp.zeros((QB, PAIR), BF16)
        own = segc_ref[mine, :][:, :1]
        low = pl.multiple_of(low_ref[s, i], 128)
        count = count_ref[s, i]
        for c in range(1, LEN // CHUNK + 1):

            @pl.when(count == c)
            def _():
                span = pl.ds(low, CHUNK * c)
                allowed = own == segr_ref[0:1, span]
                for h in range(HEADS_IN):
                    mask, lanes = masks[h % 2], slice(h // 2 * PAIR, (h // 2 + 1) * PAIR)
                    scores = dot(jnp.where(mask, keys[:, lanes], zero), qt_ref[lanes, span])
                    probs = jnp.exp(jnp.where(allowed, scores, NEGATIVE) - lse_ref[h : h + 1, span])
                    pgrad = dot(jnp.where(mask, values[:, lanes], zero), gt_ref[lanes, span])
                    low_score = (probs * (pgrad - delta_ref[h : h + 1, span])).astype(BF16)
                    v_part = dot(probs.astype(BF16), grad_ref[span, lanes])
                    k_part = dot(low_score, q_ref[span, lanes])
                    head = slice(h * HEAD_DIM, (h + 1) * HEAD_DIM)
                    dqt_ref[head, span] += dot(kt_ref[head, mine], low_score)
                    if h % 2 == 0:
                        dkey, dvalue = k_part, v_part
                    else:
                        first = h // 2 * PAIR
                        dkey, dvalue = jnp.where(mask, k_part, dkey), jnp.where(mask, v_part, dvalue)
                        dqkv_ref[mine, GROUP + first : GROUP + first + PAIR] = dkey.astype(BF16)
                        dqkv_ref[mine, 2 * GROUP + first : 2 * GROUP + first + PAIR] = dvalue.astype(BF16)

        return carry

    lax.fori_loop(0, LEN // QB, block, 0)
    dqkv_ref[:, :GROUP] = (dqt_ref[...] * HEAD_DIM**-0.5).astype(BF16).T
    dqkv = dqkv_ref[...]
    dw = dot(rowst_ref[...], dqkv)
    sums = jnp.sum(dqkv.astype(F32), axis=0, keepdims=True)
    lanes = pl.ds(pl.multiple_of(g * GROUP, GROUP), GROUP)
    sums_ref[6:7, lanes] += sums[:, :GROUP]
    sums_ref[7:8, lanes] += sums[:, 2 * GROUP :]

    @pl.when(s == 0)
    def _():
        acc_ref[g] = dw

    @pl.when(s > 0)
    def _():
        acc_ref[g] += dw

    last_s, last_g = pl.num_programs(0) - 1, pl.num_programs(1) - 1

    def copies(source, lanes, first_sem):
        if chips == 0:
            return [pltpu.make_async_copy(source, keep_ref.at[0, :, lanes], sem.at[first_sem])]
        rows = source.shape[0] // (2 * chips)
        core, chip = plane_ref[0] & 1, lax.shift_right_logical(plane_ref[0], 1)
        moves = []
        for m in range(chips):
            for side, target in enumerate((keep_ref, send_ref)):
                owner = 2 * (chip ^ m) + (core ^ side)
                piece = source.at[pl.ds(pl.multiple_of(owner * rows, rows), rows), :]
                moves.append(pltpu.make_async_copy(piece, target.at[m, :, lanes], sem.at[first_sem + 2 * m + side]))
        return moves

    def group_copies(group):
        return copies(stage_ref, pl.ds(pl.multiple_of(group * TRIPLE, TRIPLE), TRIPLE), 0)

    @pl.when(s == last_s)
    def _():
        @pl.when(g > 0)
        def _():
            for move in group_copies(g - 1):
                move.wait()

        stage_ref[...] = acc_ref[g].astype(BF16)
        for move in group_copies(g):
            move.start()

    @pl.when((g == last_g) & (s == last_s))
    def _():
        for row in range(4):
            value = jnp.sum(stats_ref[row : row + 1, :], axis=1, keepdims=True)
            sums_ref[16 + row : 17 + row, :] = jnp.broadcast_to(value, (1, sums_ref.shape[1]))
        tokens = pl.num_programs(0) * LEN
        for seq in range(pad_ref.shape[0]):
            tokens -= pad_ref[seq]
        for row in range(DIGITS):
            digit = (lax.shift_right_logical(tokens, 3 * row) & 7).astype(F32)
            sums_ref[20 + row : 21 + row, :] = jnp.full((1, sums_ref.shape[1]), digit)
        columns_ref[...] = sums_ref[...].T.astype(BF16)
        width = sums_ref.shape[1]
        moves = copies(columns_ref, slice(3 * width, 3 * width + VEC), max(1, 2 * chips))
        for move in moves:
            move.start()
        for move in group_copies(g) + moves:
            move.wait()


def attention_backward(qkv, mixed, grad, rows, lse, segment, vec, stats, low, count, pad, chips):
    seqs, _, width = mixed.shape
    groups = width // GROUP
    plane = lax.axis_index("dp").astype(jnp.int32).reshape(1)
    packed = (max(1, chips), width // max(1, 2 * chips), 3 * width + VEC)
    return pl.pallas_call(
        functools.partial(backward_kernel, chips),
        grid_spec=pltpu.PrefetchScalarGridSpec(
            num_scalar_prefetch=4,
            grid=(seqs, groups),
            in_specs=[
                pl.BlockSpec((None, LEN, TRIPLE), lambda s, g, *_: (s, 0, g)),
                pl.BlockSpec((None, LEN, GROUP), lambda s, g, *_: (s, 0, g)),
                pl.BlockSpec((None, LEN, GROUP), lambda s, g, *_: (s, 0, g)),
                pl.BlockSpec((None, LEN, width), lambda s, g, *_: (s, 0, 0)),
                pl.BlockSpec((None, None, 8, LEN), lambda s, g, *_: (s, g, 0, 0)),
                pl.BlockSpec((None, 1, LEN), lambda s, g, *_: (s, 0, 0)),
                pl.BlockSpec((16, width), lambda s, g, *_: (0, 0)),
                pl.BlockSpec((8, width), lambda s, g, *_: (0, 0)),
            ],
            out_specs=[
                pl.BlockSpec((None, LEN, TRIPLE), lambda s, g, *_: (s, 0, g)),
                pl.BlockSpec(memory_space=pl.ANY),
                pl.BlockSpec(memory_space=pl.ANY),
            ],
            scratch_shapes=[
                pltpu.VMEM((LEN, GROUP), BF16),
                pltpu.VMEM((GROUP, LEN), BF16),
                pltpu.VMEM((GROUP, LEN), BF16),
                pltpu.VMEM((GROUP, LEN), BF16),
                pltpu.VMEM((GROUP, LEN), F32),
                pltpu.VMEM((groups, width, TRIPLE), F32),
                pltpu.VMEM((8, LEN), F32),
                pltpu.VMEM((VEC, width), F32),
                pltpu.VMEM((width, TRIPLE), BF16),
                pltpu.VMEM((width, VEC), BF16),
                pltpu.VMEM((width, LEN), BF16),
                pltpu.VMEM((LEN, 128), jnp.int32),
                pltpu.SemaphoreType.DMA((2 * max(1, 2 * chips),)),
            ],
        ),
        out_shape=[
            jax.ShapeDtypeStruct((seqs, LEN, 3 * width), BF16),
            jax.ShapeDtypeStruct(packed, BF16),
            jax.ShapeDtypeStruct(packed if chips else (8, 128), BF16),
        ],
        compiler_params=pltpu.CompilerParams(vmem_limit_bytes=60 * 2**20),
        cost_estimate=cost(2 * seqs * LEN * width * (3 * width + 32 * LEN), seqs * LEN * width * 20),
        name="attention_backward",
    )(low, count, pad, plane, qkv, mixed, grad, rows, lse, segment, vec, stats)


def mean(values):
    return jnp.mean(values, axis=1, keepdims=True)


def normed_of(values):
    centred = values - mean(values)
    inverse = lax.rsqrt(mean(centred * centred) + EPSILON)
    return centred * inverse, inverse


def norm_backward(scaled, normed, inverse):
    return inverse * (scaled - mean(scaled) - normed * mean(scaled * normed))


def add_rows(sums_ref, row, values):
    sums_ref[row] += jnp.sum(values.reshape(-1, 8, values.shape[1]), axis=0)


class Blocks:
    def __init__(self, wide_ref, held_ref, sem, first_step):
        self.wide_ref, self.held_ref, self.sem, self.first_step = wide_ref, held_ref, sem, first_step

    def copy(self, k):
        width = self.held_ref.shape[2]
        columns = pl.ds(pl.multiple_of(k * width, width), width)
        return pltpu.make_async_copy(self.wide_ref.at[:, columns], self.held_ref.at[k], self.sem.at[k])

    def start(self, order):
        @pl.when(self.first_step)
        def _():
            for k in order:
                self.copy(k).start()

    def wait(self, k):
        @pl.when(self.first_step)
        def _():
            self.copy(k).wait()


def out_copy(stage_ref, dw_ref, sem, k):
    width = stage_ref.shape[1]
    columns = pl.ds(pl.multiple_of(k * width, width), width)
    slot = lax.rem(k, 2)
    return pltpu.make_async_copy(stage_ref.at[slot], dw_ref.at[:, columns], sem.at[slot])


def send_blocks(gradient, first, amount, stage_ref, dw_ref, sem):
    def step(j, carry):
        k = first + j

        @pl.when(j >= 2)
        def _():
            out_copy(stage_ref, dw_ref, sem, k - 2).wait()

        stage_ref[lax.rem(k, 2)] = gradient(j)
        out_copy(stage_ref, dw_ref, sem, k).start()
        return carry

    lax.fori_loop(0, amount, step, 0)


def upper_kernel(
    parts, width, tokens,
    pad_ref, mixed_ref, rows_ref, cot_ref, w_ref, vec_ref,
    out_ref, normed_ref, inverse_ref, upper_ref, slope_ref, dw_ref, sums_ref, stats_ref,
    held_ref, hidden_ref, low_ref, uppert_ref, stage_ref, part_ref, w_sem, sem,
):
    i = pl.program_id(0)
    last = i == pl.num_programs(0) - 1
    per_seq = LEN // tokens
    weights = Blocks(w_ref, held_ref, w_sem, i == 0)
    weights.start([0] + [k + j for j in range(parts) for k in (1, 1 + parts)])

    @pl.when(i == 0)
    def _():
        part_ref[...] = jnp.zeros_like(part_ref)

    def vector(row):
        return vec_ref[row + 2 : row + 3, :]

    def valid_of():
        place = (i % per_seq) * tokens + lax.broadcasted_iota(jnp.int32, (tokens, 1), 0)
        return (place < LEN - pad_ref[i // per_seq]).astype(F32)

    mine = pl.ds(pl.multiple_of(i * tokens, tokens), tokens)
    weights.wait(0)
    upper_ref[...] = dot(mixed_ref[...], held_ref[0])

    valid = valid_of()
    rows = rows_ref[...].astype(F32)
    branch = upper_ref[...] + vector(0)
    add_rows(part_ref, 3, valid * rows * rows)
    add_rows(part_ref, 4, valid * branch * branch)
    normed, inverse = normed_of(rows + branch)
    normed_ref[...] = normed
    inverse_ref[...] = jnp.broadcast_to(inverse, (tokens, 128))
    first = normed * vector(1) + vector(2)
    low_ref[...] = first.astype(BF16)
    upper_ref[...] = first + vector(3)

    def feed(j, carry):
        weights.wait(1 + j)
        weights.wait(1 + parts + j)
        inner = dot(low_ref[...], held_ref[1 + j]) + vec_ref[pl.ds(8 + j, 1), :]
        half = 0.5 * (1.0 + lax.erf(inner * ROOT_HALF))
        hidden = (inner * half).astype(BF16)
        hidden_ref[j, mine, :] = hidden
        slope = half + inner * jnp.exp(-0.5 * inner * inner) * INV_ROOT_TWO_PI
        slope_ref[:, pl.ds(pl.multiple_of(j * width, width), width)] = slope.astype(BF16)
        upper_ref[...] += dot(hidden, held_ref[1 + parts + j])
        return carry

    lax.fori_loop(0, parts, feed, 0)

    valid = valid_of()
    total = upper_ref[...]
    second = total - (normed_ref[...] * vector(1) + vector(2))
    add_rows(part_ref, 5, valid * second * second)
    normed, inverse = normed_of(total)
    result = normed * vector(4) + vector(5)
    add_rows(part_ref, 6, valid * result * result)
    out_ref[...] = result.astype(BF16)
    upstream = cot_ref[...].astype(F32) * valid
    add_rows(part_ref, 0, upstream * normed)
    add_rows(part_ref, 1, upstream)
    upper = norm_backward(upstream * vector(4), normed, inverse)
    upper_ref[...] = upper
    upper_low = upper.astype(BF16)
    add_rows(part_ref, 2, upper_low.astype(F32))
    uppert_ref[:, mine] = upper_low.T

    @pl.when(last)
    def _():
        sums_ref[...] = jnp.zeros_like(sums_ref)
        for row in range(3):
            sums_ref[row : row + 1, :] = jnp.sum(part_ref[row], axis=0, keepdims=True)
        for row in range(4):
            stats_ref[row : row + 1, :] = jnp.sum(part_ref[3 + row], axis=0, keepdims=True)
        stats_ref[4:, :] = jnp.zeros_like(stats_ref[4:, :])
        send_blocks(
            lambda j: dot(uppert_ref[...], hidden_ref[j]).astype(BF16).T, 0, parts, stage_ref, dw_ref, sem
        )
        for k in (parts - 2, parts - 1):
            out_copy(stage_ref, dw_ref, sem, k).wait()


def lower_kernel(
    parts, width, tokens,
    mixed_ref, normed_ref, inverse_ref, upper_ref, slope_ref, w_ref, vec_ref, sums_in_ref,
    res_ref, mgrad_ref, dw_ref, sums_ref,
    held_ref, low_ref, first_ref, acc_ref, stage_ref, part_ref, w_sem, sem,
):
    i = pl.program_id(0)
    last = i == pl.num_programs(0) - 1
    weights = Blocks(w_ref, held_ref, w_sem, i == 0)
    weights.start([k + j for j in range(parts) for k in (1 + parts, 1)] + [0])

    @pl.when(i == 0)
    def _():
        acc_ref[...] = jnp.zeros_like(acc_ref)
        part_ref[...] = jnp.zeros_like(part_ref)

    def vector(row):
        return vec_ref[row + 2 : row + 3, :]

    upper = upper_ref[...]
    res_ref[...] = upper
    low_ref[...] = upper.astype(BF16)
    first_ref[...] = (normed_ref[...] * vector(1) + vector(2)).astype(BF16)

    first_t = first_ref[...].T

    def back(j, carry):
        weights.wait(1 + parts + j)
        weights.wait(1 + j)
        slope = slope_ref[:, pl.ds(pl.multiple_of(j * width, width), width)].astype(F32)
        inner_low = (dot(low_ref[...], held_ref[1 + parts + j], 1, 1) * slope).astype(BF16)
        add_rows(part_ref, 3 + j, inner_low.astype(F32))
        acc_ref[1 + j] += dot(first_t, inner_low)
        res_ref[...] += dot(inner_low, held_ref[1 + j], 1, 1)

        @pl.when(last)
        def _():
            @pl.when(j >= 2)
            def _():
                out_copy(stage_ref, dw_ref, sem, j - 1).wait()

            stage_ref[lax.rem(1 + j, 2)] = acc_ref[1 + j].astype(BF16)
            out_copy(stage_ref, dw_ref, sem, 1 + j).start()

        return carry

    lax.fori_loop(0, parts, back, 0)

    first_grad = res_ref[...]
    normed = normed_ref[...]
    add_rows(part_ref, 0, first_grad * normed)
    add_rows(part_ref, 1, first_grad)
    residual = norm_backward(first_grad * vector(1), normed, inverse_ref[:, :1])
    res_ref[...] = residual
    branch_low = residual.astype(BF16)
    add_rows(part_ref, 2, branch_low.astype(F32))
    low_ref[...] = branch_low

    weights.wait(0)
    acc_ref[0] += dot(mixed_ref[...], low_ref[...], 0, 0)
    mgrad_ref[...] = dot(low_ref[...], held_ref[0], 1, 1).astype(BF16)

    @pl.when(last)
    def _():
        sums_ref[...] = sums_in_ref[...]
        for row in range(3):
            sums_ref[3 + row : 4 + row, :] = jnp.sum(part_ref[row], axis=0, keepdims=True)
        for j in range(parts):
            sums_ref[8 + j : 9 + j, :] = jnp.sum(part_ref[3 + j], axis=0, keepdims=True)
        for k in (parts - 1, parts):
            out_copy(stage_ref, dw_ref, sem, k).wait()
        stage_ref[0] = acc_ref[0].astype(BF16)
        out_copy(stage_ref, dw_ref, sem, 0).start()
        out_copy(stage_ref, dw_ref, sem, 0).wait()


def upper_half(mixed, rows, cotangent, w, vec, pad, tokens=512):
    count, width = mixed.shape
    parts = (w.shape[1] // width - 1) // 2

    def block(columns):
        return pl.BlockSpec((tokens, columns), lambda i, *_: (i, 0))

    def fixed(*shape):
        return pl.BlockSpec(shape, lambda i, *_: (0, 0))

    anywhere = pl.BlockSpec(memory_space=pl.ANY)
    return pl.pallas_call(
        functools.partial(upper_kernel, parts, width, tokens),
        grid_spec=pltpu.PrefetchScalarGridSpec(
            num_scalar_prefetch=1,
            grid=(count // tokens,),
            in_specs=[block(width), block(width), block(width), anywhere, fixed(24, width)],
            out_specs=[
                block(width), block(width), block(128), block(width), block(parts * width), anywhere,
                fixed(16, width), fixed(8, width),
            ],
            scratch_shapes=[
                pltpu.VMEM((1 + 2 * parts, width, width), BF16),
                pltpu.VMEM((parts, count, width), BF16),
                pltpu.VMEM((tokens, width), BF16),
                pltpu.VMEM((width, count), BF16),
                pltpu.VMEM((2, width, width), BF16),
                pltpu.VMEM((8, 8, width), F32),
                pltpu.SemaphoreType.DMA((1 + 2 * parts,)),
                pltpu.SemaphoreType.DMA((2,)),
            ],
        ),
        out_shape=[
            jax.ShapeDtypeStruct((count, width), BF16),
            jax.ShapeDtypeStruct((count, width), F32),
            jax.ShapeDtypeStruct((count, 128), F32),
            jax.ShapeDtypeStruct((count, width), F32),
            jax.ShapeDtypeStruct((count, parts * width), BF16),
            jax.ShapeDtypeStruct((width, parts * width), BF16),
            jax.ShapeDtypeStruct((16, width), F32),
            jax.ShapeDtypeStruct((8, width), F32),
        ],
        compiler_params=pltpu.CompilerParams(vmem_limit_bytes=60 * 2**20),
        cost_estimate=cost(2 * count * width * width * (1 + 3 * parts), count * width * 40 + 4 * w.size),
        name="upper_half",
    )(pad, mixed, rows, cotangent, w, vec)


def lower_half(mixed, normed, inverse, upper, slope, w, vec, sums, tokens=512):
    count, width = mixed.shape
    parts = (w.shape[1] // width - 1) // 2

    def block(columns):
        return pl.BlockSpec((tokens, columns), lambda i: (i, 0))

    def fixed(*shape):
        return pl.BlockSpec(shape, lambda i: (0, 0))

    anywhere = pl.BlockSpec(memory_space=pl.ANY)
    return pl.pallas_call(
        functools.partial(lower_kernel, parts, width, tokens),
        grid=(count // tokens,),
        in_specs=[
            block(width), block(width), block(128), block(width), block(parts * width), anywhere,
            fixed(24, width), fixed(16, width),
        ],
        out_specs=[block(width), block(width), anywhere, fixed(16, width)],
        scratch_shapes=[
            pltpu.VMEM((1 + 2 * parts, width, width), BF16),
            pltpu.VMEM((tokens, width), BF16),
            pltpu.VMEM((tokens, width), BF16),
            pltpu.VMEM((1 + parts, width, width), F32),
            pltpu.VMEM((2, width, width), BF16),
            pltpu.VMEM((3 + parts, 8, width), F32),
            pltpu.SemaphoreType.DMA((1 + 2 * parts,)),
            pltpu.SemaphoreType.DMA((2,)),
        ],
        out_shape=[
            jax.ShapeDtypeStruct((count, width), F32),
            jax.ShapeDtypeStruct((count, width), BF16),
            jax.ShapeDtypeStruct((width, (1 + parts) * width), BF16),
            jax.ShapeDtypeStruct((16, width), F32),
        ],
        compiler_params=pltpu.CompilerParams(vmem_limit_bytes=60 * 2**20),
        cost_estimate=cost(2 * count * width * width * (2 + 3 * parts), count * width * 40 + 4 * w.size),
        name="lower_half",
    )(mixed, normed, inverse, upper, slope, w, vec, sums)


def gather(shard):
    return lax.all_gather(shard, AXES, axis=0, tiled=True)


def swap(values, axis, flip):
    return lax.ppermute(values, axis, [(d, d ^ flip) for d in range(lax.axis_size(axis))])


def place_kernel(columns, lines, where_ref, *refs):
    sources, target = refs[:lines], refs[lines]
    plane, column = where_ref[0], where_ref[1]
    for m, source in enumerate(sources):
        for k in range(columns):
            target[(plane ^ m) * columns + (column ^ k)] = source[k]


def quick_gather(shard):
    planes, columns = lax.axis_size("dp"), lax.axis_size("fsdp")
    rows, width = shard.shape
    if not quick(rows):
        return gather(shard)
    column = jnp.stack([shard] + [swap(shard, "fsdp", k) for k in range(1, columns)])
    even = [column] + [swap(column, "dp", m) for m in range(2, planes, 2)]
    odd = [swap(part, "dp", 1) for part in even]
    sources = [part for pair in zip(even, odd) for part in pair]
    where = jnp.stack([lax.axis_index("dp"), lax.axis_index("fsdp")]).astype(jnp.int32)
    whole = pl.pallas_call(
        functools.partial(place_kernel, columns, len(sources)),
        grid_spec=pltpu.PrefetchScalarGridSpec(
            num_scalar_prefetch=1,
            grid=(1,),
            in_specs=[pl.BlockSpec((columns, rows, width), lambda i, *_: (0, 0, 0))] * len(sources),
            out_specs=pl.BlockSpec((planes * columns, rows, width), lambda i, *_: (0, 0, 0)),
        ),
        out_shape=jax.ShapeDtypeStruct((planes * columns, rows, width), shard.dtype),
        compiler_params=pltpu.CompilerParams(vmem_limit_bytes=24 * 2**20),
        name="place",
    )(where, *sources)
    return whole.reshape(planes * columns * rows, width)


def tree_sum(parts):
    parts = [part.astype(F32) for part in parts]
    while len(parts) > 1:
        parts = [a + b for a, b in zip(parts[::2], parts[1::2])]
    return parts[0]


def quick(rows):
    return lax.axis_size("dp") % 2 == 0 and rows % 8 == 0


def pick(values, index):
    return lax.dynamic_index_in_dim(values, index, 0, keepdims=False)


def over_planes(partial):
    return lax.psum_scatter(partial, "dp", scatter_dimension=0, tiled=True)


def over_columns(partial):
    return lax.psum_scatter(partial, "fsdp", scatter_dimension=0, tiled=True)


def join_cores(keep, send):
    other = swap(send, "dp", 1)
    return [tree_sum([keep[m], other[m]]).astype(keep.dtype) for m in range(keep.shape[0])]


def join_chips(parts):
    return tree_sum(parts[:1] + [swap(part, "dp", 2 * m) for m, part in enumerate(parts) if m]).astype(parts[0].dtype)


def blocks_for_columns(partial):
    columns = lax.axis_size("fsdp")
    blocks = partial.reshape(columns, partial.shape[0] // columns, partial.shape[1])
    return [pick(blocks, lax.axis_index("fsdp") ^ k) for k in range(columns)]


def swap_blocks(blocks):
    return blocks[:1] + [swap(block, "fsdp", k) for k, block in enumerate(blocks) if k]


def small_call(kernel, shapes, name, room=6, **options):
    params = pltpu.CompilerParams(vmem_limit_bytes=room * 2**20)
    return pl.pallas_call(kernel, out_shape=shapes, compiler_params=params, name=name, **options)


def fetching_call(kernel, shape, name, arrays, fetched, scratch=()):
    held = [pltpu.VMEM(array.shape, array.dtype) for array in arrays[:fetched]]
    return small_call(
        kernel,
        shape,
        name,
        room=60,
        in_specs=[pl.BlockSpec(memory_space=pltpu.MemorySpace.HBM)] * len(arrays),
        scratch_shapes=held + list(scratch) + [pltpu.SemaphoreType.DMA((fetched,))],
    )(*arrays)


def fetch(sources, targets, sem):
    copies = [pltpu.make_async_copy(s, t, sem.at[k]) for k, (s, t) in enumerate(zip(sources, targets))]
    for copy in copies:
        copy.start()
    return copies


def pack_far_kernel(merge_hbm, inner_hbm, outer_hbm, after_ref, far_ref, merge_ref, inner_ref, outer_ref, sem):
    for copy in fetch((merge_hbm, inner_hbm, outer_hbm), (merge_ref, inner_ref, outer_ref), sem):
        copy.wait()
    own, width = merge_ref.shape
    parts = inner_ref.shape[1] // width
    far_ref[:, :width] = merge_ref[...]
    for j in range(parts):
        for d in range(width // own):
            first, source = (1 + j) * width + d * own, (d * parts + j) * own
            far_ref[:, first : first + own] = inner_ref[:, source : source + own]
        first = (1 + parts + j) * width
        far_ref[:, first : first + width] = outer_ref[j * own : (j + 1) * own, :]


def pack_near_kernel(vectors, *refs):
    sources, near_ref, held = refs[: 3 + vectors], refs[3 + vectors], refs[4 + vectors : 7 + 2 * vectors]
    rows_ref, sem = refs[-2:]
    for copy in fetch(sources, held, sem):
        copy.wait()
    lines = held[3:]
    own, width = held[0].shape
    for g in range(width // GROUP):
        for k, source in enumerate(held[:3]):
            first = (3 * g + k) * GROUP
            near_ref[:, first : first + GROUP] = source[:, g * GROUP : (g + 1) * GROUP]
    rows_ref[...] = jnp.zeros_like(rows_ref)
    row = 0
    for line in lines:
        values = line[...].astype(F32)
        for j in range(line.shape[0] // own):
            rows_ref[row : row + 1, :own] = values[j * own : (j + 1) * own].reshape(1, own)
            row += 1
    near_ref[:, 3 * width :] = rows_ref[...].T[:own].astype(BF16)


def unpack_kernel(far_ref, merge_ref, inner_ref, outer_ref):
    own, width = merge_ref.shape
    parts = inner_ref.shape[1] // width
    merge_ref[...] = far_ref[:, :width].astype(F32)
    for j in range(parts):
        block = far_ref[:, (1 + j) * width : (2 + j) * width].astype(F32)
        for d in range(width // own):
            target = (d * parts + j) * own
            inner_ref[:, target : target + own] = block[:, d * own : (d + 1) * own]
        outer_ref[j * own : (j + 1) * own, :] = far_ref[:, (1 + parts + j) * width : (2 + parts + j) * width].astype(F32)


def finish_kernel(all_tokens, lines, *refs):
    blocks, (query_ref, key_ref, value_ref), rest = refs[: -(lines + 5)], refs[-(lines + 5) : -(lines + 2)], refs[-(lines + 2) :]
    vector_refs, stats_ref, long_ref = rest[:lines], rest[lines], rest[lines + 1]
    total = tree_sum([block[...] for block in blocks])
    own, width = query_ref.shape
    for g in range(width // GROUP):
        for k, target in enumerate((query_ref, key_ref, value_ref)):
            first = (3 * g + k) * GROUP
            target[:, g * GROUP : (g + 1) * GROUP] = total[:, first : first + GROUP]
    vectors = total[:, 3 * width :].T
    for row, target in enumerate(vector_refs):
        for j in range(target.shape[0] // own):
            long_ref[0:1, j * own : (j + 1) * own] = vectors[row + j : row + j + 1, :]
        target[...] = long_ref[0:1, : target.shape[0]].reshape(target.shape[0])
    line = total[0:1, 3 * width :]
    lane = lax.broadcasted_iota(jnp.int32, line.shape, 1)
    scale = jnp.zeros_like(line)
    for digit in range(DIGITS):
        scale = jnp.where(lane == 20 + digit, 8.0**digit, scale)
    valid = jnp.sum(line * scale, axis=1, keepdims=True)
    roots = jnp.sqrt(jnp.where((lane >= 16) & (lane < 20), line, 0.0) / (valid * width))
    roots = jnp.where(lane == 15, valid / all_tokens, roots)
    stats_ref[...] = roots[:, 15:20].reshape(5)


def pack_near(query, key, value, vectors):
    own, width = query.shape
    if quick(own):
        shape = jax.ShapeDtypeStruct((own, 3 * width + VEC), query.dtype)
        kernel = functools.partial(pack_near_kernel, len(vectors))
        arrays = (query, key, value, *vectors)
        return fetching_call(kernel, shape, "pack_near", arrays, len(arrays), [pltpu.VMEM((VEC, VEC), F32)])
    columns = jnp.concatenate([vector.reshape(-1, own) for vector in vectors]).T
    columns = jnp.pad(columns, ((0, 0), (0, VEC - columns.shape[1])))
    groups = range(0, width, GROUP)
    triples = [mat[:, first : first + GROUP] for first in groups for mat in (query, key, value)]
    return jnp.concatenate(triples + [columns], axis=1)


def pack_far(merge, inner, outer, after):
    own, width = merge.shape
    parts = inner.shape[1] // width
    if quick(own):
        shape = jax.ShapeDtypeStruct((own, (1 + 2 * parts) * width), merge.dtype)
        return fetching_call(pack_far_kernel, shape, "pack_far", (merge, inner, outer, after), 3)
    inner = inner.reshape(own, width // own, parts, own).transpose(0, 2, 1, 3).reshape(own, parts * width)
    outer = outer.reshape(parts, own, width).transpose(1, 0, 2).reshape(own, parts * width)
    return jnp.concatenate([merge, inner, outer], axis=1)


def unpack_far(far, parts):
    own, width = far.shape[0], far.shape[1] // (1 + 2 * parts)
    if quick(own):
        shapes = [(own, width), (own, parts * width), (parts * own, width)]
        shapes = [jax.ShapeDtypeStruct(shape, F32) for shape in shapes]
        return small_call(unpack_kernel, shapes, "unpack_far")(far)
    far = far.astype(F32)
    inner = far[:, width : (1 + parts) * width].reshape(own, parts, width // own, own)
    outer = far[:, (1 + parts) * width :].reshape(own, parts, width)
    return (
        far[:, :width],
        inner.transpose(0, 2, 1, 3).reshape(own, parts * width),
        outer.transpose(1, 0, 2).reshape(parts * own, width),
    )


def finish_near(blocks, parts, all_tokens, stats, valid_own):
    own = blocks[0].shape[0]
    width = (blocks[0].shape[1] - VEC) // 3
    sizes = [own] * 8 + [parts * own]
    if quick(own):
        shapes = [(own, width)] * 3 + [(size,) for size in sizes] + [(5,)]
        shapes = [jax.ShapeDtypeStruct(shape, F32) for shape in shapes]
        kernel = functools.partial(finish_kernel, all_tokens, len(sizes))
        scratch = [pltpu.VMEM((8, max(sizes)), F32)]
        query, key, value, *rest = small_call(kernel, shapes, "finish_near", scratch_shapes=scratch)(*blocks)
        return query, key, value, rest[:-1], rest[-1]
    total = tree_sum(blocks)
    triple = total[:, : 3 * width].reshape(own, width // GROUP, 3, GROUP)
    mine = total[:, 3 * width :].T
    sums = lax.psum(jnp.concatenate([jnp.sum(stats[:4], axis=1), valid_own[None]]), AXES)
    layer_stats = jnp.concatenate([sums[4:] / all_tokens, jnp.sqrt(sums[:4] / (sums[4] * width))])
    vectors = [mine[row] for row in range(8)] + [mine[8 : 8 + parts].reshape(parts * own)]
    return *(triple[:, :, k].reshape(own, width) for k in range(3)), vectors, layer_stats


def per_device(
    layer_input, cotangent, doc_lengths, pad_tail,
    query_weight, query_bias, key_weight, value_weight, value_bias,
    merge_weight, merge_bias, first_gain, first_shift,
    inner_weight, inner_bias, outer_weight, outer_bias, second_gain, second_shift,
):
    seqs, _, width = layer_input.shape
    own = query_weight.shape[0]
    devices = width // own
    parts = inner_weight.shape[1] // width
    groups = width // GROUP

    vectors = (query_bias, value_bias, merge_bias, first_gain, first_shift, outer_bias, second_gain, second_shift, inner_bias)
    near_own = pack_near(query_weight, key_weight, value_weight, vectors)
    near = quick_gather(near_own)
    far = gather(pack_far(merge_weight, inner_weight, outer_weight, near_own))
    segment, low, count = segments(doc_lengths, pad_tail)
    segment = segment[:, None, :]

    vec_rows = near[:, 3 * width :].T.astype(F32)
    bias = jnp.stack([vec_rows[0], jnp.zeros((width,), F32), vec_rows[1]])
    bias = bias.reshape(3, groups, GROUP).transpose(1, 0, 2).reshape(1, 3 * width)
    vec = vec_rows[:24]

    qkv, mixed, lse = attention_forward(layer_input, near, bias, segment, low, count)
    tokens = seqs * LEN
    flat_mixed = mixed.reshape(tokens, width)
    output, normed, inverse, upper, slope, outer_partial, sums, stats = upper_half(
        flat_mixed, layer_input.reshape(tokens, width), cotangent.reshape(tokens, width), far, vec, pad_tail
    )
    outer_grad = over_planes(outer_partial)
    residual, mixed_grad, inner_partial, sums = lower_half(flat_mixed, normed, inverse, upper, slope, far, vec, sums)
    inner_grad = over_planes(inner_partial)
    chips = lax.axis_size("dp") // 2 if quick(own) else 0
    dqkv, keep, send = attention_backward(
        qkv, mixed, mixed_grad.reshape(mixed.shape), layer_input, lse, segment, sums, stats, low, count, pad_tail, chips
    )
    far_planes = jnp.concatenate([inner_grad, outer_grad], axis=1)
    if chips:
        keep, far_planes = lax.optimization_barrier((keep, far_planes))
        far_grad = over_columns(far_planes)
        parts_own = join_cores(keep, send)
        parts_own, residual = lax.optimization_barrier((parts_own, residual))
        near_planes = join_chips(parts_own)
    else:
        far_grad = over_columns(far_planes)
        near_planes = over_planes(keep[0])
    input_gradient = residual + dot(dqkv.reshape(tokens, 3 * width), near[:, : 3 * width], 1, 1)
    if chips:
        near_planes, input_gradient, far_grad = lax.optimization_barrier((near_planes, input_gradient, far_grad))
        near_blocks = swap_blocks(blocks_for_columns(near_planes))
    else:
        near_blocks = [over_columns(near_planes)]
    valid_own = jnp.sum(LEN - pad_tail).astype(F32)
    query_grad, key_grad, value_grad, mine, layer_stats = finish_near(
        near_blocks, parts, tokens * devices, stats, valid_own
    )
    merge_grad, inner_grad, outer_grad = unpack_far(far_grad, parts)
    return (
        output.reshape(layer_input.shape),
        input_gradient.reshape(layer_input.shape),
        query_grad,
        mine[6],
        key_grad,
        value_grad,
        mine[7],
        merge_grad,
        mine[5],
        mine[3],
        mine[4],
        inner_grad,
        mine[8],
        outer_grad,
        mine[2],
        mine[0],
        mine[1],
        layer_stats,
    )


def solution(mesh):
    matrix, vector, cube = P(AXES, None), P(AXES), P(AXES, None, None)
    in_specs = (
        cube, cube, matrix, vector,
        matrix, vector, matrix, matrix, vector,
        matrix, vector, vector, vector,
        matrix, vector, matrix, vector, vector, vector,
    )
    out_specs = (
        cube, cube,
        matrix, vector, matrix, matrix, vector,
        matrix, vector, vector, vector,
        matrix, vector, matrix, vector, vector, vector,
        P(),
    )
    return jax.shard_map(per_device, mesh=mesh, in_specs=in_specs, out_specs=out_specs, check_vma=False)
```

```python
import functools

import jax
import jax.numpy as jnp
from jax import lax
from jax.experimental import pallas as pl
from jax.experimental.pallas import tpu as pltpu
from jax.sharding import PartitionSpec as P

HEAD_DIM = 64
LEN = 1024
DOCS = 8
EPSILON = 1e-12
NEGATIVE = -1e30
ROOT_HALF = 0.7071067811865476
INV_ROOT_TWO_PI = 0.3989422804014327
AXES = ("dp", "fsdp")
F32 = jnp.float32
BF16 = jnp.bfloat16

GROUP = 256
HEADS_IN = GROUP // HEAD_DIM
PAIR = 128
TRIPLE = 3 * GROUP
QB = 256
CHUNK = 256
VEC = 128
DIGITS = 8


def dot(left, right, left_dim=1, right_dim=0):
    return lax.dot_general(
        left, right, (((left_dim,), (right_dim,)), ((), ())), preferred_element_type=F32
    )


def head_masks(columns):
    lane = lax.broadcasted_iota(jnp.int32, (1, columns), 1) // HEAD_DIM
    return [lane == h for h in range(columns // HEAD_DIM)]


def cost(flops, moved):
    return pl.CostEstimate(flops=int(flops), bytes_accessed=int(moved), transcendentals=0)


def segments(doc_lengths, pad_tail):
    ends = jnp.cumsum(doc_lengths, axis=1)
    limit = (LEN - pad_tail)[:, None]
    places = jnp.arange(LEN, dtype=jnp.int32)
    segment = jnp.sum((places[None, :, None] >= ends[:, None, :]).astype(jnp.int32), axis=2)
    segment = jnp.where(places[None] < limit, segment, DOCS)
    borders = jnp.concatenate(
        [jnp.zeros_like(limit), jnp.minimum(ends, limit), limit, jnp.full_like(limit, LEN)], axis=1
    )[:, None, :]
    first = (jnp.arange(LEN // QB, dtype=jnp.int32) * QB)[None, :, None]
    low = jnp.max(jnp.where(borders <= first, borders, 0), axis=2)
    high = jnp.min(jnp.where(borders > first + QB - 1, borders, LEN), axis=2)
    low = (low // 128) * 128
    count = (high - low + CHUNK - 1) // CHUNK
    low = jnp.minimum(low, LEN - CHUNK * count)
    return segment, low.astype(jnp.int32), count.astype(jnp.int32)


def forward_kernel(
    low_ref, count_ref, rows_ref, w_ref, bias_ref, segr_ref,
    qkv_ref, mixed_ref, lse_ref, keyt_ref, segc_ref,
):
    s = pl.program_id(0)
    qkv_ref[...] = (dot(rows_ref[...], w_ref[...]) + bias_ref[0:1, :]).astype(BF16)
    keyt_ref[...] = qkv_ref[:, GROUP : 2 * GROUP].T

    @pl.when(pl.program_id(1) == 0)
    def _():
        segc_ref[...] = jnp.broadcast_to(segr_ref[...], (128, LEN)).T

    masks = head_masks(GROUP)

    def block(i, carry):
        start = pl.multiple_of(i * QB, QB)
        queries = qkv_ref[pl.ds(start, QB), :GROUP] * BF16(HEAD_DIM**-0.5)
        zero = jnp.zeros_like(queries)
        own = segc_ref[pl.ds(start, QB), :][:, :1]
        low = pl.multiple_of(low_ref[s, i], 128)
        count = count_ref[s, i]
        for c in range(1, LEN // CHUNK + 1):

            @pl.when(count == c)
            def _():
                span = pl.ds(low, CHUNK * c)
                keys = keyt_ref[:, span]
                values = qkv_ref[span, 2 * GROUP :]
                allowed = own == segr_ref[0:1, span]
                lane = lax.broadcasted_iota(jnp.int32, (QB, 128), 1)
                mixed = None
                for h in range(HEADS_IN):
                    scores = dot(jnp.where(masks[h], queries, zero), keys)
                    scores = jnp.where(allowed, scores, NEGATIVE)
                    top = jnp.max(scores, axis=1, keepdims=True)
                    expo = jnp.exp(scores - top)
                    total = jnp.sum(expo, axis=1, keepdims=True)
                    part = dot(expo.astype(BF16), values) * (1.0 / total)
                    logsum = top + jnp.log(total)
                    if h == 0:
                        mixed, sums = part, jnp.broadcast_to(logsum, (QB, 128))
                    else:
                        mixed, sums = jnp.where(masks[h], part, mixed), jnp.where(lane == h, logsum, sums)
                mixed_ref[pl.ds(start, QB), :] = mixed.astype(BF16)
                lse_ref[:, pl.ds(start, QB)] = sums.T[:8]

        return carry

    lax.fori_loop(0, LEN // QB, block, 0)


def attention_forward(rows, w, bias, segment, low, count):
    seqs, _, width = rows.shape
    groups = width // GROUP
    return pl.pallas_call(
        forward_kernel,
        grid_spec=pltpu.PrefetchScalarGridSpec(
            num_scalar_prefetch=2,
            grid=(seqs, groups),
            in_specs=[
                pl.BlockSpec((None, LEN, width), lambda s, g, *_: (s, 0, 0)),
                pl.BlockSpec((width, TRIPLE), lambda s, g, *_: (0, g)),
                pl.BlockSpec((1, TRIPLE), lambda s, g, *_: (0, g)),
                pl.BlockSpec((None, 1, LEN), lambda s, g, *_: (s, 0, 0)),
            ],
            out_specs=[
                pl.BlockSpec((None, LEN, TRIPLE), lambda s, g, *_: (s, 0, g)),
                pl.BlockSpec((None, LEN, GROUP), lambda s, g, *_: (s, 0, g)),
                pl.BlockSpec((None, None, 8, LEN), lambda s, g, *_: (s, g, 0, 0)),
            ],
            scratch_shapes=[pltpu.VMEM((GROUP, LEN), BF16), pltpu.VMEM((LEN, 128), jnp.int32)],
        ),
        out_shape=[
            jax.ShapeDtypeStruct((seqs, LEN, 3 * width), BF16),
            jax.ShapeDtypeStruct((seqs, LEN, width), BF16),
            jax.ShapeDtypeStruct((seqs, groups, 8, LEN), F32),
        ],
        compiler_params=pltpu.CompilerParams(vmem_limit_bytes=60 * 2**20),
        cost_estimate=cost(2 * seqs * LEN * width * (3 * width + 16 * LEN), seqs * LEN * width * 10),
        name="attention_forward",
    )(low, count, rows, w, bias, segment)


def backward_kernel(
    chips,
    low_ref, count_ref, pad_ref, plane_ref, qkv_ref, mixed_ref, grad_ref, rows_ref, lse_ref, segr_ref, vec_ref, stats_ref,
    dqkv_ref, keep_ref, send_ref,
    q_ref, qt_ref, gt_ref, kt_ref, dqt_ref, acc_ref, delta_ref, sums_ref, stage_ref, columns_ref, rowst_ref, segc_ref, sem,
):
    s, g = pl.program_id(0), pl.program_id(1)
    masks = head_masks(PAIR)

    @pl.when(g == 0)
    def _():
        rowst_ref[...] = rows_ref[...].T
        segc_ref[...] = jnp.broadcast_to(segr_ref[...], (128, LEN)).T

    @pl.when((g == 0) & (s == 0))
    def _():
        sums_ref[...] = jnp.zeros_like(sums_ref)
        sums_ref[:16, :] = vec_ref[...]

    grad = grad_ref[...]
    prod = grad.astype(F32) * mixed_ref[...].astype(F32)
    coarse = prod.astype(BF16)
    fine = (prod - coarse.astype(F32)).astype(BF16)
    pick = lax.broadcasted_iota(jnp.int32, (8, GROUP), 1) // HEAD_DIM
    pick = (pick == lax.broadcasted_iota(jnp.int32, (8, GROUP), 0)).astype(F32).astype(BF16)
    delta_ref[...] = dot(pick, coarse, 1, 1) + dot(pick, fine, 1, 1)
    queries = qkv_ref[:, :GROUP] * BF16(HEAD_DIM**-0.5)
    q_ref[...] = queries
    qt_ref[...] = queries.T
    gt_ref[...] = grad.T
    kt_ref[...] = qkv_ref[:, GROUP : 2 * GROUP].T
    dqt_ref[...] = jnp.zeros_like(dqt_ref)

    def block(i, carry):
        start = pl.multiple_of(i * QB, QB)
        mine = pl.ds(start, QB)
        keys = qkv_ref[mine, GROUP : 2 * GROUP]
        values = qkv_ref[mine, 2 * GROUP :]
        zero = jnp.zeros((QB, PAIR), BF16)
        own = segc_ref[mine, :][:, :1]
        low = pl.multiple_of(low_ref[s, i], 128)
        count = count_ref[s, i]
        for c in range(1, LEN // CHUNK + 1):

            @pl.when(count == c)
            def _():
                span = pl.ds(low, CHUNK * c)
                allowed = own == segr_ref[0:1, span]
                for h in range(HEADS_IN):
                    mask, lanes = masks[h % 2], slice(h // 2 * PAIR, (h // 2 + 1) * PAIR)
                    scores = dot(jnp.where(mask, keys[:, lanes], zero), qt_ref[lanes, span])
                    probs = jnp.exp(jnp.where(allowed, scores, NEGATIVE) - lse_ref[h : h + 1, span])
                    pgrad = dot(jnp.where(mask, values[:, lanes], zero), gt_ref[lanes, span])
                    low_score = (probs * (pgrad - delta_ref[h : h + 1, span])).astype(BF16)
                    v_part = dot(probs.astype(BF16), grad_ref[span, lanes])
                    k_part = dot(low_score, q_ref[span, lanes])
                    head = slice(h * HEAD_DIM, (h + 1) * HEAD_DIM)
                    dqt_ref[head, span] += dot(kt_ref[head, mine], low_score)
                    if h % 2 == 0:
                        dkey, dvalue = k_part, v_part
                    else:
                        first = h // 2 * PAIR
                        dkey, dvalue = jnp.where(mask, k_part, dkey), jnp.where(mask, v_part, dvalue)
                        dqkv_ref[mine, GROUP + first : GROUP + first + PAIR] = dkey.astype(BF16)
                        dqkv_ref[mine, 2 * GROUP + first : 2 * GROUP + first + PAIR] = dvalue.astype(BF16)

        return carry

    lax.fori_loop(0, LEN // QB, block, 0)
    dqkv_ref[:, :GROUP] = (dqt_ref[...] * HEAD_DIM**-0.5).astype(BF16).T
    dqkv = dqkv_ref[...]
    dw = dot(rowst_ref[...], dqkv)
    sums = jnp.sum(dqkv.astype(F32), axis=0, keepdims=True)
    lanes = pl.ds(pl.multiple_of(g * GROUP, GROUP), GROUP)
    sums_ref[6:7, lanes] += sums[:, :GROUP]
    sums_ref[7:8, lanes] += sums[:, 2 * GROUP :]

    @pl.when(s == 0)
    def _():
        acc_ref[g] = dw

    @pl.when(s > 0)
    def _():
        acc_ref[g] += dw

    last_s, last_g = pl.num_programs(0) - 1, pl.num_programs(1) - 1

    def copies(source, lanes, first_sem):
        if chips == 0:
            return [pltpu.make_async_copy(source, keep_ref.at[0, :, lanes], sem.at[first_sem])]
        rows = source.shape[0] // (2 * chips)
        core, chip = plane_ref[0] & 1, lax.shift_right_logical(plane_ref[0], 1)
        moves = []
        for m in range(chips):
            for side, target in enumerate((keep_ref, send_ref)):
                owner = 2 * (chip ^ m) + (core ^ side)
                piece = source.at[pl.ds(pl.multiple_of(owner * rows, rows), rows), :]
                moves.append(pltpu.make_async_copy(piece, target.at[m, :, lanes], sem.at[first_sem + 2 * m + side]))
        return moves

    def group_copies(group):
        return copies(stage_ref, pl.ds(pl.multiple_of(group * TRIPLE, TRIPLE), TRIPLE), 0)

    @pl.when(s == last_s)
    def _():
        @pl.when(g > 0)
        def _():
            for move in group_copies(g - 1):
                move.wait()

        stage_ref[...] = acc_ref[g].astype(BF16)
        for move in group_copies(g):
            move.start()

    @pl.when((g == last_g) & (s == last_s))
    def _():
        for row in range(4):
            value = jnp.sum(stats_ref[row : row + 1, :], axis=1, keepdims=True)
            sums_ref[16 + row : 17 + row, :] = jnp.broadcast_to(value, (1, sums_ref.shape[1]))
        tokens = pl.num_programs(0) * LEN
        for seq in range(pad_ref.shape[0]):
            tokens -= pad_ref[seq]
        for row in range(DIGITS):
            digit = (lax.shift_right_logical(tokens, 3 * row) & 7).astype(F32)
            sums_ref[20 + row : 21 + row, :] = jnp.full((1, sums_ref.shape[1]), digit)
        columns_ref[...] = sums_ref[...].T.astype(BF16)
        width = sums_ref.shape[1]
        moves = copies(columns_ref, slice(3 * width, 3 * width + VEC), max(1, 2 * chips))
        for move in moves:
            move.start()
        for move in group_copies(g) + moves:
            move.wait()


def attention_backward(qkv, mixed, grad, rows, lse, segment, vec, stats, low, count, pad, chips):
    seqs, _, width = mixed.shape
    groups = width // GROUP
    plane = lax.axis_index("dp").astype(jnp.int32).reshape(1)
    packed = (max(1, chips), width // max(1, 2 * chips), 3 * width + VEC)
    return pl.pallas_call(
        functools.partial(backward_kernel, chips),
        grid_spec=pltpu.PrefetchScalarGridSpec(
            num_scalar_prefetch=4,
            grid=(seqs, groups),
            in_specs=[
                pl.BlockSpec((None, LEN, TRIPLE), lambda s, g, *_: (s, 0, g)),
                pl.BlockSpec((None, LEN, GROUP), lambda s, g, *_: (s, 0, g)),
                pl.BlockSpec((None, LEN, GROUP), lambda s, g, *_: (s, 0, g)),
                pl.BlockSpec((None, LEN, width), lambda s, g, *_: (s, 0, 0)),
                pl.BlockSpec((None, None, 8, LEN), lambda s, g, *_: (s, g, 0, 0)),
                pl.BlockSpec((None, 1, LEN), lambda s, g, *_: (s, 0, 0)),
                pl.BlockSpec((16, width), lambda s, g, *_: (0, 0)),
                pl.BlockSpec((8, width), lambda s, g, *_: (0, 0)),
            ],
            out_specs=[
                pl.BlockSpec((None, LEN, TRIPLE), lambda s, g, *_: (s, 0, g)),
                pl.BlockSpec(memory_space=pl.ANY),
                pl.BlockSpec(memory_space=pl.ANY),
            ],
            scratch_shapes=[
                pltpu.VMEM((LEN, GROUP), BF16),
                pltpu.VMEM((GROUP, LEN), BF16),
                pltpu.VMEM((GROUP, LEN), BF16),
                pltpu.VMEM((GROUP, LEN), BF16),
                pltpu.VMEM((GROUP, LEN), F32),
                pltpu.VMEM((groups, width, TRIPLE), F32),
                pltpu.VMEM((8, LEN), F32),
                pltpu.VMEM((VEC, width), F32),
                pltpu.VMEM((width, TRIPLE), BF16),
                pltpu.VMEM((width, VEC), BF16),
                pltpu.VMEM((width, LEN), BF16),
                pltpu.VMEM((LEN, 128), jnp.int32),
                pltpu.SemaphoreType.DMA((2 * max(1, 2 * chips),)),
            ],
        ),
        out_shape=[
            jax.ShapeDtypeStruct((seqs, LEN, 3 * width), BF16),
            jax.ShapeDtypeStruct(packed, BF16),
            jax.ShapeDtypeStruct(packed if chips else (8, 128), BF16),
        ],
        compiler_params=pltpu.CompilerParams(vmem_limit_bytes=60 * 2**20),
        cost_estimate=cost(2 * seqs * LEN * width * (3 * width + 32 * LEN), seqs * LEN * width * 20),
        name="attention_backward",
    )(low, count, pad, plane, qkv, mixed, grad, rows, lse, segment, vec, stats)


def mean(values):
    return jnp.mean(values, axis=1, keepdims=True)


def normed_of(values):
    centred = values - mean(values)
    inverse = lax.rsqrt(mean(centred * centred) + EPSILON)
    return centred * inverse, inverse


def norm_backward(scaled, normed, inverse):
    return inverse * (scaled - mean(scaled) - normed * mean(scaled * normed))


def add_rows(sums_ref, row, values):
    sums_ref[row] += jnp.sum(values.reshape(-1, 8, values.shape[1]), axis=0)


class Blocks:
    def __init__(self, wide_ref, held_ref, sem, first_step):
        self.wide_ref, self.held_ref, self.sem, self.first_step = wide_ref, held_ref, sem, first_step

    def copy(self, k):
        width = self.held_ref.shape[2]
        columns = pl.ds(pl.multiple_of(k * width, width), width)
        return pltpu.make_async_copy(self.wide_ref.at[:, columns], self.held_ref.at[k], self.sem.at[k])

    def start(self, order):
        @pl.when(self.first_step)
        def _():
            for k in order:
                self.copy(k).start()

    def wait(self, k):
        @pl.when(self.first_step)
        def _():
            self.copy(k).wait()


def out_copy(stage_ref, dw_ref, sem, k):
    width = stage_ref.shape[1]
    columns = pl.ds(pl.multiple_of(k * width, width), width)
    slot = lax.rem(k, 2)
    return pltpu.make_async_copy(stage_ref.at[slot], dw_ref.at[:, columns], sem.at[slot])


def send_blocks(gradient, first, amount, stage_ref, dw_ref, sem):
    def step(j, carry):
        k = first + j

        @pl.when(j >= 2)
        def _():
            out_copy(stage_ref, dw_ref, sem, k - 2).wait()

        stage_ref[lax.rem(k, 2)] = gradient(j)
        out_copy(stage_ref, dw_ref, sem, k).start()
        return carry

    lax.fori_loop(0, amount, step, 0)


def upper_kernel(
    parts, width, tokens,
    pad_ref, mixed_ref, rows_ref, cot_ref, w_ref, vec_ref,
    out_ref, normed_ref, inverse_ref, upper_ref, slope_ref, dw_ref, sums_ref, stats_ref,
    held_ref, hidden_ref, low_ref, uppert_ref, stage_ref, part_ref, w_sem, sem,
):
    i = pl.program_id(0)
    last = i == pl.num_programs(0) - 1
    per_seq = LEN // tokens
    weights = Blocks(w_ref, held_ref, w_sem, i == 0)
    weights.start([0] + [k + j for j in range(parts) for k in (1, 1 + parts)])

    @pl.when(i == 0)
    def _():
        part_ref[...] = jnp.zeros_like(part_ref)

    def vector(row):
        return vec_ref[row + 2 : row + 3, :]

    def valid_of():
        place = (i % per_seq) * tokens + lax.broadcasted_iota(jnp.int32, (tokens, 1), 0)
        return (place < LEN - pad_ref[i // per_seq]).astype(F32)

    mine = pl.ds(pl.multiple_of(i * tokens, tokens), tokens)
    weights.wait(0)
    upper_ref[...] = dot(mixed_ref[...], held_ref[0])

    valid = valid_of()
    rows = rows_ref[...].astype(F32)
    branch = upper_ref[...] + vector(0)
    add_rows(part_ref, 3, valid * rows * rows)
    add_rows(part_ref, 4, valid * branch * branch)
    normed, inverse = normed_of(rows + branch)
    normed_ref[...] = normed
    inverse_ref[...] = jnp.broadcast_to(inverse, (tokens, 128))
    first = normed * vector(1) + vector(2)
    low_ref[...] = first.astype(BF16)
    upper_ref[...] = first + vector(3)

    def feed(j, carry):
        weights.wait(1 + j)
        weights.wait(1 + parts + j)
        inner = dot(low_ref[...], held_ref[1 + j]) + vec_ref[pl.ds(8 + j, 1), :]
        half = 0.5 * (1.0 + lax.erf(inner * ROOT_HALF))
        hidden = (inner * half).astype(BF16)
        hidden_ref[j, mine, :] = hidden
        slope = half + inner * jnp.exp(-0.5 * inner * inner) * INV_ROOT_TWO_PI
        slope_ref[:, pl.ds(pl.multiple_of(j * width, width), width)] = slope.astype(BF16)
        upper_ref[...] += dot(hidden, held_ref[1 + parts + j])
        return carry

    lax.fori_loop(0, parts, feed, 0)

    valid = valid_of()
    total = upper_ref[...]
    second = total - (normed_ref[...] * vector(1) + vector(2))
    add_rows(part_ref, 5, valid * second * second)
    normed, inverse = normed_of(total)
    result = normed * vector(4) + vector(5)
    add_rows(part_ref, 6, valid * result * result)
    out_ref[...] = result.astype(BF16)
    upstream = cot_ref[...].astype(F32) * valid
    add_rows(part_ref, 0, upstream * normed)
    add_rows(part_ref, 1, upstream)
    upper = norm_backward(upstream * vector(4), normed, inverse)
    upper_ref[...] = upper
    upper_low = upper.astype(BF16)
    add_rows(part_ref, 2, upper_low.astype(F32))
    uppert_ref[:, mine] = upper_low.T

    @pl.when(last)
    def _():
        sums_ref[...] = jnp.zeros_like(sums_ref)
        for row in range(3):
            sums_ref[row : row + 1, :] = jnp.sum(part_ref[row], axis=0, keepdims=True)
        for row in range(4):
            stats_ref[row : row + 1, :] = jnp.sum(part_ref[3 + row], axis=0, keepdims=True)
        stats_ref[4:, :] = jnp.zeros_like(stats_ref[4:, :])
        send_blocks(
            lambda j: dot(uppert_ref[...], hidden_ref[j]).astype(BF16).T, 0, parts, stage_ref, dw_ref, sem
        )
        for k in (parts - 2, parts - 1):
            out_copy(stage_ref, dw_ref, sem, k).wait()


def lower_kernel(
    parts, width, tokens,
    mixed_ref, normed_ref, inverse_ref, upper_ref, slope_ref, w_ref, vec_ref, sums_in_ref,
    res_ref, mgrad_ref, dw_ref, sums_ref,
    held_ref, low_ref, first_ref, acc_ref, stage_ref, part_ref, w_sem, sem,
):
    i = pl.program_id(0)
    last = i == pl.num_programs(0) - 1
    weights = Blocks(w_ref, held_ref, w_sem, i == 0)
    weights.start([k + j for j in range(parts) for k in (1 + parts, 1)] + [0])

    @pl.when(i == 0)
    def _():
        acc_ref[...] = jnp.zeros_like(acc_ref)
        part_ref[...] = jnp.zeros_like(part_ref)

    def vector(row):
        return vec_ref[row + 2 : row + 3, :]

    upper = upper_ref[...]
    res_ref[...] = upper
    low_ref[...] = upper.astype(BF16)
    first_ref[...] = (normed_ref[...] * vector(1) + vector(2)).astype(BF16)

    first_t = first_ref[...].T

    def back(j, carry):
        weights.wait(1 + parts + j)
        weights.wait(1 + j)
        slope = slope_ref[:, pl.ds(pl.multiple_of(j * width, width), width)].astype(F32)
        inner_low = (dot(low_ref[...], held_ref[1 + parts + j], 1, 1) * slope).astype(BF16)
        add_rows(part_ref, 3 + j, inner_low.astype(F32))
        acc_ref[1 + j] += dot(first_t, inner_low)
        res_ref[...] += dot(inner_low, held_ref[1 + j], 1, 1)

        @pl.when(last)
        def _():
            @pl.when(j >= 2)
            def _():
                out_copy(stage_ref, dw_ref, sem, j - 1).wait()

            stage_ref[lax.rem(1 + j, 2)] = acc_ref[1 + j].astype(BF16)
            out_copy(stage_ref, dw_ref, sem, 1 + j).start()

        return carry

    lax.fori_loop(0, parts, back, 0)

    first_grad = res_ref[...]
    normed = normed_ref[...]
    add_rows(part_ref, 0, first_grad * normed)
    add_rows(part_ref, 1, first_grad)
    residual = norm_backward(first_grad * vector(1), normed, inverse_ref[:, :1])
    res_ref[...] = residual
    branch_low = residual.astype(BF16)
    add_rows(part_ref, 2, branch_low.astype(F32))
    low_ref[...] = branch_low

    weights.wait(0)
    acc_ref[0] += dot(mixed_ref[...], low_ref[...], 0, 0)
    mgrad_ref[...] = dot(low_ref[...], held_ref[0], 1, 1).astype(BF16)

    @pl.when(last)
    def _():
        sums_ref[...] = sums_in_ref[...]
        for row in range(3):
            sums_ref[3 + row : 4 + row, :] = jnp.sum(part_ref[row], axis=0, keepdims=True)
        for j in range(parts):
            sums_ref[8 + j : 9 + j, :] = jnp.sum(part_ref[3 + j], axis=0, keepdims=True)
        for k in (parts - 1, parts):
            out_copy(stage_ref, dw_ref, sem, k).wait()
        stage_ref[0] = acc_ref[0].astype(BF16)
        out_copy(stage_ref, dw_ref, sem, 0).start()
        out_copy(stage_ref, dw_ref, sem, 0).wait()


def upper_half(mixed, rows, cotangent, w, vec, pad, tokens=512):
    count, width = mixed.shape
    parts = (w.shape[1] // width - 1) // 2

    def block(columns):
        return pl.BlockSpec((tokens, columns), lambda i, *_: (i, 0))

    def fixed(*shape):
        return pl.BlockSpec(shape, lambda i, *_: (0, 0))

    anywhere = pl.BlockSpec(memory_space=pl.ANY)
    return pl.pallas_call(
        functools.partial(upper_kernel, parts, width, tokens),
        grid_spec=pltpu.PrefetchScalarGridSpec(
            num_scalar_prefetch=1,
            grid=(count // tokens,),
            in_specs=[block(width), block(width), block(width), anywhere, fixed(24, width)],
            out_specs=[
                block(width), block(width), block(128), block(width), block(parts * width), anywhere,
                fixed(16, width), fixed(8, width),
            ],
            scratch_shapes=[
                pltpu.VMEM((1 + 2 * parts, width, width), BF16),
                pltpu.VMEM((parts, count, width), BF16),
                pltpu.VMEM((tokens, width), BF16),
                pltpu.VMEM((width, count), BF16),
                pltpu.VMEM((2, width, width), BF16),
                pltpu.VMEM((8, 8, width), F32),
                pltpu.SemaphoreType.DMA((1 + 2 * parts,)),
                pltpu.SemaphoreType.DMA((2,)),
            ],
        ),
        out_shape=[
            jax.ShapeDtypeStruct((count, width), BF16),
            jax.ShapeDtypeStruct((count, width), F32),
            jax.ShapeDtypeStruct((count, 128), F32),
            jax.ShapeDtypeStruct((count, width), F32),
            jax.ShapeDtypeStruct((count, parts * width), BF16),
            jax.ShapeDtypeStruct((width, parts * width), BF16),
            jax.ShapeDtypeStruct((16, width), F32),
            jax.ShapeDtypeStruct((8, width), F32),
        ],
        compiler_params=pltpu.CompilerParams(vmem_limit_bytes=60 * 2**20),
        cost_estimate=cost(2 * count * width * width * (1 + 3 * parts), count * width * 40 + 4 * w.size),
        name="upper_half",
    )(pad, mixed, rows, cotangent, w, vec)


def lower_half(mixed, normed, inverse, upper, slope, w, vec, sums, tokens=512):
    count, width = mixed.shape
    parts = (w.shape[1] // width - 1) // 2

    def block(columns):
        return pl.BlockSpec((tokens, columns), lambda i: (i, 0))

    def fixed(*shape):
        return pl.BlockSpec(shape, lambda i: (0, 0))

    anywhere = pl.BlockSpec(memory_space=pl.ANY)
    return pl.pallas_call(
        functools.partial(lower_kernel, parts, width, tokens),
        grid=(count // tokens,),
        in_specs=[
            block(width), block(width), block(128), block(width), block(parts * width), anywhere,
            fixed(24, width), fixed(16, width),
        ],
        out_specs=[block(width), block(width), anywhere, fixed(16, width)],
        scratch_shapes=[
            pltpu.VMEM((1 + 2 * parts, width, width), BF16),
            pltpu.VMEM((tokens, width), BF16),
            pltpu.VMEM((tokens, width), BF16),
            pltpu.VMEM((1 + parts, width, width), F32),
            pltpu.VMEM((2, width, width), BF16),
            pltpu.VMEM((3 + parts, 8, width), F32),
            pltpu.SemaphoreType.DMA((1 + 2 * parts,)),
            pltpu.SemaphoreType.DMA((2,)),
        ],
        out_shape=[
            jax.ShapeDtypeStruct((count, width), F32),
            jax.ShapeDtypeStruct((count, width), BF16),
            jax.ShapeDtypeStruct((width, (1 + parts) * width), BF16),
            jax.ShapeDtypeStruct((16, width), F32),
        ],
        compiler_params=pltpu.CompilerParams(vmem_limit_bytes=60 * 2**20),
        cost_estimate=cost(2 * count * width * width * (2 + 3 * parts), count * width * 40 + 4 * w.size),
        name="lower_half",
    )(mixed, normed, inverse, upper, slope, w, vec, sums)


def gather(shard):
    return lax.all_gather(shard, AXES, axis=0, tiled=True)


def swap(values, axis, flip):
    return lax.ppermute(values, axis, [(d, d ^ flip) for d in range(lax.axis_size(axis))])


def place_kernel(columns, lines, where_ref, *refs):
    sources, target = refs[:lines], refs[lines]
    plane, column = where_ref[0], where_ref[1]
    for m, source in enumerate(sources):
        for k in range(columns):
            target[(plane ^ m) * columns + (column ^ k)] = source[k]


def quick_gather(shard):
    planes, columns = lax.axis_size("dp"), lax.axis_size("fsdp")
    rows, width = shard.shape
    if not quick(rows):
        return gather(shard)
    column = jnp.stack([shard] + [swap(shard, "fsdp", k) for k in range(1, columns)])
    even = [column] + [swap(column, "dp", m) for m in range(2, planes, 2)]
    odd = [swap(part, "dp", 1) for part in even]
    sources = [part for pair in zip(even, odd) for part in pair]
    where = jnp.stack([lax.axis_index("dp"), lax.axis_index("fsdp")]).astype(jnp.int32)
    whole = pl.pallas_call(
        functools.partial(place_kernel, columns, len(sources)),
        grid_spec=pltpu.PrefetchScalarGridSpec(
            num_scalar_prefetch=1,
            grid=(1,),
            in_specs=[pl.BlockSpec((columns, rows, width), lambda i, *_: (0, 0, 0))] * len(sources),
            out_specs=pl.BlockSpec((planes * columns, rows, width), lambda i, *_: (0, 0, 0)),
        ),
        out_shape=jax.ShapeDtypeStruct((planes * columns, rows, width), shard.dtype),
        compiler_params=pltpu.CompilerParams(vmem_limit_bytes=24 * 2**20),
        name="place",
    )(where, *sources)
    return whole.reshape(planes * columns * rows, width)


def tree_sum(parts):
    parts = [part.astype(F32) for part in parts]
    while len(parts) > 1:
        parts = [a + b for a, b in zip(parts[::2], parts[1::2])]
    return parts[0]


def quick(rows):
    return lax.axis_size("dp") % 2 == 0 and rows % 8 == 0


def pick(values, index):
    return lax.dynamic_index_in_dim(values, index, 0, keepdims=False)


def over_planes(partial):
    return lax.psum_scatter(partial, "dp", scatter_dimension=0, tiled=True)


def over_columns(partial):
    return lax.psum_scatter(partial, "fsdp", scatter_dimension=0, tiled=True)


def join_cores(keep, send):
    other = swap(send, "dp", 1)
    return [tree_sum([keep[m], other[m]]).astype(keep.dtype) for m in range(keep.shape[0])]


def join_chips(parts):
    return tree_sum(parts[:1] + [swap(part, "dp", 2 * m) for m, part in enumerate(parts) if m]).astype(parts[0].dtype)


def blocks_for_columns(partial):
    columns = lax.axis_size("fsdp")
    blocks = partial.reshape(columns, partial.shape[0] // columns, partial.shape[1])
    return [pick(blocks, lax.axis_index("fsdp") ^ k) for k in range(columns)]


def swap_blocks(blocks):
    return blocks[:1] + [swap(block, "fsdp", k) for k, block in enumerate(blocks) if k]


def small_call(kernel, shapes, name, room=6, **options):
    params = pltpu.CompilerParams(vmem_limit_bytes=room * 2**20)
    return pl.pallas_call(kernel, out_shape=shapes, compiler_params=params, name=name, **options)


def fetching_call(kernel, shape, name, arrays, fetched, scratch=()):
    held = [pltpu.VMEM(array.shape, array.dtype) for array in arrays[:fetched]]
    return small_call(
        kernel,
        shape,
        name,
        room=60,
        in_specs=[pl.BlockSpec(memory_space=pltpu.MemorySpace.HBM)] * len(arrays),
        scratch_shapes=held + list(scratch) + [pltpu.SemaphoreType.DMA((fetched,))],
    )(*arrays)


def fetch(sources, targets, sem):
    copies = [pltpu.make_async_copy(s, t, sem.at[k]) for k, (s, t) in enumerate(zip(sources, targets))]
    for copy in copies:
        copy.start()
    return copies


def pack_far_kernel(merge_hbm, inner_hbm, outer_hbm, after_ref, far_ref, merge_ref, inner_ref, outer_ref, sem):
    for copy in fetch((merge_hbm, inner_hbm, outer_hbm), (merge_ref, inner_ref, outer_ref), sem):
        copy.wait()
    own, width = merge_ref.shape
    parts = inner_ref.shape[1] // width
    far_ref[:, :width] = merge_ref[...]
    for j in range(parts):
        for d in range(width // own):
            first, source = (1 + j) * width + d * own, (d * parts + j) * own
            far_ref[:, first : first + own] = inner_ref[:, source : source + own]
        first = (1 + parts + j) * width
        far_ref[:, first : first + width] = outer_ref[j * own : (j + 1) * own, :]


def pack_near_kernel(vectors, *refs):
    sources, near_ref, held = refs[: 3 + vectors], refs[3 + vectors], refs[4 + vectors : 7 + 2 * vectors]
    rows_ref, sem = refs[-2:]
    for copy in fetch(sources, held, sem):
        copy.wait()
    lines = held[3:]
    own, width = held[0].shape
    for g in range(width // GROUP):
        for k, source in enumerate(held[:3]):
            first = (3 * g + k) * GROUP
            near_ref[:, first : first + GROUP] = source[:, g * GROUP : (g + 1) * GROUP]
    rows_ref[...] = jnp.zeros_like(rows_ref)
    row = 0
    for line in lines:
        values = line[...].astype(F32)
        for j in range(line.shape[0] // own):
            rows_ref[row : row + 1, :own] = values[j * own : (j + 1) * own].reshape(1, own)
            row += 1
    near_ref[:, 3 * width :] = rows_ref[...].T[:own].astype(BF16)


def unpack_kernel(far_ref, merge_ref, inner_ref, outer_ref):
    own, width = merge_ref.shape
    parts = inner_ref.shape[1] // width
    merge_ref[...] = far_ref[:, :width].astype(F32)
    for j in range(parts):
        block = far_ref[:, (1 + j) * width : (2 + j) * width].astype(F32)
        for d in range(width // own):
            target = (d * parts + j) * own
            inner_ref[:, target : target + own] = block[:, d * own : (d + 1) * own]
        outer_ref[j * own : (j + 1) * own, :] = far_ref[:, (1 + parts + j) * width : (2 + parts + j) * width].astype(F32)


def finish_kernel(all_tokens, lines, *refs):
    blocks, (query_ref, key_ref, value_ref), rest = refs[: -(lines + 5)], refs[-(lines + 5) : -(lines + 2)], refs[-(lines + 2) :]
    vector_refs, stats_ref, long_ref = rest[:lines], rest[lines], rest[lines + 1]
    total = tree_sum([block[...] for block in blocks])
    own, width = query_ref.shape
    for g in range(width // GROUP):
        for k, target in enumerate((query_ref, key_ref, value_ref)):
            first = (3 * g + k) * GROUP
            target[:, g * GROUP : (g + 1) * GROUP] = total[:, first : first + GROUP]
    vectors = total[:, 3 * width :].T
    for row, target in enumerate(vector_refs):
        for j in range(target.shape[0] // own):
            long_ref[0:1, j * own : (j + 1) * own] = vectors[row + j : row + j + 1, :]
        target[...] = long_ref[0:1, : target.shape[0]].reshape(target.shape[0])
    line = total[0:1, 3 * width :]
    lane = lax.broadcasted_iota(jnp.int32, line.shape, 1)
    scale = jnp.zeros_like(line)
    for digit in range(DIGITS):
        scale = jnp.where(lane == 20 + digit, 8.0**digit, scale)
    valid = jnp.sum(line * scale, axis=1, keepdims=True)
    roots = jnp.sqrt(jnp.where((lane >= 16) & (lane < 20), line, 0.0) / (valid * width))
    roots = jnp.where(lane == 15, valid / all_tokens, roots)
    stats_ref[...] = roots[:, 15:20].reshape(5)


def pack_near(query, key, value, vectors):
    own, width = query.shape
    if quick(own):
        shape = jax.ShapeDtypeStruct((own, 3 * width + VEC), query.dtype)
        kernel = functools.partial(pack_near_kernel, len(vectors))
        arrays = (query, key, value, *vectors)
        return fetching_call(kernel, shape, "pack_near", arrays, len(arrays), [pltpu.VMEM((VEC, VEC), F32)])
    columns = jnp.concatenate([vector.reshape(-1, own) for vector in vectors]).T
    columns = jnp.pad(columns, ((0, 0), (0, VEC - columns.shape[1])))
    groups = range(0, width, GROUP)
    triples = [mat[:, first : first + GROUP] for first in groups for mat in (query, key, value)]
    return jnp.concatenate(triples + [columns], axis=1)


def pack_far(merge, inner, outer, after):
    own, width = merge.shape
    parts = inner.shape[1] // width
    if quick(own):
        shape = jax.ShapeDtypeStruct((own, (1 + 2 * parts) * width), merge.dtype)
        return fetching_call(pack_far_kernel, shape, "pack_far", (merge, inner, outer, after), 3)
    inner = inner.reshape(own, width // own, parts, own).transpose(0, 2, 1, 3).reshape(own, parts * width)
    outer = outer.reshape(parts, own, width).transpose(1, 0, 2).reshape(own, parts * width)
    return jnp.concatenate([merge, inner, outer], axis=1)


def unpack_far(far, parts):
    own, width = far.shape[0], far.shape[1] // (1 + 2 * parts)
    if quick(own):
        shapes = [(own, width), (own, parts * width), (parts * own, width)]
        shapes = [jax.ShapeDtypeStruct(shape, F32) for shape in shapes]
        return small_call(unpack_kernel, shapes, "unpack_far")(far)
    far = far.astype(F32)
    inner = far[:, width : (1 + parts) * width].reshape(own, parts, width // own, own)
    outer = far[:, (1 + parts) * width :].reshape(own, parts, width)
    return (
        far[:, :width],
        inner.transpose(0, 2, 1, 3).reshape(own, parts * width),
        outer.transpose(1, 0, 2).reshape(parts * own, width),
    )


def finish_near(blocks, parts, all_tokens, stats, valid_own):
    own = blocks[0].shape[0]
    width = (blocks[0].shape[1] - VEC) // 3
    sizes = [own] * 8 + [parts * own]
    if quick(own):
        shapes = [(own, width)] * 3 + [(size,) for size in sizes] + [(5,)]
        shapes = [jax.ShapeDtypeStruct(shape, F32) for shape in shapes]
        kernel = functools.partial(finish_kernel, all_tokens, len(sizes))
        scratch = [pltpu.VMEM((8, max(sizes)), F32)]
        query, key, value, *rest = small_call(kernel, shapes, "finish_near", scratch_shapes=scratch)(*blocks)
        return query, key, value, rest[:-1], rest[-1]
    total = tree_sum(blocks)
    triple = total[:, : 3 * width].reshape(own, width // GROUP, 3, GROUP)
    mine = total[:, 3 * width :].T
    sums = lax.psum(jnp.concatenate([jnp.sum(stats[:4], axis=1), valid_own[None]]), AXES)
    layer_stats = jnp.concatenate([sums[4:] / all_tokens, jnp.sqrt(sums[:4] / (sums[4] * width))])
    vectors = [mine[row] for row in range(8)] + [mine[8 : 8 + parts].reshape(parts * own)]
    return *(triple[:, :, k].reshape(own, width) for k in range(3)), vectors, layer_stats


def per_device(
    layer_input, cotangent, doc_lengths, pad_tail,
    query_weight, query_bias, key_weight, value_weight, value_bias,
    merge_weight, merge_bias, first_gain, first_shift,
    inner_weight, inner_bias, outer_weight, outer_bias, second_gain, second_shift,
):
    seqs, _, width = layer_input.shape
    own = query_weight.shape[0]
    devices = width // own
    parts = inner_weight.shape[1] // width
    groups = width // GROUP

    vectors = (query_bias, value_bias, merge_bias, first_gain, first_shift, outer_bias, second_gain, second_shift, inner_bias)
    near_own = pack_near(query_weight, key_weight, value_weight, vectors)
    near = quick_gather(near_own)
    far = gather(pack_far(merge_weight, inner_weight, outer_weight, near_own))
    segment, low, count = segments(doc_lengths, pad_tail)
    segment = segment[:, None, :]

    vec_rows = near[:, 3 * width :].T.astype(F32)
    bias = jnp.stack([vec_rows[0], jnp.zeros((width,), F32), vec_rows[1]])
    bias = bias.reshape(3, groups, GROUP).transpose(1, 0, 2).reshape(1, 3 * width)
    vec = vec_rows[:24]

    qkv, mixed, lse = attention_forward(layer_input, near, bias, segment, low, count)
    tokens = seqs * LEN
    flat_mixed = mixed.reshape(tokens, width)
    output, normed, inverse, upper, slope, outer_partial, sums, stats = upper_half(
        flat_mixed, layer_input.reshape(tokens, width), cotangent.reshape(tokens, width), far, vec, pad_tail
    )
    outer_grad = over_planes(outer_partial)
    residual, mixed_grad, inner_partial, sums = lower_half(flat_mixed, normed, inverse, upper, slope, far, vec, sums)
    inner_grad = over_planes(inner_partial)
    chips = lax.axis_size("dp") // 2 if quick(own) else 0
    dqkv, keep, send = attention_backward(
        qkv, mixed, mixed_grad.reshape(mixed.shape), layer_input, lse, segment, sums, stats, low, count, pad_tail, chips
    )
    far_planes = jnp.concatenate([inner_grad, outer_grad], axis=1)
    if chips:
        keep, far_planes = lax.optimization_barrier((keep, far_planes))
        far_grad = over_columns(far_planes)
        parts_own = join_cores(keep, send)
        parts_own, residual = lax.optimization_barrier((parts_own, residual))
        near_planes = join_chips(parts_own)
    else:
        far_grad = over_columns(far_planes)
        near_planes = over_planes(keep[0])
    input_gradient = residual + dot(dqkv.reshape(tokens, 3 * width), near[:, : 3 * width], 1, 1)
    if chips:
        near_planes, input_gradient = lax.optimization_barrier((near_planes, input_gradient))
        near_blocks = swap_blocks(blocks_for_columns(near_planes))
    else:
        near_blocks = [over_columns(near_planes)]
    merge_grad, inner_grad, outer_grad = unpack_far(far_grad, parts)
    near_blocks[0], merge_grad = lax.optimization_barrier((near_blocks[0], merge_grad))
    valid_own = jnp.sum(LEN - pad_tail).astype(F32)
    query_grad, key_grad, value_grad, mine, layer_stats = finish_near(
        near_blocks, parts, tokens * devices, stats, valid_own
    )
    return (
        output.reshape(layer_input.shape),
        input_gradient.reshape(layer_input.shape),
        query_grad,
        mine[6],
        key_grad,
        value_grad,
        mine[7],
        merge_grad,
        mine[5],
        mine[3],
        mine[4],
        inner_grad,
        mine[8],
        outer_grad,
        mine[2],
        mine[0],
        mine[1],
        layer_stats,
    )


def solution(mesh):
    matrix, vector, cube = P(AXES, None), P(AXES), P(AXES, None, None)
    in_specs = (
        cube, cube, matrix, vector,
        matrix, vector, matrix, matrix, vector,
        matrix, vector, vector, vector,
        matrix, vector, matrix, vector, vector, vector,
    )
    out_specs = (
        cube, cube,
        matrix, vector, matrix, matrix, vector,
        matrix, vector, vector, vector,
        matrix, vector, matrix, vector, vector, vector,
        P(),
    )
    return jax.shard_map(per_device, mesh=mesh, in_specs=in_specs, out_specs=out_specs, check_vma=False)
```
